32 devices in a mesh: tm: 4 (over z), width: 4 (over x, core), head: 2 (over y).
Axes of the slice: x: 2, y: 2, z: 4, core: 2. Of those that a mesh axis runs over, the one named last changes fastest.
Arguments:
- query_heads: bfloat16 [12, 36, 40, 256], P('tm', None, 'width', 'head'), may hold values from -18 to 18
- key_heads: bfloat16 [12, 36, 40, 256], P('tm', None, 'width', 'head'), may hold values from -18 to 18
- value_heads: bfloat16 [12, 36, 40, 256], P('tm', None, 'width', 'head'), may hold values from -10 to 10
- row_valid: int32 [36], replicated, may hold values from 0 to 1, as said below
- out_weight: bfloat16 [256, 3072], P(None, 'head'), may hold values from -0.375 to 0.375
- grad_mixed: bfloat16 [12, 36, 40, 3072], P('tm', None, 'width', 'head'), may hold values from -6 to 6
Outputs:
- mixed: bfloat16 [12, 36, 40, 3072], P('tm', None, 'width', 'head')
- grad_query: bfloat16 [12, 36, 40, 256], P('tm', None, 'width', 'head')
- grad_key: bfloat16 [12, 36, 40, 256], P('tm', None, 'width', 'head')
- grad_value: bfloat16 [12, 36, 40, 256], P('tm', None, 'width', 'head')
- grad_weight: float32 [256, 3072], P(('tm', 'width'), 'head')
The draws below stay inside these ranges and needn't reach their ends.
Inputs may be any that keep to these rules, and one draw needn't show every extreme that they name: row_valid is 1 on every row before the last 9 rows; among the last 9 rows at least one is 1 and at least one is 0.
All inputs are finite; a program needn't handle non-finite values.
Results may differ from the reference program's by a relative error of at most 0.015.
Values may be sent and summed in bfloat16 or wider, within the bound.
A program may use at most 256 MiB of HBM per device.

```python
import math
import jax
import jax.numpy as jnp
from jax import lax

TF = 3
TH = 9
TW = 10
HD = 128
D = 3072
HEADS = 2
FRAMES = 12
ROWS = 36
COLS = 40
N_TM = 4
N_WIDTH = 4


def drawn_pair(key):
    full_shape = (FRAMES, ROWS, COLS, HEADS * HD)
    seeded = jax.random.fold_in(key, 11)
    query_array = jnp.clip(jax.random.normal(jax.random.fold_in(seeded, 1), full_shape, jnp.float32), -4.0, 4.0)
    key_array = jnp.clip(jax.random.normal(jax.random.fold_in(seeded, 2), full_shape, jnp.float32), -4.0, 4.0)
    return (query_array, key_array)


def draw_query_heads(key, part):
    return drawn_pair(key)[0].astype(jnp.bfloat16)


def draw_key_heads(key, part):
    return drawn_pair(key)[1].astype(jnp.bfloat16)


def draw_value_heads(key, part):
    full_shape = (FRAMES, ROWS, COLS, HEADS * HD)
    tile_shape = (FRAMES // TF, ROWS // TH, COLS // TW, HEADS * HD)
    seeded = jax.random.fold_in(key, 23)
    noise = jnp.clip(jax.random.normal(jax.random.fold_in(seeded, 1), full_shape, jnp.float32), -4.0, 4.0)
    offsets = jnp.clip(jax.random.normal(jax.random.fold_in(seeded, 2), tile_shape, jnp.float32), -3.0, 3.0)
    offsets = jnp.repeat(jnp.repeat(jnp.repeat(offsets, TF, axis=0), TH, axis=1), TW, axis=2)
    return (noise + 2.0 * offsets).astype(jnp.bfloat16)


def draw_row_valid(key, part):
    seeded = jax.random.fold_in(key, 31)
    bits = jax.random.randint(jax.random.fold_in(seeded, 1), (ROWS,), 0, 2)
    first = jax.random.randint(jax.random.fold_in(seeded, 2), (), 0, TH)
    second = (first + 1 + jax.random.randint(jax.random.fold_in(seeded, 3), (), 0, TH - 1)) % TH
    local = jnp.arange(ROWS, dtype=jnp.int32) - (ROWS - TH)
    bits = jnp.where(local < 0, 1, bits)
    bits = jnp.where(local == first, 1, bits)
    bits = jnp.where(local == second, 0, bits)
    return bits.astype(jnp.int32)


def levels(rng, dims, cuts, least, top_value):
    def one(dim, parts):
        heights = jax.random.uniform(jax.random.fold_in(jax.random.fold_in(rng, 6), dim), (parts,), jnp.float32, least / len(cuts), top_value / len(cuts))
        return jnp.repeat(jnp.exp(heights), dims[dim] // parts).reshape((-1,) + (1,) * (len(dims) - dim - 1))

    gain = one(*cuts[0])
    for cut in cuts[1:]:
        gain = gain * one(*cut)
    return gain


def normal_values(stream_key, shape, deviation, most, cuts=(), kind=jnp.bfloat16):
    values = deviation * jax.random.normal(stream_key, shape, jnp.float32)
    if cuts:
        values = values * levels(stream_key, shape, cuts, -0.22, 0.18)
    return jnp.clip(values, -most, most).astype(kind)


def setup_inputs(seed: int = 0) -> dict:
    arg_keys = jax.random.split(jax.random.key(seed), 7)
    query_heads = draw_query_heads(jax.random.fold_in(arg_keys[6], 71), 0)
    key_heads = draw_key_heads(jax.random.fold_in(arg_keys[6], 71), 0)
    value_heads = draw_value_heads(jax.random.fold_in(arg_keys[6], 71), 0)
    row_valid = draw_row_valid(jax.random.fold_in(arg_keys[6], 71), 0)
    out_weight = normal_values(arg_keys[4], (HEADS * HD, D), (HEADS * HD) ** -0.5, 0.375, ((1, 2),))
    grad_mixed = normal_values(arg_keys[5], (FRAMES, ROWS, COLS, D), 1.0, 6.0, ((0, 4), (2, 4), (3, 2)))
    return dict(query_heads=query_heads, key_heads=key_heads, value_heads=value_heads, row_valid=row_valid, out_weight=out_weight, grad_mixed=grad_mixed)


NEG_FILL = -1e+30

def band_layout(tile_count):
    band_tiles = min(4, tile_count)
    layout = []
    for band_index in range(tile_count // 2):
        key_tile = min(max(2 * band_index - 1, 0), tile_count - band_tiles)
        layout.append((2 * band_index, key_tile, band_tiles))
    return layout

def tile_number(frames, rows, columns, row_start, tile_rows):
    row_ids = lax.broadcasted_iota(jnp.int32, (frames, rows, columns), 1)
    return ((row_ids + row_start) // tile_rows).reshape(-1)

def band_parts(query_block, key_wide, value_wide, live_wide, tile_rows, scale, entry):
    query_tile, key_tile, band_tiles = entry
    frames, rows, columns, depth = query_block.shape
    query_low = query_tile * tile_rows
    key_low = key_tile * tile_rows
    key_rows = band_tiles * tile_rows
    query_band = query_block[:, query_low:query_low + 2 * tile_rows].reshape(-1, depth)
    key_band = key_wide[:, key_low:key_low + key_rows].reshape(-1, depth)
    value_band = value_wide[:, key_low:key_low + key_rows].reshape(-1, depth)
    live_band = live_wide[:, key_low:key_low + key_rows].reshape(-1)
    query_tiles = tile_number(frames, 2 * tile_rows, columns, query_low, tile_rows)
    key_tiles = tile_number(key_wide.shape[0], key_rows, key_wide.shape[2], key_low, tile_rows)
    allowed = live_band[None, :] & (jnp.abs(query_tiles[:, None] - key_tiles[None, :]) <= 1)
    scores = jnp.dot(query_band, key_band.T, preferred_element_type=jnp.float32) * scale
    scores = jnp.where(allowed, scores, NEG_FILL)
    return (query_band, key_band, value_band, scores)

def attend_forward(query_block, key_wide, value_wide, live_wide, tile_rows, scale):
    frames, rows, columns, depth = query_block.shape
    outputs = []
    logs = []
    for entry in band_layout(rows // tile_rows):
        query_band, key_band, value_band, scores = band_parts(query_block, key_wide, value_wide, live_wide, tile_rows, scale, entry)
        peak = lax.optimization_barrier(jnp.max(scores, axis=1, keepdims=True))
        expos = jnp.exp(scores - peak)
        totals = lax.optimization_barrier(jnp.sum(expos, axis=1, keepdims=True))
        attended = jnp.dot(expos.astype(jnp.bfloat16), value_band, preferred_element_type=jnp.float32) / totals
        outputs.append(attended.astype(jnp.bfloat16).reshape(frames, 2 * tile_rows, columns, depth))
        logs.append((peak + jnp.log(totals)).reshape(frames, 2 * tile_rows, columns))
    return (jnp.concatenate(outputs, axis=1), jnp.concatenate(logs, axis=1))

def attend_backward(query_block, key_wide, value_wide, live_wide, lse_block, grad_block, delta_block, tile_rows, scale):
    frames, rows, columns, depth = query_block.shape
    wide_frames = key_wide.shape[0]
    wide_columns = key_wide.shape[2]
    grad_pair = jnp.zeros((2, wide_frames, rows, wide_columns, depth), jnp.float32)
    grad_parts = []
    for entry in band_layout(rows // tile_rows):
        query_tile, key_tile, band_tiles = entry
        query_low = query_tile * tile_rows
        key_low = key_tile * tile_rows
        key_rows = band_tiles * tile_rows
        query_band, key_band, value_band, scores = band_parts(query_block, key_wide, value_wide, live_wide, tile_rows, scale, entry)
        lse_band = lse_block[:, query_low:query_low + 2 * tile_rows].reshape(-1)
        delta_band = delta_block[:, query_low:query_low + 2 * tile_rows].reshape(-1)
        grad_band = grad_block[:, query_low:query_low + 2 * tile_rows].reshape(-1, depth)
        probs = jnp.exp(scores - lse_band[:, None])
        dprob = jnp.dot(grad_band, value_band.T, preferred_element_type=jnp.float32)
        dscore = (probs * (dprob - delta_band[:, None]) * scale).astype(jnp.bfloat16)
        grad_query_band = jnp.dot(dscore, key_band, preferred_element_type=jnp.float32)
        grad_key_band = jnp.dot(dscore.T, query_band, preferred_element_type=jnp.float32)
        grad_value_band = jnp.dot(probs.astype(jnp.bfloat16).T, grad_band, preferred_element_type=jnp.float32)
        grad_pair = grad_pair.at[0, :, key_low:key_low + key_rows].add(grad_key_band.reshape(wide_frames, key_rows, wide_columns, depth))
        grad_pair = grad_pair.at[1, :, key_low:key_low + key_rows].add(grad_value_band.reshape(wide_frames, key_rows, wide_columns, depth))
        grad_parts.append(grad_query_band.reshape(frames, 2 * tile_rows, columns, depth))
    return (jnp.concatenate(grad_parts, axis=1), grad_pair)

def reference(query_heads, key_heads, value_heads, row_valid, out_weight, grad_mixed):
    scale = 1.0 / math.sqrt(HD)
    frames_all, rows_all, columns_all, head_width = query_heads.shape
    block_count = N_TM * N_WIDTH
    pad_sizes = ((TF, TF), (0, 0), (TW, TW), (0, 0))
    live_rows = row_valid > 0
    zero = jnp.zeros((), jnp.int32)
    frame_step = jnp.asarray(TF).astype(jnp.int32)
    column_step = jnp.asarray(TW).astype(jnp.int32)

    def live_for(block_time, block_column):
        frame_ids = (block_time - 1) * frame_step + jnp.arange(3 * TF, dtype=jnp.int32)
        column_ids = (block_column - 1) * column_step + jnp.arange(3 * TW, dtype=jnp.int32)
        frame_ok = (frame_ids >= 0) & (frame_ids < frames_all)
        column_ok = (column_ids >= 0) & (column_ids < columns_all)
        return frame_ok[:, None, None] & live_rows[None, :, None] & column_ok[None, None, :]
    head_outputs = []
    head_logs = []
    for head_index in range(HEADS):
        low = head_index * HD
        query_one = query_heads[..., low:low + HD]
        key_padded = jnp.pad(key_heads[..., low:low + HD], pad_sizes)
        value_padded = jnp.pad(value_heads[..., low:low + HD], pad_sizes)

        def forward_step(block_index, carry):
            out_all, lse_all = carry
            block_index = jnp.asarray(block_index).astype(jnp.int32)
            block_time = block_index // N_WIDTH
            block_column = block_index % N_WIDTH
            corner = (block_time * frame_step, zero, block_column * column_step, zero)
            query_block = lax.dynamic_slice(query_one, corner, (TF, rows_all, TW, HD))
            key_wide = lax.dynamic_slice(key_padded, corner, (3 * TF, rows_all, 3 * TW, HD))
            value_wide = lax.dynamic_slice(value_padded, corner, (3 * TF, rows_all, 3 * TW, HD))
            attended, lse_block = attend_forward(query_block, key_wide, value_wide, live_for(block_time, block_column), TH, scale)
            out_all = lax.dynamic_update_slice(out_all, attended, corner)
            lse_all = lax.dynamic_update_slice(lse_all, lse_block, corner[:3])
            return (out_all, lse_all)
        start = (jnp.zeros((frames_all, rows_all, columns_all, HD), jnp.bfloat16), jnp.zeros((frames_all, rows_all, columns_all), jnp.float32))
        out_all, lse_all = lax.fori_loop(0, block_count, forward_step, start)
        head_outputs.append(out_all)
        head_logs.append(lse_all)
    attended_all = jnp.concatenate(head_outputs, axis=-1)
    attended_flat = attended_all.reshape(-1, head_width)
    grad_flat = grad_mixed.reshape(-1, D)
    mixed = jnp.dot(attended_flat, out_weight, preferred_element_type=jnp.float32).astype(jnp.bfloat16).reshape(frames_all, rows_all, columns_all, D)
    grad_weight = jnp.dot(attended_flat.T, grad_flat, preferred_element_type=jnp.float32)
    grad_attended = jnp.dot(grad_flat, out_weight.T, preferred_element_type=jnp.float32).astype(jnp.bfloat16).reshape(frames_all, rows_all, columns_all, head_width)
    query_grads = []
    key_grads = []
    value_grads = []
    for head_index in range(HEADS):
        low = head_index * HD
        query_one = query_heads[..., low:low + HD]
        key_padded = jnp.pad(key_heads[..., low:low + HD], pad_sizes)
        value_padded = jnp.pad(value_heads[..., low:low + HD], pad_sizes)
        grad_one = grad_attended[..., low:low + HD]
        delta_one = lax.optimization_barrier(jnp.sum(grad_one.astype(jnp.float32) * head_outputs[head_index].astype(jnp.float32), axis=-1))
        lse_one = head_logs[head_index]

        def backward_step(block_index, carry):
            grad_query_all, grad_pair_all = carry
            block_index = jnp.asarray(block_index).astype(jnp.int32)
            block_time = block_index // N_WIDTH
            block_column = block_index % N_WIDTH
            corner = (block_time * frame_step, zero, block_column * column_step, zero)
            query_block = lax.dynamic_slice(query_one, corner, (TF, rows_all, TW, HD))
            key_wide = lax.dynamic_slice(key_padded, corner, (3 * TF, rows_all, 3 * TW, HD))
            value_wide = lax.dynamic_slice(value_padded, corner, (3 * TF, rows_all, 3 * TW, HD))
            grad_block = lax.dynamic_slice(grad_one, corner, (TF, rows_all, TW, HD))
            lse_block = lax.dynamic_slice(lse_one, corner[:3], (TF, rows_all, TW))
            delta_block = lax.dynamic_slice(delta_one, corner[:3], (TF, rows_all, TW))
            grad_query_block, grad_pair = attend_backward(query_block, key_wide, value_wide, live_for(block_time, block_column), lse_block, grad_block, delta_block, TH, scale)
            grad_query_all = lax.dynamic_update_slice(grad_query_all, grad_query_block.astype(jnp.bfloat16), corner)
            pair_corner = (zero, block_time * frame_step, zero, block_column * column_step, zero)
            current = lax.dynamic_slice(grad_pair_all, pair_corner, (2, 3 * TF, rows_all, 3 * TW, HD))
            grad_pair_all = lax.dynamic_update_slice(grad_pair_all, current + grad_pair, pair_corner)
            return (grad_query_all, grad_pair_all)
        start = (jnp.zeros((frames_all, rows_all, columns_all, HD), jnp.bfloat16), jnp.zeros((2, frames_all + 2 * TF, rows_all, columns_all + 2 * TW, HD), jnp.float32))
        grad_query_all, grad_pair_all = lax.fori_loop(0, block_count, backward_step, start)
        inner = grad_pair_all[:, TF:TF + frames_all, :, TW:TW + columns_all]
        query_grads.append(grad_query_all)
        key_grads.append(inner[0].astype(jnp.bfloat16))
        value_grads.append(inner[1].astype(jnp.bfloat16))
    grad_query = jnp.concatenate(query_grads, axis=-1)
    grad_key = jnp.concatenate(key_grads, axis=-1)
    grad_value = jnp.concatenate(value_grads, axis=-1)
    return (mixed, grad_query, grad_key, grad_value, grad_weight)
```

```python
import functools
import math

import jax
import jax.numpy as jnp
from jax import lax
from jax.experimental import pallas as pl
from jax.experimental.pallas import tpu as pltpu
from jax.sharding import PartitionSpec as P

TH = 9
FAR = 1e30
LOG2E = 1.4426950408889634


def round_up(value, step):
    return -(-value // step) * step


def dot_nt(left, right):
    return lax.dot_general(
        left, right, (((1,), (1,)), ((), ())), preferred_element_type=jnp.float32
    )


MESH = pl.DeviceIdType.MESH


def columns_of(step):
    return pl.multiple_of(step, 128)


def row_within(places):
    return places - TH * jnp.floor((places + 0.5) * (1.0 / TH))


def attention_kernel(
    valid_ref, qkv_ref, gm_hbm, w_hbm,
    att_ref, other_ref, gq_ref, gk_ref, gv_ref, share_ref,
    k_all, v_all, q_all, g_all, s_buf, bias, top, out, grad, grad_k, grad_v,
    gm, weight, part_own, part_other, part_in, att_in, st_own, st_all, stats,
    terms, in_w, in_t, sum_w, send_t,
    send_sem, recv_sem, own_sem, peer_send, peer_recv, w_send, w_recv, t_send, t_recv,
    *, tiles, block, wide, count, scale,
):
    depth = q_all.shape[-1]
    half = wide // 2
    halves = ((0, half), (half, half))
    t_index, w_index, h_index = (lax.axis_index(name) for name in ("tm", "width", "head"))
    t_count, w_count = lax.axis_size("tm"), lax.axis_size("width")
    t_back, t_ahead = t_index > 0, t_index < t_count - 1
    w_back, w_ahead = w_index > 0, w_index < w_count - 1
    exists = [
        None, t_back, t_ahead, w_back, w_ahead,
        t_back & w_back, t_ahead & w_back, t_back & w_ahead, t_ahead & w_ahead,
    ]
    t_above = (t_index + 1, w_index, h_index)
    t_below = (t_index - 1, w_index, h_index)
    w_above = (t_index, w_index + 1, h_index)
    w_below = (t_index, w_index - 1, h_index)
    peer = (t_index, w_index, 1 - h_index)
    direct = [(1, t_ahead, t_above), (2, t_back, t_below), (3, w_ahead, w_above), (4, w_back, w_below)]
    onward = [
        (5, 1, t_back & w_ahead, w_above), (7, 1, t_back & w_back, w_below),
        (6, 2, t_ahead & w_ahead, w_above), (8, 2, t_ahead & w_back, w_below),
    ]
    near, far = (3, 4), (5, 6, 7, 8)
    q_ref, k_ref, v_ref = qkv_ref.at[0], qkv_ref.at[1], qkv_ref.at[2]

    def slot_of(which, slot):
        if which == 4:
            return st_all.at[slot]
        dest = (k_all, v_all, q_all, g_all)[which]
        return dest.at[:, slot * block : (slot + 1) * block, :]

    def remote(which, source, slot, device):
        return pltpu.make_async_remote_copy(
            src_ref=source, dst_ref=slot_of(which, slot),
            send_sem=send_sem.at[which, slot], recv_sem=recv_sem.at[which, slot],
            device_id=device, device_id_type=MESH,
        )

    def send_direct(which, source):
        for slot, there, device in direct:
            @pl.when(there)
            def _():
                remote(which, source, slot, device).start()

    def send_onward(which):
        for slot, via, there, device in onward:
            @pl.when(there)
            def _():
                remote(which, slot_of(which, via), slot, device).start()

    def receive(which, slots):
        for slot in slots:
            @pl.when(exists[slot])
            def _():
                remote(which, slot_of(which, slot), slot, peer).wait_recv()

    def sent(which, source):
        for slot, there, device in direct:
            @pl.when(there)
            def _():
                remote(which, source, slot, device).wait_send()
        for slot, via, there, device in onward:
            @pl.when(there)
            def _():
                remote(which, slot_of(which, via), slot, device).wait_send()

    def swap(index, source, dest):
        return pltpu.make_async_remote_copy(
            src_ref=source, dst_ref=dest, send_sem=peer_send.at[index],
            recv_sem=peer_recv.at[index], device_id=peer, device_id_type=MESH,
        )

    def w_copy(hop):
        dest = lax.rem(w_index + hop, w_count)
        return pltpu.make_async_remote_copy(
            src_ref=terms.at[dest], dst_ref=in_w.at[hop - 1],
            send_sem=w_send.at[hop - 1], recv_sem=w_recv.at[hop - 1],
            device_id=(t_index, dest, h_index), device_id_type=MESH,
        )

    def t_copy(hop):
        dest = lax.rem(t_index + hop, t_count)
        return pltpu.make_async_remote_copy(
            src_ref=send_t.at[dest], dst_ref=in_t.at[hop - 1],
            send_sem=t_send.at[hop - 1], recv_sem=t_recv.at[hop - 1],
            device_id=(dest, w_index, h_index), device_id_type=MESH,
        )

    own = [
        pltpu.make_async_copy(source, dest, own_sem.at[index])
        for index, (source, dest) in enumerate((
            (k_ref, slot_of(0, 0)), (v_ref, slot_of(1, 0)), (q_ref, slot_of(2, 0)),
            (gm_hbm, gm), (w_hbm, weight),
        ))
    ]
    for copy in own:
        copy.start()

    barrier = pltpu.get_barrier_semaphore()
    partners = [(there, device) for _, there, device in direct]
    for there, device in partners:
        @pl.when(there)
        def _():
            pl.semaphore_signal(barrier, inc=1, device_id=device, device_id_type=MESH)
    pl.semaphore_signal(barrier, inc=1, device_id=peer, device_id_type=MESH)
    greeted = 1 + sum(jnp.where(there, 1, 0) for there, _ in partners)
    for hop in range(1, w_count):
        dest = lax.rem(w_index + hop, w_count)
        pl.semaphore_signal(
            barrier, inc=1, device_id=(t_index, dest, h_index), device_id_type=MESH
        )
    for hop in range(1, t_count):
        dest = lax.rem(t_index + hop, t_count)
        pl.semaphore_signal(
            barrier, inc=1, device_id=(dest, w_index, h_index), device_id_type=MESH
        )
    pl.semaphore_wait(barrier, greeted + w_count + t_count - 2)

    send_direct(0, k_ref)
    send_direct(1, v_ref)

    fill = jnp.zeros((tiles, wide - 9 * block, depth), jnp.bfloat16)
    hole = jnp.zeros((tiles, block, depth), jnp.bfloat16)
    for dest in (k_all, v_all, q_all, g_all):
        dest[:, 9 * block :, :] = fill
        for slot in range(1, 9):
            @pl.when(jnp.logical_not(exists[slot]))
            def _():
                dest[:, slot * block : (slot + 1) * block, :] = hole

    places = lax.broadcasted_iota(jnp.int32, (8, wide), 1)
    inside = jnp.zeros((8, wide), jnp.float32)
    within = jnp.zeros((8, wide), jnp.int32)
    for slot in range(9):
        here = (places >= slot * block) & (places < slot * block + count)
        there = 1.0 if slot == 0 else jnp.where(exists[slot], 1.0, 0.0)
        inside = jnp.where(here, there, inside)
        within = jnp.where(here, places - slot * block, within)
    rows = row_within(within.astype(jnp.float32))
    for tile in range(tiles):
        allowed = jnp.zeros((8, wide), jnp.float32)
        for row in range(TH):
            valid = jnp.where(valid_ref[tile * TH + row] > 0, 1.0, 0.0)
            allowed = jnp.where(rows == row, valid, allowed)
        bias[tile] = jnp.where(allowed * inside > 0, 0.0, -FAR)

    for copy in own:
        copy.wait()
    first = h_index == 0

    @pl.loop(0, tiles)
    def _(tile):
        parts = dot_nt(gm[tile], weight[...]).astype(jnp.bfloat16)
        part_own[tile] = jnp.where(first, parts[:, :depth], parts[:, depth:])
        part_other[tile] = jnp.where(first, parts[:, depth:], parts[:, :depth])

    swap(0, part_other, part_in).start()
    receive(0, (1, 2))
    send_onward(0)
    swap(0, part_other, part_in).wait()
    g_all[:, :block, :] = (
        part_own[...].astype(jnp.float32) + part_in[...].astype(jnp.float32)
    ).astype(jnp.bfloat16)
    send_direct(2, q_ref)
    send_direct(3, slot_of(3, 0))

    top[...] = jnp.full(top.shape, -3e38, jnp.float32)
    out[...] = jnp.zeros(out.shape, jnp.float32)
    grad[...] = jnp.zeros(grad.shape, jnp.float32)
    ones = jnp.ones((wide, depth), jnp.bfloat16)

    def over_pairs(body):
        @pl.loop(0, tiles)
        def _(tile):
            @pl.loop(jnp.maximum(tile - 1, 0), jnp.minimum(tile + 1, tiles - 1) + 1)
            def _(row):
                body(tile, row)

    def score_part(start, size):
        def body(tile, row):
            keys = k_all[row, start : start + size, :]
            scores = dot_nt(q_all[tile, :block, :], keys) * (scale * LOG2E)
            scores = scores + bias[row, 0:1, start : start + size]
            s_buf[2 * tile + row, :, start : start + size] = scores
            best = top[tile]
            for lane in range(0, size, 128):
                best = jnp.maximum(best, scores[:, lane : lane + 128])
            top[tile] = best
        over_pairs(body)

    def value_part(start, size):
        def body(tile, row):
            span = slice(start, start + size)
            expos = jnp.exp2(s_buf[2 * tile + row, :, span] - top[tile][:, :1])
            s_buf[2 * tile + row, :, span] = expos
            values = jnp.concatenate([v_all[row, span, :], ones[:size]], axis=1)
            out[tile] += jnp.dot(
                expos.astype(jnp.bfloat16), values, preferred_element_type=jnp.float32
            )
        over_pairs(body)

    def query_part(start, size):
        def body(tile, row):
            span = slice(start, start + size)
            dprob = dot_nt(g_all[tile, :block, :], v_all[row, span, :])
            dscore = s_buf[2 * tile + row, :, span] * (dprob - grad_k[tile][:, :1])
            grad[tile] += jnp.dot(
                dscore.astype(jnp.bfloat16), k_all[row, span, :],
                preferred_element_type=jnp.float32,
            )
        over_pairs(body)

    def key_part(start, size):
        def body(tile, row):
            span = slice(start, start + size)
            queries, grads = q_all[row, span, :], g_all[row, span, :]
            lse, delta = stats[row, 0:1, span], stats[row, 1:2, span]
            probs = jnp.exp2(
                dot_nt(k_all[tile, :block, :], queries) * (scale * LOG2E) - lse
            )
            grad_v[tile] += jnp.dot(
                probs.astype(jnp.bfloat16), grads, preferred_element_type=jnp.float32
            )
            dscore = probs * (dot_nt(v_all[tile, :block, :], grads) - delta)
            grad_k[tile] += jnp.dot(
                dscore.astype(jnp.bfloat16), queries, preferred_element_type=jnp.float32
            )
        over_pairs(body)

    receive(0, near)
    score_part(*halves[0])
    receive(1, (1, 2))
    send_onward(1)
    receive(0, far)
    score_part(*halves[1])

    @pl.loop(0, tiles)
    def _(tile):
        peak = jnp.max(top[tile], axis=1, keepdims=True)
        top[tile] = jnp.broadcast_to(peak, top.shape[1:])

    receive(1, near)
    value_part(*halves[0])
    for which in (2, 3):
        receive(which, (1, 2))
        send_onward(which)
    receive(1, far)
    value_part(*halves[1])

    @pl.loop(0, tiles)
    def _(tile):
        total = out[tile][:, depth:]
        attended = (out[tile][:, :depth] / total).astype(jnp.bfloat16)
        att_ref[tile] = attended
        grads = g_all[tile, :block, :]
        delta = jnp.sum(
            grads.astype(jnp.float32) * attended.astype(jnp.float32), axis=1, keepdims=True
        )
        lanes = lax.broadcasted_iota(jnp.int32, (block, 128), 1)
        columns = jnp.where(lanes == 0, top[tile] + jnp.log2(total), delta)
        span = st_own.shape[-1]
        columns = jnp.concatenate([columns, jnp.zeros((span - block, 128), jnp.float32)], axis=0)
        st_own[tile] = columns.T[:8]
        grad_k[tile] = jnp.broadcast_to(delta, grad_k.shape[1:])

    swap(1, att_ref, att_in).start()
    send_direct(4, st_own)
    query_part(*halves[0])
    receive(4, (1, 2))
    send_onward(4)
    query_part(*halves[1])

    @pl.loop(0, tiles)
    def _(tile):
        gq_ref[tile] = (grad[tile] * (scale / out[tile][:, depth:])).astype(jnp.bfloat16)

    swap(1, att_ref, att_in).wait()
    other_ref[...] = att_in[...]
    own_att, other_att = (
        jnp.where(first, att_ref[...], att_in[...]), jnp.where(first, att_in[...], att_ref[...])
    )
    heads = jnp.concatenate([own_att, other_att], axis=2).reshape(tiles * block, 2 * depth)
    share_rows, width = share_ref.shape
    step = 512
    for start in range(0, width, step):
        piece = gm[:, :, start : start + step].reshape(tiles * block, step)
        result = lax.dot_general(
            heads, piece, (((0,), (0,)), ((), ())), preferred_element_type=jnp.float32
        )
        for part in range(t_count * w_count):
            terms[part % w_count, part // w_count, :, start : start + step] = result[
                part * share_rows : (part + 1) * share_rows
            ].astype(jnp.bfloat16)
    for hop in range(1, w_count):
        w_copy(hop).start()

    first_row = lax.broadcasted_iota(jnp.int32, (tiles, 8, wide), 1) == 0
    stats[...] = jnp.where(first_row, FAR, 0.0)
    stats[:, :, :block] = st_own[:, :, :block]

    def note(slots):
        for slot in slots:
            @pl.when(exists[slot])
            def _():
                stats[:, :, slot * block : (slot + 1) * block] = st_all[slot, :, :, :block]

    grad_k[...] = jnp.zeros(grad_k.shape, jnp.float32)
    grad_v[...] = jnp.zeros(grad_v.shape, jnp.float32)
    for which in (2, 3, 4):
        receive(which, near)
    note((1, 2, 3, 4))
    key_part(*halves[0])

    whole = terms[w_index].astype(jnp.float32)
    for hop in range(1, w_count):
        w_copy(hop).wait()
        whole = whole + in_w[hop - 1].astype(jnp.float32)
    sum_w[...] = whole
    send_t[...] = whole.astype(jnp.bfloat16)
    for hop in range(1, t_count):
        t_copy(hop).start()

    for which in (2, 3, 4):
        receive(which, far)
    note(far)
    key_part(*halves[1])

    places = lax.broadcasted_iota(jnp.int32, (block, 128), 0)
    rows = row_within(places.astype(jnp.float32))
    for tile in range(tiles):
        live = jnp.zeros((block, 128), jnp.float32)
        for row in range(TH):
            valid = jnp.where(valid_ref[tile * TH + row] > 0, 1.0, 0.0)
            live = jnp.where(rows == row, valid, live)
        gk_ref[tile] = jnp.where(live > 0, grad_k[tile] * scale, 0.0).astype(jnp.bfloat16)
        gv_ref[tile] = jnp.where(live > 0, grad_v[tile], 0.0).astype(jnp.bfloat16)

    share = sum_w[t_index]
    for hop in range(1, t_count):
        t_copy(hop).wait()
        share = share + in_t[hop - 1].astype(jnp.float32)
    share_ref[...] = share
    for which, source in enumerate((k_ref, v_ref, q_ref, slot_of(3, 0), st_own)):
        sent(which, source)


def lay_out(cells, block, tile_rows):
    frames, columns, rows, depth = cells.shape
    tiles = rows // tile_rows
    cells = cells.reshape(frames * columns, tiles, tile_rows, depth).transpose(1, 0, 2, 3)
    cells = cells.reshape(tiles, frames * columns * tile_rows, depth)
    return jnp.pad(cells, ((0, 0), (0, block - cells.shape[1]), (0, 0)))


def lay_back(cells, frames, columns, tile_rows):
    tiles, _, depth = cells.shape
    count = frames * columns
    cells = cells[:, : count * tile_rows].reshape(tiles, count, tile_rows, depth)
    return cells.transpose(1, 0, 2, 3).reshape(frames, columns, tiles * tile_rows, depth)


def shards(query_heads, key_heads, value_heads, row_valid, out_weight, grad_mixed):
    frames, rows, columns, depth = query_heads.shape
    scale = 1.0 / math.sqrt(depth)
    tiles = rows // TH
    count = frames * columns * TH
    block = round_up(count, 16)
    wide = round_up(9 * block, 256)
    swap = (0, 2, 1, 3)
    qkv = jnp.stack([query_heads.transpose(swap), key_heads.transpose(swap), value_heads.transpose(swap)])
    qkv = jax.vmap(lambda cells: lay_out(cells, block, TH))(qkv)
    grad_in = lay_out(grad_mixed.transpose(swap), block, TH)
    t_count, w_count = lax.axis_size("tm"), lax.axis_size("width")
    share_rows, width = out_weight.shape[0] // (t_count * w_count), out_weight.shape[1]

    pairs = tiles * 3 - 2
    work = pairs * block * wide
    in_vmem = pl.BlockSpec(memory_space=pltpu.VMEM)
    anywhere = pl.BlockSpec(memory_space=pl.ANY)
    flat = jax.ShapeDtypeStruct((tiles, block, depth), jnp.bfloat16)
    bf16 = lambda *shape: pltpu.VMEM(shape, jnp.bfloat16)
    f32 = lambda *shape: pltpu.VMEM(shape, jnp.float32)
    dma = lambda *shape: pltpu.SemaphoreType.DMA(shape)
    span = round_up(block, 128)
    attended, other, grad_query, grad_key, grad_value, grad_weight = pl.pallas_call(
        functools.partial(
            attention_kernel, tiles=tiles, block=block, wide=wide, count=count, scale=scale
        ),
        out_shape=(flat,) * 5 + (jax.ShapeDtypeStruct((share_rows, width), jnp.float32),),
        in_specs=[pl.BlockSpec(memory_space=pltpu.SMEM)] + [anywhere] * 3,
        out_specs=(in_vmem,) * 6,
        scratch_shapes=[
            bf16(tiles, wide, depth), bf16(tiles, wide, depth),
            bf16(tiles, wide, depth), bf16(tiles, wide, depth),
            f32(pairs, block, wide), f32(tiles, 8, wide), f32(tiles, block, 128),
            f32(tiles, block, 2 * depth), f32(tiles, block, depth),
            f32(tiles, block, depth), f32(tiles, block, depth),
            bf16(tiles, block, width), bf16(2 * depth, width),
            bf16(tiles, block, depth), bf16(tiles, block, depth), bf16(tiles, block, depth),
            bf16(tiles, block, depth),
            f32(tiles, 8, span), f32(9, tiles, 8, span), f32(tiles, 8, wide),
            bf16(w_count, t_count, share_rows, width),
            bf16(w_count - 1, t_count, share_rows, width),
            bf16(t_count - 1, share_rows, width),
            f32(t_count, share_rows, width), bf16(t_count, share_rows, width),
            dma(5, 9), dma(5, 9), dma(5), dma(2), dma(2),
            dma(w_count - 1), dma(w_count - 1), dma(t_count - 1), dma(t_count - 1),
        ],
        compiler_params=pltpu.CompilerParams(
            vmem_limit_bytes=58 << 20, collective_id=0, has_side_effects=True
        ),
        cost_estimate=pl.CostEstimate(
            flops=16 * work * depth, transcendentals=2 * work,
            bytes_accessed=4 * tiles * wide * depth,
        ),
        name="attention",
    )(row_valid, qkv, grad_in, out_weight)

    first = lax.axis_index("head") == 0
    heads_all = jnp.concatenate(
        [jnp.where(first, attended, other), jnp.where(first, other, attended)], axis=2
    )
    heads_all = lay_back(heads_all, frames, columns, TH)
    mixed = lax.dot_general(
        heads_all, out_weight, (((3,), (0,)), ((), ())), preferred_element_type=jnp.float32
    ).astype(jnp.bfloat16)
    back = lambda cells: lay_back(cells, frames, columns, TH).transpose(swap)
    return (mixed.transpose(swap), back(grad_query), back(grad_key), back(grad_value), grad_weight)


def solution(mesh):
    split = P("tm", None, "width", "head")
    return jax.shard_map(
        shards,
        mesh=mesh,
        in_specs=(split, split, split, P(), P(None, "head"), split),
        out_specs=(split, split, split, split, P(("tm", "width"), "head")),
        check_vma=False,
    )
```

```python
import functools
import math

import jax
import jax.numpy as jnp
from jax import lax
from jax.experimental import pallas as pl
from jax.experimental.pallas import tpu as pltpu
from jax.sharding import PartitionSpec as P

TH = 9
FAR = 1e30
LOG2E = 1.4426950408889634


def round_up(value, step):
    return -(-value // step) * step


def dot_nt(left, right):
    return lax.dot_general(
        left, right, (((1,), (1,)), ((), ())), preferred_element_type=jnp.float32
    )


MESH = pl.DeviceIdType.MESH


def columns_of(step):
    return pl.multiple_of(step, 128)


def row_within(places):
    return places - TH * jnp.floor((places + 0.5) * (1.0 / TH))


def attention_kernel(
    valid_ref, qkv_ref, gm_hbm, w_hbm,
    mixed_ref, gq_ref, gk_ref, gv_ref, share_ref,
    k_all, v_all, q_all, g_all, s_buf, bias, top, out, grad, grad_k, grad_v,
    gm, weight, flat, att_ref, part_own, part_other, part_in, att_in, st_own, st_all, stats,
    terms, in_w, in_t, sum_w, send_t, stage,
    send_sem, recv_sem, own_sem, peer_send, peer_recv, w_send, w_recv, t_send, t_recv, out_sem,
    *, tiles, block, wide, count, tall, scale,
):
    depth = q_all.shape[-1]
    half = wide // 2
    halves = ((0, half), (half, half))
    t_index, w_index, h_index = (lax.axis_index(name) for name in ("tm", "width", "head"))
    t_count, w_count = lax.axis_size("tm"), lax.axis_size("width")
    t_back, t_ahead = t_index > 0, t_index < t_count - 1
    w_back, w_ahead = w_index > 0, w_index < w_count - 1
    exists = [
        None, t_back, t_ahead, w_back, w_ahead,
        t_back & w_back, t_ahead & w_back, t_back & w_ahead, t_ahead & w_ahead,
    ]
    t_above = (t_index + 1, w_index, h_index)
    t_below = (t_index - 1, w_index, h_index)
    w_above = (t_index, w_index + 1, h_index)
    w_below = (t_index, w_index - 1, h_index)
    peer = (t_index, w_index, 1 - h_index)
    direct = [(1, t_ahead, t_above), (2, t_back, t_below), (3, w_ahead, w_above), (4, w_back, w_below)]
    even = lax.rem(w_index, 2) == 0
    odd = jnp.logical_not(even)
    over_w = [
        (5, 1, t_back & w_ahead, even, w_above), (7, 1, t_back & w_back, odd, w_below),
        (6, 2, t_ahead & w_ahead, even, w_above), (8, 2, t_ahead & w_back, odd, w_below),
    ]
    over_t = [
        (5, 3, t_ahead & w_back & even, t_above), (7, 4, t_ahead & w_ahead & odd, t_above),
        (6, 3, t_back & w_back & even, t_below), (8, 4, t_back & w_ahead & odd, t_below),
    ]
    turned = ((5, 7), (6, 8), (5, 7), (6, 8), ())

    def routes(which):
        found = []
        for slot, via, there, within_chip, device in over_w:
            there = there & within_chip if slot in turned[which] else there
            found.append((slot, slot, via, there, device))
        for slot, via, there, device in over_t:
            if slot in turned[which]:
                found.append((slot + 4, slot, via, there, device))
        return found

    near, far = (3, 4), (5, 6, 7, 8)
    q_ref, k_ref, v_ref = qkv_ref.at[0], qkv_ref.at[1], qkv_ref.at[2]

    def slot_of(which, slot):
        if which == 4:
            return st_all.at[slot]
        dest = (k_all, v_all, q_all, g_all)[which]
        return dest.at[:, slot * block : (slot + 1) * block, :]

    def remote(which, source, slot, device, lane=None):
        return pltpu.make_async_remote_copy(
            src_ref=source, dst_ref=slot_of(which, slot),
            send_sem=send_sem.at[which, slot if lane is None else lane],
            recv_sem=recv_sem.at[which, slot],
            device_id=device, device_id_type=MESH,
        )

    def send_direct(which, source):
        for slot, there, device in direct:
            @pl.when(there)
            def _():
                remote(which, source, slot, device).start()

    def send_onward(which, vias):
        receive(which, vias)
        for lane, slot, via, there, device in routes(which):
            if via in vias:
                @pl.when(there)
                def _():
                    remote(which, slot_of(which, via), slot, device, lane).start()

    def receive(which, slots):
        for slot in slots:
            @pl.when(exists[slot])
            def _():
                remote(which, slot_of(which, slot), slot, peer).wait_recv()

    def sent(which, source):
        for slot, there, device in direct:
            @pl.when(there)
            def _():
                remote(which, source, slot, device).wait_send()
        for lane, slot, via, there, device in routes(which):
            @pl.when(there)
            def _():
                remote(which, slot_of(which, via), slot, device, lane).wait_send()

    def swap(index, source, dest):
        return pltpu.make_async_remote_copy(
            src_ref=source, dst_ref=dest, send_sem=peer_send.at[index],
            recv_sem=peer_recv.at[index], device_id=peer, device_id_type=MESH,
        )

    def w_copy(hop):
        dest = lax.rem(w_index + hop, w_count)
        return pltpu.make_async_remote_copy(
            src_ref=terms.at[dest], dst_ref=in_w.at[hop - 1],
            send_sem=w_send.at[hop - 1], recv_sem=w_recv.at[hop - 1],
            device_id=(t_index, dest, h_index), device_id_type=MESH,
        )

    def t_copy(hop):
        dest = lax.rem(t_index + hop, t_count)
        return pltpu.make_async_remote_copy(
            src_ref=send_t.at[dest], dst_ref=in_t.at[hop - 1],
            send_sem=t_send.at[hop - 1], recv_sem=t_recv.at[hop - 1],
            device_id=(dest, w_index, h_index), device_id_type=MESH,
        )

    own = [
        pltpu.make_async_copy(source, dest, own_sem.at[index])
        for index, (source, dest) in enumerate((
            (k_ref, slot_of(0, 0)), (v_ref, slot_of(1, 0)), (q_ref, slot_of(2, 0)),
            (gm_hbm, gm), (w_hbm, weight),
        ))
    ]
    for copy in own:
        copy.start()

    barrier = pltpu.get_barrier_semaphore()
    partners = [(there, device) for _, there, device in direct]
    for there, device in partners:
        @pl.when(there)
        def _():
            pl.semaphore_signal(barrier, inc=1, device_id=device, device_id_type=MESH)
    pl.semaphore_signal(barrier, inc=1, device_id=peer, device_id_type=MESH)
    greeted = 1 + sum(jnp.where(there, 1, 0) for there, _ in partners)
    for hop in range(1, w_count):
        dest = lax.rem(w_index + hop, w_count)
        pl.semaphore_signal(
            barrier, inc=1, device_id=(t_index, dest, h_index), device_id_type=MESH
        )
    for hop in range(1, t_count):
        dest = lax.rem(t_index + hop, t_count)
        pl.semaphore_signal(
            barrier, inc=1, device_id=(dest, w_index, h_index), device_id_type=MESH
        )
    pl.semaphore_wait(barrier, greeted + w_count + t_count - 2)

    send_direct(0, k_ref)

    fill = jnp.zeros((tiles, wide - 9 * block, depth), jnp.bfloat16)
    hole = jnp.zeros((tiles, block, depth), jnp.bfloat16)
    for dest in (k_all, v_all, q_all, g_all):
        dest[:, 9 * block :, :] = fill
        for slot in range(1, 9):
            @pl.when(jnp.logical_not(exists[slot]))
            def _():
                dest[:, slot * block : (slot + 1) * block, :] = hole

    places = lax.broadcasted_iota(jnp.int32, (8, wide), 1)
    inside = jnp.zeros((8, wide), jnp.float32)
    within = jnp.zeros((8, wide), jnp.int32)
    for slot in range(9):
        here = (places >= slot * block) & (places < slot * block + count)
        there = 1.0 if slot == 0 else jnp.where(exists[slot], 1.0, 0.0)
        inside = jnp.where(here, there, inside)
        within = jnp.where(here, places - slot * block, within)
    rows = row_within(within.astype(jnp.float32))
    for tile in range(tiles):
        allowed = jnp.zeros((8, wide), jnp.float32)
        for row in range(TH):
            valid = jnp.where(valid_ref[tile * TH + row] > 0, 1.0, 0.0)
            allowed = jnp.where(rows == row, valid, allowed)
        bias[tile] = jnp.where(allowed * inside > 0, 0.0, -FAR)

    send_direct(1, v_ref)
    for copy in own:
        copy.wait()
    first = h_index == 0
    cells, high = gm.shape[0] // tall, mixed_ref.shape[1]
    step = 6 * tall

    @pl.loop(0, cells // 6)
    def _(piece):
        span = pl.ds(pl.multiple_of(piece * step, step), step)
        flat[span, :] = dot_nt(gm[span, :], weight[...]).astype(jnp.bfloat16)

    spots = lax.broadcasted_iota(jnp.int32, (block, gm.shape[0]), 1)
    order = lax.broadcasted_iota(jnp.int32, (block, gm.shape[0]), 0).astype(jnp.float32)
    groups = jnp.floor((order + 0.5) * (1.0 / TH))
    source_spot = (groups * (tall - TH) + order).astype(jnp.int32)
    source_spot = jnp.where(order < count, source_spot, -high)

    @pl.loop(0, tiles)
    def _(tile):
        pick = jnp.where(spots == source_spot + tile * TH, 1.0, 0.0).astype(jnp.bfloat16)
        parts = jnp.dot(pick, flat[...], preferred_element_type=jnp.float32).astype(jnp.bfloat16)
        part_own[tile] = jnp.where(first, parts[:, :depth], parts[:, depth:])
        part_other[tile] = jnp.where(first, parts[:, depth:], parts[:, :depth])

    swap(0, part_other, part_in).start()

    top[...] = jnp.full(top.shape, -3e38, jnp.float32)
    out[...] = jnp.zeros(out.shape, jnp.float32)
    grad[...] = jnp.zeros(grad.shape, jnp.float32)
    ones = jnp.ones((wide, depth), jnp.bfloat16)

    def over_pairs(body):
        @pl.loop(0, tiles)
        def _(tile):
            @pl.loop(jnp.maximum(tile - 1, 0), jnp.minimum(tile + 1, tiles - 1) + 1)
            def _(row):
                body(tile, row)

    def score_part(start, size):
        def body(tile, row):
            keys = k_all[row, start : start + size, :]
            scores = dot_nt(q_all[tile, :block, :], keys) * (scale * LOG2E)
            scores = scores + bias[row, 0:1, start : start + size]
            s_buf[2 * tile + row, :, start : start + size] = scores
            best = top[tile]
            for lane in range(0, size, 128):
                best = jnp.maximum(best, scores[:, lane : lane + 128])
            top[tile] = best
        over_pairs(body)

    def value_part(start, size):
        def body(tile, row):
            span = slice(start, start + size)
            expos = jnp.exp2(s_buf[2 * tile + row, :, span] - top[tile][:, :1])
            s_buf[2 * tile + row, :, span] = expos
            values = jnp.concatenate([v_all[row, span, :], ones[:size]], axis=1)
            out[tile] += jnp.dot(
                expos.astype(jnp.bfloat16), values, preferred_element_type=jnp.float32
            )
        over_pairs(body)

    def query_part(start, size):
        def body(tile, row):
            span = slice(start, start + size)
            dprob = dot_nt(g_all[tile, :block, :], v_all[row, span, :])
            dscore = s_buf[2 * tile + row, :, span] * (dprob - grad_k[tile][:, :1])
            grad[tile] += jnp.dot(
                dscore.astype(jnp.bfloat16), k_all[row, span, :],
                preferred_element_type=jnp.float32,
            )
        over_pairs(body)

    def key_part(start, size):
        def body(tile, row):
            span = slice(start, start + size)
            queries, grads = q_all[row, span, :], g_all[row, span, :]
            lse, delta = stats[row, 0:1, span], stats[row, 1:2, span]
            probs = jnp.exp2(
                dot_nt(k_all[tile, :block, :], queries) * (scale * LOG2E) - lse
            )
            grad_v[tile] += jnp.dot(
                probs.astype(jnp.bfloat16), grads, preferred_element_type=jnp.float32
            )
            dscore = probs * (dot_nt(v_all[tile, :block, :], grads) - delta)
            grad_k[tile] += jnp.dot(
                dscore.astype(jnp.bfloat16), queries, preferred_element_type=jnp.float32
            )
        over_pairs(body)

    send_onward(0, (1, 2))
    send_onward(0, near)
    score_part(*halves[0])
    send_onward(1, (1, 2))
    send_onward(1, near)
    send_direct(2, q_ref)
    swap(0, part_other, part_in).wait()
    g_all[:, :block, :] = (
        part_own[...].astype(jnp.float32) + part_in[...].astype(jnp.float32)
    ).astype(jnp.bfloat16)
    send_direct(3, slot_of(3, 0))
    receive(0, far)
    score_part(*halves[1])

    @pl.loop(0, tiles)
    def _(tile):
        peak = jnp.max(top[tile], axis=1, keepdims=True)
        top[tile] = jnp.broadcast_to(peak, top.shape[1:])

    value_part(*halves[0])
    send_onward(2, (1, 2))
    send_onward(2, near)
    receive(1, far)
    value_part(*halves[1])
    send_onward(3, (1, 2))
    send_onward(3, near)

    @pl.loop(0, tiles)
    def _(tile):
        total = out[tile][:, depth:]
        attended = (out[tile][:, :depth] / total).astype(jnp.bfloat16)
        att_ref[tile] = attended
        grads = g_all[tile, :block, :]
        delta = jnp.sum(
            grads.astype(jnp.float32) * attended.astype(jnp.float32), axis=1, keepdims=True
        )
        lanes = lax.broadcasted_iota(jnp.int32, (block, 128), 1)
        columns = jnp.where(lanes == 0, top[tile] + jnp.log2(total), delta)
        span = st_own.shape[-1]
        columns = jnp.concatenate([columns, jnp.zeros((span - block, 128), jnp.float32)], axis=0)
        st_own[tile] = columns.T[:8]
        grad_k[tile] = jnp.broadcast_to(delta, grad_k.shape[1:])

    swap(1, att_ref, att_in).start()
    send_direct(4, st_own)
    query_part(*halves[0])
    send_onward(4, (1, 2))
    query_part(*halves[1])

    @pl.loop(0, tiles)
    def _(tile):
        gq_ref[tile] = (grad[tile] * (scale / out[tile][:, depth:])).astype(jnp.bfloat16)

    swap(1, att_ref, att_in).wait()
    own_att, other_att = (
        jnp.where(first, att_ref[...], att_in[...]), jnp.where(first, att_in[...], att_ref[...])
    )
    heads = jnp.concatenate([own_att, other_att], axis=2).reshape(tiles * block, 2 * depth)
    spots = lax.broadcasted_iota(jnp.int32, (step, tiles * block), 0)
    columns = lax.broadcasted_iota(jnp.int32, (step, tiles * block), 1)
    goal_spot = jnp.full((step, tiles * block), -step * cells, jnp.int32)
    for tile in range(tiles):
        place = columns - tile * block
        groups = jnp.floor((place.astype(jnp.float32) + 0.5) * (1.0 / TH)).astype(jnp.int32)
        here = (place >= 0) & (place < count)
        goal_spot = jnp.where(here, groups * (tall - TH) + place + tile * TH, goal_spot)

    @pl.loop(0, cells // 6)
    def _(piece):
        pick = jnp.where(spots + piece * step == goal_spot, 1.0, 0.0).astype(jnp.bfloat16)
        moved = jnp.dot(pick, heads, preferred_element_type=jnp.float32)
        flat[pl.ds(pl.multiple_of(piece * step, step), step), :] = moved.astype(jnp.bfloat16)

    share_rows, width = share_ref.shape
    for start in range(0, width, 512):
        result = lax.dot_general(
            flat[...], gm[:, start : start + 512], (((0,), (0,)), ((), ())),
            preferred_element_type=jnp.float32,
        )
        for part in range(t_count * w_count):
            terms[part % w_count, part // w_count, :, start : start + 512] = result[
                part * share_rows : (part + 1) * share_rows
            ].astype(jnp.bfloat16)
    for hop in range(1, w_count):
        w_copy(hop).start()

    first_row = lax.broadcasted_iota(jnp.int32, (tiles, 8, wide), 1) == 0
    stats[...] = jnp.where(first_row, FAR, 0.0)
    stats[:, :, :block] = st_own[:, :, :block]

    def note(slots):
        for slot in slots:
            @pl.when(exists[slot])
            def _():
                stats[:, :, slot * block : (slot + 1) * block] = st_all[slot, :, :, :block]

    grad_k[...] = jnp.zeros(grad_k.shape, jnp.float32)
    grad_v[...] = jnp.zeros(grad_v.shape, jnp.float32)
    receive(4, near)
    note((1, 2, 3, 4))
    key_part(*halves[0])

    def put(piece, slot):
        return pltpu.make_async_copy(
            stage.at[slot], mixed_ref.at[pl.ds(piece * 6, 6)], out_sem.at[slot]
        )

    for piece in range(cells // 6):
        slot = piece % 2
        if piece >= 2:
            put(piece - 2, slot).wait()
        result = jnp.dot(
            flat[piece * step : (piece + 1) * step, :], weight[...],
            preferred_element_type=jnp.float32,
        ).astype(jnp.bfloat16)
        for cell in range(6):
            stage[slot, cell] = result[cell * tall : cell * tall + high]
        put(piece, slot).start()

    whole = terms[w_index].astype(jnp.float32)
    for hop in range(1, w_count):
        w_copy(hop).wait()
        whole = whole + in_w[hop - 1].astype(jnp.float32)
    sum_w[...] = whole
    send_t[...] = whole.astype(jnp.bfloat16)
    for hop in range(1, t_count):
        t_copy(hop).start()

    for which in (2, 3, 4):
        receive(which, far)
    note(far)
    key_part(*halves[1])

    places = lax.broadcasted_iota(jnp.int32, (block, 128), 0)
    rows = row_within(places.astype(jnp.float32))
    for tile in range(tiles):
        live = jnp.zeros((block, 128), jnp.float32)
        for row in range(TH):
            valid = jnp.where(valid_ref[tile * TH + row] > 0, 1.0, 0.0)
            live = jnp.where(rows == row, valid, live)
        gk_ref[tile] = jnp.where(live > 0, grad_k[tile] * scale, 0.0).astype(jnp.bfloat16)
        gv_ref[tile] = jnp.where(live > 0, grad_v[tile], 0.0).astype(jnp.bfloat16)

    for piece in range(cells // 6 - 2, cells // 6):
        put(piece, piece % 2).wait()
    share = sum_w[t_index]
    for hop in range(1, t_count):
        t_copy(hop).wait()
        share = share + in_t[hop - 1].astype(jnp.float32)
    share_ref[...] = share
    for which, source in enumerate((k_ref, v_ref, q_ref, slot_of(3, 0), st_own)):
        sent(which, source)


def lay_out(cells, block, tile_rows):
    frames, columns, rows, depth = cells.shape
    tiles = rows // tile_rows
    cells = cells.reshape(frames * columns, tiles, tile_rows, depth).transpose(1, 0, 2, 3)
    cells = cells.reshape(tiles, frames * columns * tile_rows, depth)
    return jnp.pad(cells, ((0, 0), (0, block - cells.shape[1]), (0, 0)))


def lay_back(cells, frames, columns, tile_rows):
    tiles, _, depth = cells.shape
    count = frames * columns
    cells = cells[:, : count * tile_rows].reshape(tiles, count, tile_rows, depth)
    return cells.transpose(1, 0, 2, 3).reshape(frames, columns, tiles * tile_rows, depth)


def shards(query_heads, key_heads, value_heads, row_valid, out_weight, grad_mixed):
    frames, rows, columns, depth = query_heads.shape
    scale = 1.0 / math.sqrt(depth)
    tiles = rows // TH
    count = frames * columns * TH
    block = round_up(count, 16)
    wide = round_up(9 * block, 256)
    swap = (0, 2, 1, 3)
    qkv = jnp.stack([query_heads.transpose(swap), key_heads.transpose(swap), value_heads.transpose(swap)])
    qkv = jax.vmap(lambda cells: lay_out(cells, block, TH))(qkv)
    tall = round_up(rows, 16)
    cells = frames * columns
    grad_in = jnp.pad(grad_mixed.transpose(swap), ((0, 0), (0, 0), (0, tall - rows), (0, 0)))
    grad_in = grad_in.reshape(cells * tall, grad_mixed.shape[-1])
    t_count, w_count = lax.axis_size("tm"), lax.axis_size("width")
    share_rows, width = out_weight.shape[0] // (t_count * w_count), out_weight.shape[1]

    pairs = tiles * 3 - 2
    work = pairs * block * wide
    in_vmem = pl.BlockSpec(memory_space=pltpu.VMEM)
    anywhere = pl.BlockSpec(memory_space=pl.ANY)
    flat = jax.ShapeDtypeStruct((tiles, block, depth), jnp.bfloat16)
    bf16 = lambda *shape: pltpu.VMEM(shape, jnp.bfloat16)
    f32 = lambda *shape: pltpu.VMEM(shape, jnp.float32)
    dma = lambda *shape: pltpu.SemaphoreType.DMA(shape)
    span = round_up(block, 128)
    mixed, grad_query, grad_key, grad_value, grad_weight = pl.pallas_call(
        functools.partial(
            attention_kernel, tiles=tiles, block=block, wide=wide, count=count, tall=tall,
            scale=scale,
        ),
        out_shape=(
            jax.ShapeDtypeStruct((cells, rows, width), jnp.bfloat16), flat, flat, flat,
            jax.ShapeDtypeStruct((share_rows, width), jnp.float32),
        ),
        in_specs=[pl.BlockSpec(memory_space=pltpu.SMEM)] + [anywhere] * 3,
        out_specs=(anywhere,) + (in_vmem,) * 4,
        scratch_shapes=[
            bf16(tiles, wide, depth), bf16(tiles, wide, depth),
            bf16(tiles, wide, depth), bf16(tiles, wide, depth),
            f32(pairs, block, wide), f32(tiles, 8, wide), f32(tiles, block, 128),
            f32(tiles, block, 2 * depth), f32(tiles, block, depth),
            f32(tiles, block, depth), f32(tiles, block, depth),
            bf16(cells * tall, width), bf16(2 * depth, width),
            bf16(cells * tall, 2 * depth), bf16(tiles, block, depth),
            bf16(tiles, block, depth), bf16(tiles, block, depth), bf16(tiles, block, depth),
            bf16(tiles, block, depth),
            f32(tiles, 8, span), f32(9, tiles, 8, span), f32(tiles, 8, wide),
            bf16(w_count, t_count, share_rows, width),
            bf16(w_count - 1, t_count, share_rows, width),
            bf16(t_count - 1, share_rows, width),
            f32(t_count, share_rows, width), bf16(t_count, share_rows, width),
            bf16(2, 6, rows, width),
            dma(5, 13), dma(5, 9), dma(5), dma(2), dma(2),
            dma(w_count - 1), dma(w_count - 1), dma(t_count - 1), dma(t_count - 1),
            dma(2),
        ],
        compiler_params=pltpu.CompilerParams(
            vmem_limit_bytes=58 << 20, collective_id=0, has_side_effects=True
        ),
        cost_estimate=pl.CostEstimate(
            flops=16 * work * depth, transcendentals=2 * work,
            bytes_accessed=4 * tiles * wide * depth,
        ),
        name="attention",
    )(row_valid, qkv, grad_in, out_weight)

    mixed = mixed.reshape(frames, columns, rows, width)
    back = lambda cells: lay_back(cells, frames, columns, TH).transpose(swap)
    return (mixed.transpose(swap), back(grad_query), back(grad_key), back(grad_value), grad_weight)


def solution(mesh):
    split = P("tm", None, "width", "head")
    return jax.shard_map(
        shards,
        mesh=mesh,
        in_specs=(split, split, split, P(), P(None, "head"), split),
        out_specs=(split, split, split, split, P(("tm", "width"), "head")),
        check_vma=False,
    )
```

```python
import functools
import math

import jax
import jax.numpy as jnp
from jax import lax
from jax.experimental import pallas as pl
from jax.experimental.pallas import tpu as pltpu
from jax.sharding import PartitionSpec as P

TH = 9
FAR = 1e30
LOG2E = 1.4426950408889634


def round_up(value, step):
    return -(-value // step) * step


def dot_nt(left, right):
    return lax.dot_general(
        left, right, (((1,), (1,)), ((), ())), preferred_element_type=jnp.float32
    )


MESH = pl.DeviceIdType.MESH


def row_within(places):
    return places - TH * jnp.floor((places + 0.5) * (1.0 / TH))


def goal_spots(tiles, block, count, tall, none):
    columns = lax.broadcasted_iota(jnp.int32, (8, tiles * block), 1)
    goal = jnp.full((8, tiles * block), none, jnp.int32)
    for tile in range(tiles):
        place = columns - tile * block
        groups = jnp.floor((place.astype(jnp.float32) + 0.5) * (1.0 / TH)).astype(jnp.int32)
        here = (place >= 0) & (place < count)
        goal = jnp.where(here, groups * (tall - TH) + place + tile * TH, goal)
    return goal[0:1]


def picked(spots, goal):
    return jnp.where(spots == goal, 1.0, 0.0).astype(jnp.bfloat16)


def attention_kernel(
    valid_ref, q_hbm, k_hbm, v_hbm, gm_hbm, w_hbm,
    all_ref, share_ref,
    k_all, v_all, q_all, g_all, q_own, k_own, v_own, g_own,
    s_buf, bias, top, out, grad_k, grad_v, landed, tall_qkv, gm_land,
    gm, weight, flat_t, att_ref, part_other, part_in, att_in,
    st_own, st_all, stats, terms, in_w, in_t, sum_w, send_t,
    send_sem, recv_sem, own_sem, gm_sem, peer_send, peer_recv, w_send, w_recv, t_send, t_recv,
    *, tiles, block, wide, count, tall, scale,
):
    depth = q_all.shape[-1]
    half = wide // 2
    halves = ((0, half), (half, half))
    t_index, w_index, h_index = (lax.axis_index(name) for name in ("tm", "width", "head"))
    t_count, w_count = lax.axis_size("tm"), lax.axis_size("width")
    t_back, t_ahead = t_index > 0, t_index < t_count - 1
    w_back, w_ahead = w_index > 0, w_index < w_count - 1
    exists = [
        None, t_back, t_ahead, w_back, w_ahead,
        t_back & w_back, t_ahead & w_back, t_back & w_ahead, t_ahead & w_ahead,
    ]
    t_above = (t_index + 1, w_index, h_index)
    t_below = (t_index - 1, w_index, h_index)
    w_above = (t_index, w_index + 1, h_index)
    w_below = (t_index, w_index - 1, h_index)
    peer = (t_index, w_index, 1 - h_index)
    direct = [(1, t_ahead, t_above), (2, t_back, t_below), (3, w_ahead, w_above), (4, w_back, w_below)]
    even = lax.rem(w_index, 2) == 0
    odd = jnp.logical_not(even)
    over_w = [
        (5, 1, t_back & w_ahead, even, w_above), (7, 1, t_back & w_back, odd, w_below),
        (6, 2, t_ahead & w_ahead, even, w_above), (8, 2, t_ahead & w_back, odd, w_below),
    ]
    over_t = [
        (5, 3, t_ahead & w_back & even, t_above), (7, 4, t_ahead & w_ahead & odd, t_above),
        (6, 3, t_back & w_back & even, t_below), (8, 4, t_back & w_ahead & odd, t_below),
    ]
    turned = ((5, 7), (6, 8), (5, 7), (6, 8), ())

    def routes(which):
        found = []
        for slot, via, there, within_chip, device in over_w:
            there = there & within_chip if slot in turned[which] else there
            found.append((slot, slot, via, there, device))
        for slot, via, there, device in over_t:
            if slot in turned[which]:
                found.append((slot + 4, slot, via, there, device))
        return found

    near, far = (3, 4), (5, 6, 7, 8)
    cells, high = landed.shape[1], landed.shape[2]
    group = gm_land.shape[1]
    pieces, step = cells // group, group * tall

    def slot_of(which, slot):
        if which == 4:
            return st_all.at[slot]
        dest = (k_all, v_all, q_all, g_all)[which]
        return dest.at[:, slot * block : (slot + 1) * block, :]

    def remote(which, source, slot, device, lane=None):
        return pltpu.make_async_remote_copy(
            src_ref=source, dst_ref=slot_of(which, slot),
            send_sem=send_sem.at[which, slot if lane is None else lane],
            recv_sem=recv_sem.at[which, slot],
            device_id=device, device_id_type=MESH,
        )

    def send_direct(which, source):
        for slot, there, device in direct:
            @pl.when(there)
            def _():
                remote(which, source, slot, device).start()

    def send_onward(which, vias):
        receive(which, vias)
        for lane, slot, via, there, device in routes(which):
            if via in vias:
                @pl.when(there)
                def _():
                    remote(which, slot_of(which, via), slot, device, lane).start()

    def receive(which, slots):
        for slot in slots:
            @pl.when(exists[slot])
            def _():
                remote(which, slot_of(which, slot), slot, peer).wait_recv()

    def sent(which, source):
        for slot, there, device in direct:
            @pl.when(there)
            def _():
                remote(which, source, slot, device).wait_send()
        for lane, slot, via, there, device in routes(which):
            @pl.when(there)
            def _():
                remote(which, slot_of(which, via), slot, device, lane).wait_send()

    def swap(index, source, dest):
        return pltpu.make_async_remote_copy(
            src_ref=source, dst_ref=dest, send_sem=peer_send.at[index],
            recv_sem=peer_recv.at[index], device_id=peer, device_id_type=MESH,
        )

    def w_copy(hop):
        dest = lax.rem(w_index + hop, w_count)
        return pltpu.make_async_remote_copy(
            src_ref=terms.at[dest], dst_ref=in_w.at[hop - 1],
            send_sem=w_send.at[hop - 1], recv_sem=w_recv.at[hop - 1],
            device_id=(t_index, dest, h_index), device_id_type=MESH,
        )

    def t_copy(hop):
        dest = lax.rem(t_index + hop, t_count)
        return pltpu.make_async_remote_copy(
            src_ref=send_t.at[dest], dst_ref=in_t.at[hop - 1],
            send_sem=t_send.at[hop - 1], recv_sem=t_recv.at[hop - 1],
            device_id=(dest, w_index, h_index), device_id_type=MESH,
        )

    own = [
        pltpu.make_async_copy(source, dest, own_sem.at[index])
        for index, (source, dest) in enumerate((
            (q_hbm, landed.at[0]), (k_hbm, landed.at[1]), (v_hbm, landed.at[2]), (w_hbm, weight),
        ))
    ]
    for copy in own:
        copy.start()

    def gm_copy(piece):
        return pltpu.make_async_copy(
            gm_hbm.at[pl.ds(piece * group, group)], gm_land.at[piece % 2], gm_sem.at[piece % 2]
        )

    for piece in range(2):
        gm_copy(piece).start()

    barrier = pltpu.get_barrier_semaphore()
    partners = [(there, device) for _, there, device in direct]
    for there, device in partners:
        @pl.when(there)
        def _():
            pl.semaphore_signal(barrier, inc=1, device_id=device, device_id_type=MESH)
    pl.semaphore_signal(barrier, inc=1, device_id=peer, device_id_type=MESH)
    greeted = 1 + sum(jnp.where(there, 1, 0) for there, _ in partners)
    for hop in range(1, w_count):
        dest = lax.rem(w_index + hop, w_count)
        pl.semaphore_signal(
            barrier, inc=1, device_id=(t_index, dest, h_index), device_id_type=MESH
        )
    for hop in range(1, t_count):
        dest = lax.rem(t_index + hop, t_count)
        pl.semaphore_signal(
            barrier, inc=1, device_id=(dest, w_index, h_index), device_id_type=MESH
        )

    spots = lax.broadcasted_iota(jnp.int32, (block, cells * tall), 1)
    order = lax.broadcasted_iota(jnp.int32, (block, 128), 0).astype(jnp.float32)
    groups = jnp.floor((order + 0.5) * (1.0 / TH))
    goal = (groups * (tall - TH) + order).astype(jnp.int32)
    goal = jnp.where(order < count, goal, -2 * high)[:, :1]
    tall_qkv[...] = jnp.zeros(tall_qkv.shape, jnp.bfloat16)
    for copy in own[:3]:
        copy.wait()

    @pl.loop(0, cells)
    def _(cell):
        span = pl.ds(pl.multiple_of(cell * tall, tall), high)
        for index in range(3):
            tall_qkv[span, index * depth : (index + 1) * depth] = landed[index, cell]

    @pl.loop(0, tiles)
    def _(tile):
        moved = jnp.dot(
            picked(spots, goal + tile * TH), tall_qkv[...], preferred_element_type=jnp.float32
        ).astype(jnp.bfloat16)
        for index, (mine, dest) in enumerate(((q_own, q_all), (k_own, k_all), (v_own, v_all))):
            part = moved[:, index * depth : (index + 1) * depth]
            mine[tile] = part
            dest[tile, :block, :] = part

    pl.semaphore_wait(barrier, greeted + w_count + t_count - 2)
    send_direct(0, k_own)

    fill = jnp.zeros((tiles, wide - 9 * block, depth), jnp.bfloat16)
    hole = jnp.zeros((tiles, block, depth), jnp.bfloat16)
    for dest in (k_all, v_all, q_all, g_all):
        dest[:, 9 * block :, :] = fill
        for slot in range(1, 9):
            @pl.when(jnp.logical_not(exists[slot]))
            def _():
                dest[:, slot * block : (slot + 1) * block, :] = hole

    places = lax.broadcasted_iota(jnp.int32, (8, wide), 1)
    inside = jnp.zeros((8, wide), jnp.float32)
    within = jnp.zeros((8, wide), jnp.int32)
    for slot in range(9):
        here = (places >= slot * block) & (places < slot * block + count)
        there = 1.0 if slot == 0 else jnp.where(exists[slot], 1.0, 0.0)
        inside = jnp.where(here, there, inside)
        within = jnp.where(here, places - slot * block, within)
    rows = row_within(within.astype(jnp.float32))
    for tile in range(tiles):
        allowed = jnp.zeros((8, wide), jnp.float32)
        for row in range(TH):
            valid = jnp.where(valid_ref[tile * TH + row] > 0, 1.0, 0.0)
            allowed = jnp.where(rows == row, valid, allowed)
        bias[tile] = jnp.where(allowed * inside > 0, 0.0, -FAR)

    send_direct(1, v_own)
    own[3].wait()
    first = h_index == 0

    for piece in range(pieces):
        gm_copy(piece).wait()

        @pl.loop(0, group)
        def _(cell):
            low = piece * step + cell * tall
            gm[pl.ds(pl.multiple_of(low + tall - 16, 16), 16), :] = jnp.zeros(
                (16, gm.shape[1]), jnp.bfloat16
            )
            gm[pl.ds(pl.multiple_of(low, 16), high), :] = gm_land[piece % 2, cell]

        span = slice(piece * step, (piece + 1) * step)
        tall_qkv[span, : 2 * depth] = dot_nt(gm[span, :], weight[...]).astype(jnp.bfloat16)
        if piece + 2 < pieces:
            gm_copy(piece + 2).start()

    @pl.loop(0, tiles)
    def _(tile):
        pick = picked(spots, goal + tile * TH)
        parts = jnp.dot(pick, tall_qkv[:, : 2 * depth], preferred_element_type=jnp.float32).astype(jnp.bfloat16)
        g_own[tile] = jnp.where(first, parts[:, :depth], parts[:, depth:])
        part_other[tile] = jnp.where(first, parts[:, depth:], parts[:, :depth])

    swap(0, part_other, part_in).start()

    top[...] = jnp.full(top.shape, -3e38, jnp.float32)
    out[...] = jnp.zeros(out.shape, jnp.float32)
    grad_v[...] = jnp.zeros(grad_v.shape, jnp.float32)
    ones = jnp.ones((wide, depth), jnp.bfloat16)

    def over_rows(body):
        @pl.loop(0, 2)
        def _(end):
            body(end * (tiles - 1), end * (tiles - 2), 2)

        @pl.loop(1, tiles - 1)
        def _(row):
            body(row, row - 1, 2)
            body(row, row + 1, 1)

    def score_part(start, size):
        span = slice(start, start + size)

        def body(row, low, some):
            mine = pl.ds(low, some)
            queries = q_own[mine].reshape(some * block, depth)
            scores = dot_nt(queries, k_all[row, span, :]) * (scale * LOG2E)
            scores = scores + bias[row, 0:1, span]
            s_buf[pl.ds(2 * row + low, some), :, span] = scores.reshape(some, block, size)
            best = top[mine].reshape(some * block, 128)
            for lane in range(0, size, 128):
                best = jnp.maximum(best, scores[:, lane : lane + 128])
            top[mine] = best.reshape(some, block, 128)
        over_rows(body)

    def value_part(start, size):
        span = slice(start, start + size)

        def body(row, low, some):
            mine, slots = pl.ds(low, some), pl.ds(2 * row + low, some)
            peaks = top[mine].reshape(some * block, 128)[:, :1]
            expos = jnp.exp2(s_buf[slots, :, span].reshape(some * block, size) - peaks)
            s_buf[slots, :, span] = expos.reshape(some, block, size)
            values = jnp.concatenate([v_all[row, span, :], ones[:size]], axis=1)
            out[mine] += jnp.dot(
                expos.astype(jnp.bfloat16), values, preferred_element_type=jnp.float32
            ).reshape(some, block, 2 * depth)
        over_rows(body)

    def query_part(start, size):
        span = slice(start, start + size)

        def body(row, low, some):
            mine, slots = pl.ds(low, some), pl.ds(2 * row + low, some)
            deltas = grad_k[mine].reshape(some * block, depth)[:, :1]
            dprob = dot_nt(g_own[mine].reshape(some * block, depth), v_all[row, span, :])
            dscore = s_buf[slots, :, span].reshape(some * block, size) * (dprob - deltas)
            grad_v[mine] += jnp.dot(
                dscore.astype(jnp.bfloat16), k_all[row, span, :],
                preferred_element_type=jnp.float32,
            ).reshape(some, block, depth)
        over_rows(body)

    def key_part(start, size):
        span = slice(start, start + size)

        def body(row, low, some):
            mine = pl.ds(low, some)
            queries, grads = q_all[row, span, :], g_all[row, span, :]
            lse, delta = stats[row, 0:1, span], stats[row, 1:2, span]
            keys = k_own[mine].reshape(some * block, depth)
            values = v_own[mine].reshape(some * block, depth)
            probs = jnp.exp2(dot_nt(keys, queries) * (scale * LOG2E) - lse)
            grad_v[mine] += jnp.dot(
                probs.astype(jnp.bfloat16), grads, preferred_element_type=jnp.float32
            ).reshape(some, block, depth)
            dscore = probs * (dot_nt(values, grads) - delta)
            grad_k[mine] += jnp.dot(
                dscore.astype(jnp.bfloat16), queries, preferred_element_type=jnp.float32
            ).reshape(some, block, depth)
        over_rows(body)

    send_onward(0, (1, 2))
    send_onward(0, near)
    score_part(*halves[0])
    send_onward(1, (1, 2))
    send_onward(1, near)
    send_direct(2, q_own)
    swap(0, part_other, part_in).wait()
    grads = (
        g_own[...].astype(jnp.float32) + part_in[...].astype(jnp.float32)
    ).astype(jnp.bfloat16)
    g_own[...] = grads
    g_all[:, :block, :] = grads
    send_direct(3, g_own)
    receive(0, far)
    score_part(*halves[1])

    @pl.loop(0, tiles)
    def _(tile):
        peak = jnp.max(top[tile], axis=1, keepdims=True)
        top[tile] = jnp.broadcast_to(peak, top.shape[1:])

    value_part(*halves[0])
    send_onward(2, (1, 2))
    send_onward(2, near)
    receive(1, far)
    value_part(*halves[1])
    send_onward(3, (1, 2))
    send_onward(3, near)

    @pl.loop(0, tiles)
    def _(tile):
        total = out[tile][:, depth:]
        attended = (out[tile][:, :depth] / total).astype(jnp.bfloat16)
        att_ref[tile] = attended
        grads = g_own[tile]
        delta = jnp.sum(
            grads.astype(jnp.float32) * attended.astype(jnp.float32), axis=1, keepdims=True
        )
        lanes = lax.broadcasted_iota(jnp.int32, (block, 128), 1)
        columns = jnp.where(lanes == 0, top[tile] + jnp.log2(total), delta)
        span = st_own.shape[-1]
        columns = jnp.concatenate([columns, jnp.zeros((span - block, 128), jnp.float32)], axis=0)
        st_own[tile] = columns.T[:8]
        grad_k[tile] = jnp.broadcast_to(delta, grad_k.shape[1:])

    swap(1, att_ref, att_in).start()
    send_direct(4, st_own)
    send_onward(4, (1, 2))
    query_part(*halves[0])
    query_part(*halves[1])

    @pl.loop(0, tiles)
    def _(tile):
        all_ref[tile, :, 2 * depth : 3 * depth] = (
            grad_v[tile] * (scale / out[tile][:, depth:])
        ).astype(jnp.bfloat16)

    swap(1, att_ref, att_in).wait()
    own_att, other_att = (
        jnp.where(first, att_ref[...], att_in[...]), jnp.where(first, att_in[...], att_ref[...])
    )
    all_ref[:, :, :depth] = own_att
    all_ref[:, :, depth : 2 * depth] = other_att
    heads = all_ref[:, :, : 2 * depth].reshape(tiles * block, 2 * depth)
    spots = lax.broadcasted_iota(jnp.int32, (step, tiles * block), 0)
    goal = goal_spots(tiles, block, count, tall, -step * pieces)

    @pl.loop(0, pieces)
    def _(piece):
        pick = picked(spots, goal - piece * step)
        moved = jnp.dot(pick, heads, preferred_element_type=jnp.float32)
        tall_qkv[pl.ds(pl.multiple_of(piece * step, step), step), : 2 * depth] = moved.astype(jnp.bfloat16)

    flat_t[...] = tall_qkv[:, : 2 * depth].astype(jnp.float32).T.astype(jnp.bfloat16)
    share_rows, width = share_ref.shape
    for start in range(0, width, 512):
        result = jnp.dot(
            flat_t[...], gm[:, start : start + 512], preferred_element_type=jnp.float32
        )
        for part in range(t_count * w_count):
            terms[part % w_count, part // w_count, :, start : start + 512] = result[
                part * share_rows : (part + 1) * share_rows
            ].astype(jnp.bfloat16)
    for hop in range(1, w_count):
        w_copy(hop).start()

    first_row = lax.broadcasted_iota(jnp.int32, (tiles, 8, wide), 1) == 0
    stats[...] = jnp.where(first_row, FAR, 0.0)
    stats[:, :, :block] = st_own[:, :, :block]

    def note(slots):
        for slot in slots:
            @pl.when(exists[slot])
            def _():
                stats[:, :, slot * block : (slot + 1) * block] = st_all[slot, :, :, :block]

    grad_k[...] = jnp.zeros(grad_k.shape, jnp.float32)
    grad_v[...] = jnp.zeros(grad_v.shape, jnp.float32)
    receive(4, near)
    note((1, 2, 3, 4))
    key_part(*halves[0])

    whole = terms[w_index].astype(jnp.float32)
    for hop in range(1, w_count):
        w_copy(hop).wait()
        whole = whole + in_w[hop - 1].astype(jnp.float32)
    sum_w[...] = whole
    send_t[...] = whole.astype(jnp.bfloat16)
    for hop in range(1, t_count):
        t_copy(hop).start()

    for which in (2, 3, 4):
        receive(which, far)
    note(far)
    key_part(*halves[1])

    places = lax.broadcasted_iota(jnp.int32, (block, 128), 0)
    rows = row_within(places.astype(jnp.float32))
    for tile in range(tiles):
        live = jnp.zeros((block, 128), jnp.float32)
        for row in range(TH):
            valid = jnp.where(valid_ref[tile * TH + row] > 0, 1.0, 0.0)
            live = jnp.where(rows == row, valid, live)
        all_ref[tile, :, 3 * depth : 4 * depth] = jnp.where(
            live > 0, grad_k[tile] * scale, 0.0
        ).astype(jnp.bfloat16)
        all_ref[tile, :, 4 * depth :] = jnp.where(
            live > 0, grad_v[tile], 0.0
        ).astype(jnp.bfloat16)

    share = sum_w[t_index]
    for hop in range(1, t_count):
        t_copy(hop).wait()
        share = share + in_t[hop - 1].astype(jnp.float32)
    share_ref[...] = share
    for which, source in enumerate((k_own, v_own, q_own, g_own, st_own)):
        sent(which, source)


def project_kernel(
    all_ref, w_ref, share_in, mixed_ref, gq_ref, gk_ref, gv_ref, share_ref,
    *, block, count, tall, depth,
):
    group, high = mixed_ref.shape[:2]
    total = all_ref.shape[0]
    step = group * tall
    goal = goal_spots(total // block, block, count, tall, -step * pl.num_programs(0))
    spots = lax.broadcasted_iota(jnp.int32, (step, total), 0)
    pick = picked(spots, goal - pl.program_id(0) * step)
    moved = jnp.dot(pick, all_ref[...], preferred_element_type=jnp.float32).astype(jnp.bfloat16)
    mixed = jnp.dot(
        moved[:, : 2 * depth], w_ref[...], preferred_element_type=jnp.float32
    ).astype(jnp.bfloat16)
    for cell in range(group):
        span = slice(cell * tall, cell * tall + high)
        mixed_ref[cell] = mixed[span]
        for index, dest in enumerate((gq_ref, gk_ref, gv_ref)):
            dest[cell] = moved[span, (2 + index) * depth : (3 + index) * depth]
    share_ref[...] = share_in[...]


def shards(query_heads, key_heads, value_heads, row_valid, out_weight, grad_mixed):
    frames, rows, columns, depth = query_heads.shape
    scale = 1.0 / math.sqrt(depth)
    tiles = rows // TH
    count = frames * columns * TH
    block = round_up(count, 16)
    wide = round_up(9 * block, 256)
    cells, tall = frames * columns, round_up(rows, 16)
    group = 6
    swap = (0, 2, 1, 3)
    native = lambda x: x.transpose(swap).reshape(cells, rows, x.shape[-1])
    t_count, w_count = lax.axis_size("tm"), lax.axis_size("width")
    share_rows, width = out_weight.shape[0] // (t_count * w_count), out_weight.shape[1]

    pairs = tiles * 3 - 2
    work = pairs * block * wide
    in_vmem = pl.BlockSpec(memory_space=pltpu.VMEM)
    anywhere = pl.BlockSpec(memory_space=pl.ANY)
    bf16 = lambda *shape: pltpu.VMEM(shape, jnp.bfloat16)
    f32 = lambda *shape: pltpu.VMEM(shape, jnp.float32)
    dma = lambda *shape: pltpu.SemaphoreType.DMA(shape)
    span = round_up(block, 128)
    results, share = pl.pallas_call(
        functools.partial(
            attention_kernel, tiles=tiles, block=block, wide=wide, count=count, tall=tall,
            scale=scale,
        ),
        out_shape=(
            jax.ShapeDtypeStruct((tiles, block, 5 * depth), jnp.bfloat16),
            jax.ShapeDtypeStruct((share_rows, width), jnp.float32),
        ),
        in_specs=[pl.BlockSpec(memory_space=pltpu.SMEM)] + [anywhere] * 5,
        out_specs=(in_vmem,) * 2,
        scratch_shapes=(
            [bf16(tiles, wide, depth)] * 4 + [bf16(tiles, block, depth)] * 4
            + [
                f32(pairs, block, wide), f32(tiles, 8, wide), f32(tiles, block, 128),
                f32(tiles, block, 2 * depth), f32(tiles, block, depth), f32(tiles, block, depth),
                bf16(3, cells, rows, depth), bf16(cells * tall, 3 * depth),
                bf16(2, group, rows, width),
                bf16(cells * tall, width), bf16(2 * depth, width),
                bf16(2 * depth, cells * tall),
            ]
            + [bf16(tiles, block, depth)] * 4
            + [
                f32(tiles, 8, span), f32(9, tiles, 8, span), f32(tiles, 8, wide),
                bf16(w_count, t_count, share_rows, width),
                bf16(w_count - 1, t_count, share_rows, width),
                bf16(t_count - 1, share_rows, width),
                f32(t_count, share_rows, width), bf16(t_count, share_rows, width),
                dma(5, 13), dma(5, 9), dma(4), dma(2), dma(2), dma(2),
                dma(w_count - 1), dma(w_count - 1), dma(t_count - 1), dma(t_count - 1),
            ]
        ),
        compiler_params=pltpu.CompilerParams(
            vmem_limit_bytes=60 << 20, collective_id=0, has_side_effects=True
        ),
        cost_estimate=pl.CostEstimate(
            flops=16 * work * depth, transcendentals=2 * work,
            bytes_accessed=4 * tiles * wide * depth,
        ),
        name="attention",
    )(
        row_valid, native(query_heads), native(key_heads), native(value_heads),
        native(grad_mixed), out_weight,
    )

    whole = lambda *shape: pl.BlockSpec(shape, lambda piece: (0,) * len(shape))
    part = lambda size: pl.BlockSpec((group, rows, size), lambda piece: (piece, 0, 0))
    cell_shape = lambda size: jax.ShapeDtypeStruct((cells, rows, size), jnp.bfloat16)
    mixed, *grads, grad_weight = pl.pallas_call(
        functools.partial(project_kernel, block=block, count=count, tall=tall, depth=depth),
        grid=(cells // group,),
        out_shape=(
            cell_shape(width), cell_shape(depth), cell_shape(depth), cell_shape(depth),
            jax.ShapeDtypeStruct((share_rows, width), jnp.float32),
        ),
        in_specs=[
            whole(tiles * block, 5 * depth), whole(2 * depth, width), whole(share_rows, width),
        ],
        out_specs=(part(width), part(depth), part(depth), part(depth), whole(share_rows, width)),
        compiler_params=pltpu.CompilerParams(vmem_limit_bytes=32 << 20),
        cost_estimate=pl.CostEstimate(
            flops=4 * cells * tall * depth * width, transcendentals=0,
            bytes_accessed=2 * cells * rows * width,
        ),
        name="project",
    )(results.reshape(tiles * block, 5 * depth), out_weight, share)

    back = lambda x: x.reshape(frames, columns, rows, x.shape[-1]).transpose(swap)
    return (back(mixed), *(back(x) for x in grads), grad_weight)


def solution(mesh):
    split = P("tm", None, "width", "head")
    return jax.shard_map(
        shards,
        mesh=mesh,
        in_specs=(split, split, split, P(), P(None, "head"), split),
        out_specs=(split, split, split, split, P(("tm", "width"), "head")),
        check_vma=False,
    )
```

```python
import functools
import math

import jax
import jax.numpy as jnp
from jax import lax
from jax.experimental import pallas as pl
from jax.experimental.pallas import tpu as pltpu
from jax.sharding import PartitionSpec as P

TH = 9
FAR = 1e30
LOG2E = 1.4426950408889634


def round_up(value, step):
    return -(-value // step) * step


def dot_nt(left, right):
    return lax.dot_general(
        left, right, (((1,), (1,)), ((), ())), preferred_element_type=jnp.float32
    )


MESH = pl.DeviceIdType.MESH


def row_within(places):
    return places - TH * jnp.floor((places + 0.5) * (1.0 / TH))


def goal_spots(tiles, span, low, count, tall, none):
    columns = lax.broadcasted_iota(jnp.int32, (8, tiles * span), 1)
    goal = jnp.full((8, tiles * span), none, jnp.int32)
    for tile in range(tiles):
        place = columns - tile * span + low
        groups = jnp.floor((place.astype(jnp.float32) + 0.5) * (1.0 / TH)).astype(jnp.int32)
        here = (columns >= tile * span) & (columns < (tile + 1) * span) & (place < count)
        goal = jnp.where(here, groups * (tall - TH) + place + tile * TH, goal)
    return goal[0:1]


def window(piece, group, block):
    span = min(round_up(group * TH + 15, 16), block)
    low = jnp.minimum(piece * (group * TH) // 16 * 16, block - span)
    return span, pl.multiple_of(low, 16)


def picked(spots, goal):
    return jnp.where(spots == goal, 1.0, 0.0).astype(jnp.bfloat16)


def attention_kernel(
    valid_ref, q_hbm, k_hbm, v_hbm, gm_hbm, w_hbm,
    all_ref, share_ref,
    k_all, v_all, q_all, g_all, q_own, k_own, v_own, g_own,
    s_buf, bias, top, out, grad_k, grad_v, landed, tall_qkv, gm_land,
    gm, weight, flat_t, att_ref, part_other, part_in, att_in,
    st_own, st_all, stats, terms, in_core, send_w, in_w, in_t, sum_w, send_t,
    send_sem, recv_sem, own_sem, gm_sem, peer_send, peer_recv, w_send, w_recv, t_send, t_recv,
    core_sem,
    *, tiles, block, wide, count, tall, scale,
):
    depth = q_all.shape[-1]
    half = wide // 2
    halves = ((0, half), (half, half))
    t_index, w_index, h_index = (lax.axis_index(name) for name in ("tm", "width", "head"))
    t_count, w_count = lax.axis_size("tm"), lax.axis_size("width")
    t_back, t_ahead = t_index > 0, t_index < t_count - 1
    w_back, w_ahead = w_index > 0, w_index < w_count - 1
    exists = [
        None, t_back, t_ahead, w_back, w_ahead,
        t_back & w_back, t_ahead & w_back, t_back & w_ahead, t_ahead & w_ahead,
    ]
    t_above = (t_index + 1, w_index, h_index)
    t_below = (t_index - 1, w_index, h_index)
    w_above = (t_index, w_index + 1, h_index)
    w_below = (t_index, w_index - 1, h_index)
    peer = (t_index, w_index, 1 - h_index)
    direct = [(1, t_ahead, t_above), (2, t_back, t_below), (3, w_ahead, w_above), (4, w_back, w_below)]
    even = lax.rem(w_index, 2) == 0
    odd = jnp.logical_not(even)
    over_w = [
        (5, 1, t_back & w_ahead, even, w_above), (7, 1, t_back & w_back, odd, w_below),
        (6, 2, t_ahead & w_ahead, even, w_above), (8, 2, t_ahead & w_back, odd, w_below),
    ]
    over_t = [
        (5, 3, t_ahead & w_back & even, t_above), (7, 4, t_ahead & w_ahead & odd, t_above),
        (6, 3, t_back & w_back & even, t_below), (8, 4, t_back & w_ahead & odd, t_below),
    ]
    turned = ((), (6, 8), (5, 7), (6, 8), ())

    def routes(which):
        found = []
        for slot, via, there, within_chip, device in over_w:
            there = there & within_chip if slot in turned[which] else there
            found.append((slot, slot, via, there, device))
        for slot, via, there, device in over_t:
            if slot in turned[which]:
                found.append((slot + 4, slot, via, there, device))
        return found

    near, far = (3, 4), (5, 6, 7, 8)
    cells, high = landed.shape[1], landed.shape[2]
    group = gm_land.shape[1]
    pieces, step = cells // group, group * tall

    def slot_of(which, slot):
        if which == 4:
            return st_all.at[slot]
        dest = (k_all, v_all, q_all, g_all)[which]
        return dest.at[:, slot * block : (slot + 1) * block, :]

    def remote(which, source, slot, device, lane=None):
        return pltpu.make_async_remote_copy(
            src_ref=source, dst_ref=slot_of(which, slot),
            send_sem=send_sem.at[which, slot if lane is None else lane],
            recv_sem=recv_sem.at[which, slot],
            device_id=device, device_id_type=MESH,
        )

    def send_direct(which, source):
        for slot, there, device in direct:
            @pl.when(there)
            def _():
                remote(which, source, slot, device).start()

    def send_onward(which, vias):
        receive(which, vias)
        for lane, slot, via, there, device in routes(which):
            if via in vias:
                @pl.when(there)
                def _():
                    remote(which, slot_of(which, via), slot, device, lane).start()

    def receive(which, slots):
        for slot in slots:
            @pl.when(exists[slot])
            def _():
                remote(which, slot_of(which, slot), slot, peer).wait_recv()

    def sent(which, source):
        for slot, there, device in direct:
            @pl.when(there)
            def _():
                remote(which, source, slot, device).wait_send()
        for lane, slot, via, there, device in routes(which):
            @pl.when(there)
            def _():
                remote(which, slot_of(which, via), slot, device, lane).wait_send()

    def swap(index, source, dest):
        return pltpu.make_async_remote_copy(
            src_ref=source, dst_ref=dest, send_sem=peer_send.at[index],
            recv_sem=peer_recv.at[index], device_id=peer, device_id_type=MESH,
        )

    chips, core = w_count // 2, lax.rem(w_index, 2)
    chip = w_index // 2
    mate = (t_index, chip * 2 + 1 - core, h_index)

    def core_copy():
        return pltpu.make_async_remote_copy(
            src_ref=terms.at[1 - core], dst_ref=in_core, send_sem=core_sem.at[0],
            recv_sem=core_sem.at[1], device_id=mate, device_id_type=MESH,
        )

    def w_copy(hop):
        dest = lax.rem(chip + hop, chips)
        return pltpu.make_async_remote_copy(
            src_ref=send_w.at[dest], dst_ref=in_w.at[hop - 1],
            send_sem=w_send.at[hop - 1], recv_sem=w_recv.at[hop - 1],
            device_id=(t_index, dest * 2 + core, h_index), device_id_type=MESH,
        )

    def t_copy(hop):
        dest = lax.rem(t_index + hop, t_count)
        return pltpu.make_async_remote_copy(
            src_ref=send_t.at[dest], dst_ref=in_t.at[hop - 1],
            send_sem=t_send.at[hop - 1], recv_sem=t_recv.at[hop - 1],
            device_id=(dest, w_index, h_index), device_id_type=MESH,
        )

    own = [
        pltpu.make_async_copy(source, dest, own_sem.at[index])
        for index, (source, dest) in enumerate((
            (q_hbm, landed.at[0]), (k_hbm, landed.at[1]), (v_hbm, landed.at[2]), (w_hbm, weight),
        ))
    ]
    for copy in own:
        copy.start()

    def gm_copy(piece):
        return pltpu.make_async_copy(
            gm_hbm.at[pl.ds(piece * group, group)], gm_land.at[piece % 2], gm_sem.at[piece % 2]
        )

    for piece in range(2):
        gm_copy(piece).start()

    barrier = pltpu.get_barrier_semaphore()
    partners = [(there, device) for _, there, device in direct]
    for there, device in partners:
        @pl.when(there)
        def _():
            pl.semaphore_signal(barrier, inc=1, device_id=device, device_id_type=MESH)
    pl.semaphore_signal(barrier, inc=1, device_id=peer, device_id_type=MESH)
    greeted = 1 + sum(jnp.where(there, 1, 0) for there, _ in partners)
    pl.semaphore_signal(barrier, inc=1, device_id=mate, device_id_type=MESH)
    for hop in range(1, chips):
        dest = lax.rem(chip + hop, chips) * 2 + core
        pl.semaphore_signal(
            barrier, inc=1, device_id=(t_index, dest, h_index), device_id_type=MESH
        )
    for hop in range(1, t_count):
        dest = lax.rem(t_index + hop, t_count)
        pl.semaphore_signal(
            barrier, inc=1, device_id=(dest, w_index, h_index), device_id_type=MESH
        )

    cuts = []
    for start, stop in ((0, 16), (16, cells)):
        some = (block if stop == cells else stop * TH) - start * TH
        order = lax.broadcasted_iota(jnp.int32, (some, 128), 0).astype(jnp.float32)
        groups = jnp.floor((order + 0.5) * (1.0 / TH))
        goal = (groups * (tall - TH) + order).astype(jnp.int32)
        goal = jnp.where(order < count - start * TH, goal, -2 * high)[:, :1]
        spots = lax.broadcasted_iota(jnp.int32, (some, (stop - start) * tall), 1)
        rows = slice(start * TH, start * TH + some)
        cuts.append((rows, slice(start * tall, stop * tall), spots, goal))
    tall_qkv[...] = jnp.zeros(tall_qkv.shape, jnp.bfloat16)
    for copy in own[:3]:
        copy.wait()

    @pl.loop(0, cells)
    def _(cell):
        span = pl.ds(pl.multiple_of(cell * tall, tall), high)
        for index in range(3):
            tall_qkv[span, index * depth : (index + 1) * depth] = landed[index, cell]

    @pl.loop(0, tiles)
    def _(tile):
        for rows, span, spots, goal in cuts:
            moved = jnp.dot(
                picked(spots, goal + tile * TH), tall_qkv[span, :],
                preferred_element_type=jnp.float32,
            ).astype(jnp.bfloat16)
            for index, (mine, dest) in enumerate(
                ((q_own, q_all), (k_own, k_all), (v_own, v_all))
            ):
                part = moved[:, index * depth : (index + 1) * depth]
                mine[tile, rows, :] = part
                dest[tile, rows, :] = part

    pl.semaphore_wait(barrier, greeted + chips + t_count - 1)
    send_direct(0, k_own)
    send_direct(1, v_own)

    fill = jnp.zeros((tiles, wide - 9 * block, depth), jnp.bfloat16)
    hole = jnp.zeros((tiles, block, depth), jnp.bfloat16)
    for dest in (k_all, v_all, q_all, g_all):
        dest[:, 9 * block :, :] = fill
        for slot in range(1, 9):
            @pl.when(jnp.logical_not(exists[slot]))
            def _():
                dest[:, slot * block : (slot + 1) * block, :] = hole

    places = lax.broadcasted_iota(jnp.int32, (8, wide), 1)
    inside = jnp.zeros((8, wide), jnp.float32)
    within = jnp.zeros((8, wide), jnp.int32)
    for slot in range(9):
        here = (places >= slot * block) & (places < slot * block + count)
        there = 1.0 if slot == 0 else jnp.where(exists[slot], 1.0, 0.0)
        inside = jnp.where(here, there, inside)
        within = jnp.where(here, places - slot * block, within)
    rows = row_within(within.astype(jnp.float32))
    for tile in range(tiles):
        allowed = jnp.zeros((8, wide), jnp.float32)
        for row in range(TH):
            valid = jnp.where(valid_ref[tile * TH + row] > 0, 1.0, 0.0)
            allowed = jnp.where(rows == row, valid, allowed)
        bias[tile] = jnp.where(allowed * inside > 0, 0.0, -FAR)

    own[3].wait()
    first = h_index == 0

    for piece in range(pieces):
        gm_copy(piece).wait()

        @pl.loop(0, group)
        def _(cell):
            low = piece * step + cell * tall
            gm[pl.ds(pl.multiple_of(low + tall - 16, 16), 16), :] = jnp.zeros(
                (16, gm.shape[1]), jnp.bfloat16
            )
            gm[pl.ds(pl.multiple_of(low, 16), high), :] = gm_land[piece % 2, cell]

        span = slice(piece * step, (piece + 1) * step)
        tall_qkv[span, : 2 * depth] = dot_nt(gm[span, :], weight[...]).astype(jnp.bfloat16)
        if piece + 2 < pieces:
            gm_copy(piece + 2).start()

    @pl.loop(0, tiles)
    def _(tile):
        for rows, span, spots, goal in cuts:
            parts = jnp.dot(
                picked(spots, goal + tile * TH), tall_qkv[span, : 2 * depth],
                preferred_element_type=jnp.float32,
            ).astype(jnp.bfloat16)
            g_own[tile, rows, :] = jnp.where(first, parts[:, :depth], parts[:, depth:])
            part_other[tile, rows, :] = jnp.where(first, parts[:, depth:], parts[:, :depth])

    swap(0, part_other, part_in).start()

    top[...] = jnp.full(top.shape, -3e38, jnp.float32)
    out[...] = jnp.zeros(out.shape, jnp.float32)
    grad_v[...] = jnp.zeros(grad_v.shape, jnp.float32)
    ones = jnp.ones((wide, depth), jnp.bfloat16)

    def over_rows(body):
        @pl.loop(0, 2)
        def _(end):
            body(end * (tiles - 1), end * (tiles - 2), 2)

        @pl.loop(1, tiles - 1)
        def _(row):
            body(row, row - 1, 2)
            body(row, row + 1, 1)

    def score_part(start, size):
        span = slice(start, start + size)

        def body(row, low, some):
            mine = pl.ds(low, some)
            queries = q_own[mine].reshape(some * block, depth)
            scores = dot_nt(queries, k_all[row, span, :]) * (scale * LOG2E)
            scores = scores + bias[row, 0:1, span]
            s_buf[pl.ds(2 * row + low, some), :, span] = scores.reshape(some, block, size)
            best = top[mine].reshape(some * block, 128)
            for lane in range(0, size, 128):
                best = jnp.maximum(best, scores[:, lane : lane + 128])
            top[mine] = best.reshape(some, block, 128)
        over_rows(body)

    def value_part(start, size):
        span = slice(start, start + size)

        def body(row, low, some):
            mine, slots = pl.ds(low, some), pl.ds(2 * row + low, some)
            peaks = top[mine].reshape(some * block, 128)[:, :1]
            expos = jnp.exp2(s_buf[slots, :, span].reshape(some * block, size) - peaks)
            s_buf[slots, :, span] = expos.reshape(some, block, size)
            values = jnp.concatenate([v_all[row, span, :], ones[:size]], axis=1)
            out[mine] += jnp.dot(
                expos.astype(jnp.bfloat16), values, preferred_element_type=jnp.float32
            ).reshape(some, block, 2 * depth)
        over_rows(body)

    def query_part(start, size):
        span = slice(start, start + size)

        def body(row, low, some):
            mine, slots = pl.ds(low, some), pl.ds(2 * row + low, some)
            deltas = grad_k[mine].reshape(some * block, depth)[:, :1]
            dprob = dot_nt(g_own[mine].reshape(some * block, depth), v_all[row, span, :])
            dscore = s_buf[slots, :, span].reshape(some * block, size) * (dprob - deltas)
            grad_v[mine] += jnp.dot(
                dscore.astype(jnp.bfloat16), k_all[row, span, :],
                preferred_element_type=jnp.float32,
            ).reshape(some, block, depth)
        over_rows(body)

    def key_part(start, size):
        span = slice(start, start + size)

        def body(row, low, some):
            mine = pl.ds(low, some)
            queries, grads = q_all[row, span, :], g_all[row, span, :]
            lse, delta = stats[row, 0:1, span], stats[row, 1:2, span]
            keys = k_own[mine].reshape(some * block, depth)
            values = v_own[mine].reshape(some * block, depth)
            probs = jnp.exp2(dot_nt(keys, queries) * (scale * LOG2E) - lse)
            grad_v[mine] += jnp.dot(
                probs.astype(jnp.bfloat16), grads, preferred_element_type=jnp.float32
            ).reshape(some, block, depth)
            dscore = probs * (dot_nt(values, grads) - delta)
            grad_k[mine] += jnp.dot(
                dscore.astype(jnp.bfloat16), queries, preferred_element_type=jnp.float32
            ).reshape(some, block, depth)
        over_rows(body)

    send_onward(0, (1, 2))
    send_onward(1, near)
    send_direct(2, q_own)
    receive(0, near)
    score_part(*halves[0])
    swap(0, part_other, part_in).wait()
    grads = (
        g_own[...].astype(jnp.float32) + part_in[...].astype(jnp.float32)
    ).astype(jnp.bfloat16)
    g_own[...] = grads
    g_all[:, :block, :] = grads
    send_onward(1, (1, 2))
    send_direct(3, g_own)
    receive(0, far)
    score_part(*halves[1])

    @pl.loop(0, tiles)
    def _(tile):
        peak = jnp.max(top[tile], axis=1, keepdims=True)
        top[tile] = jnp.broadcast_to(peak, top.shape[1:])

    value_part(*halves[0])
    receive(1, far)
    value_part(*halves[1])
    send_onward(2, near)
    send_onward(2, (1, 2))

    @pl.loop(0, tiles)
    def _(tile):
        total = out[tile][:, depth:]
        attended = (out[tile][:, :depth] / total).astype(jnp.bfloat16)
        att_ref[tile] = attended
        grads = g_own[tile]
        delta = jnp.sum(
            grads.astype(jnp.float32) * attended.astype(jnp.float32), axis=1, keepdims=True
        )
        lanes = lax.broadcasted_iota(jnp.int32, (block, 128), 1)
        columns = jnp.where(lanes == 0, top[tile] + jnp.log2(total), delta)
        span = st_own.shape[-1]
        columns = jnp.concatenate([columns, jnp.zeros((span - block, 128), jnp.float32)], axis=0)
        st_own[tile] = columns.T[:8]
        grad_k[tile] = jnp.broadcast_to(delta, grad_k.shape[1:])

    swap(1, att_ref, att_in).start()
    send_direct(4, st_own)
    query_part(*halves[0])
    send_onward(3, near)
    send_onward(3, (1, 2))
    send_onward(4, (1, 2))
    query_part(*halves[1])

    @pl.loop(0, tiles)
    def _(tile):
        all_ref[tile, :, 2 * depth : 3 * depth] = (
            grad_v[tile] * (scale / out[tile][:, depth:])
        ).astype(jnp.bfloat16)

    swap(1, att_ref, att_in).wait()
    own_att, other_att = (
        jnp.where(first, att_ref[...], att_in[...]), jnp.where(first, att_in[...], att_ref[...])
    )
    all_ref[:, :, :depth] = own_att
    all_ref[:, :, depth : 2 * depth] = other_att
    spots = lax.broadcasted_iota(jnp.int32, (step, 128), 0)[:, :1]

    @pl.loop(0, pieces)
    def _(piece):
        some, low = window(piece, group, block)
        goal = goal_spots(tiles, some, low, count, tall, -1) - piece * step
        heads = all_ref[:, pl.ds(low, some), : 2 * depth].reshape(tiles * some, 2 * depth)
        moved = jnp.dot(picked(spots, goal), heads, preferred_element_type=jnp.float32)
        tall_qkv[pl.ds(pl.multiple_of(piece * step, step), step), : 2 * depth] = moved.astype(
            jnp.bfloat16
        )

    flat_t[...] = tall_qkv[:, : 2 * depth].astype(jnp.float32).T.astype(jnp.bfloat16)
    share_rows, width = share_ref.shape
    for start in range(0, width, 512):
        result = jnp.dot(
            flat_t[...], gm[:, start : start + 512], preferred_element_type=jnp.float32
        )
        for part in range(t_count * w_count):
            column, frame = part % w_count, part // w_count
            terms[column % 2, column // 2, frame, :, start : start + 512] = result[
                part * share_rows : (part + 1) * share_rows
            ].astype(jnp.bfloat16)
    core_copy().start()

    first_row = lax.broadcasted_iota(jnp.int32, (tiles, 8, wide), 1) == 0
    stats[...] = jnp.where(first_row, FAR, 0.0)
    stats[:, :, :block] = st_own[:, :, :block]

    def note(slots):
        for slot in slots:
            @pl.when(exists[slot])
            def _():
                stats[:, :, slot * block : (slot + 1) * block] = st_all[slot, :, :, :block]

    grad_k[...] = jnp.zeros(grad_k.shape, jnp.float32)
    grad_v[...] = jnp.zeros(grad_v.shape, jnp.float32)
    receive(4, near)
    note((1, 2, 3, 4))
    core_copy().wait()
    send_w[...] = (
        terms[core].astype(jnp.float32) + in_core[...].astype(jnp.float32)
    ).astype(jnp.bfloat16)
    for hop in range(1, chips):
        w_copy(hop).start()
    key_part(*halves[0])

    whole = send_w[chip].astype(jnp.float32)
    for hop in range(1, chips):
        w_copy(hop).wait()
        whole = whole + in_w[hop - 1].astype(jnp.float32)
    sum_w[...] = whole
    send_t[...] = whole.astype(jnp.bfloat16)
    for hop in range(1, t_count):
        t_copy(hop).start()

    for which in (2, 3, 4):
        receive(which, far)
    note(far)
    key_part(*halves[1])

    places = lax.broadcasted_iota(jnp.int32, (block, 128), 0)
    rows = row_within(places.astype(jnp.float32))
    for tile in range(tiles):
        live = jnp.zeros((block, 128), jnp.float32)
        for row in range(TH):
            valid = jnp.where(valid_ref[tile * TH + row] > 0, 1.0, 0.0)
            live = jnp.where(rows == row, valid, live)
        all_ref[tile, :, 3 * depth : 4 * depth] = jnp.where(
            live > 0, grad_k[tile] * scale, 0.0
        ).astype(jnp.bfloat16)
        all_ref[tile, :, 4 * depth :] = jnp.where(
            live > 0, grad_v[tile], 0.0
        ).astype(jnp.bfloat16)

    share = sum_w[t_index]
    for hop in range(1, t_count):
        t_copy(hop).wait()
        share = share + in_t[hop - 1].astype(jnp.float32)
    share_ref[...] = share
    for which, source in enumerate((k_own, v_own, q_own, g_own, st_own)):
        sent(which, source)


def project_kernel(
    all_ref, w_ref, share_in, mixed_ref, gq_ref, gk_ref, gv_ref, share_ref,
    *, block, count, tall, depth,
):
    group, high = mixed_ref.shape[:2]
    tiles, width = all_ref.shape[0], all_ref.shape[2]
    step, piece = group * tall, pl.program_id(0)
    some, low = window(piece, group, block)
    goal = goal_spots(tiles, some, low, count, tall, -1) - piece * step
    spots = lax.broadcasted_iota(jnp.int32, (step, 128), 0)[:, :1]
    cells = all_ref[:, pl.ds(low, some), :].reshape(tiles * some, width)
    moved = jnp.dot(
        picked(spots, goal), cells, preferred_element_type=jnp.float32
    ).astype(jnp.bfloat16)
    mixed = jnp.dot(
        moved[:, : 2 * depth], w_ref[...], preferred_element_type=jnp.float32
    ).astype(jnp.bfloat16)
    for cell in range(group):
        span = slice(cell * tall, cell * tall + high)
        mixed_ref[cell] = mixed[span]
        for index, dest in enumerate((gq_ref, gk_ref, gv_ref)):
            dest[cell] = moved[span, (2 + index) * depth : (3 + index) * depth]
    share_ref[...] = share_in[...]


def shards(query_heads, key_heads, value_heads, row_valid, out_weight, grad_mixed):
    frames, rows, columns, depth = query_heads.shape
    scale = 1.0 / math.sqrt(depth)
    tiles = rows // TH
    count = frames * columns * TH
    block = round_up(count, 16)
    wide = round_up(9 * block, 256)
    cells, tall = frames * columns, round_up(rows, 16)
    group = 6
    swap = (0, 2, 1, 3)
    native = lambda x: x.transpose(swap).reshape(cells, rows, x.shape[-1])
    t_count, w_count = lax.axis_size("tm"), lax.axis_size("width")
    share_rows, width = out_weight.shape[0] // (t_count * w_count), out_weight.shape[1]

    pairs = tiles * 3 - 2
    work = pairs * block * wide
    in_vmem = pl.BlockSpec(memory_space=pltpu.VMEM)
    anywhere = pl.BlockSpec(memory_space=pl.ANY)
    bf16 = lambda *shape: pltpu.VMEM(shape, jnp.bfloat16)
    f32 = lambda *shape: pltpu.VMEM(shape, jnp.float32)
    dma = lambda *shape: pltpu.SemaphoreType.DMA(shape)
    span = round_up(block, 128)
    results, share = pl.pallas_call(
        functools.partial(
            attention_kernel, tiles=tiles, block=block, wide=wide, count=count, tall=tall,
            scale=scale,
        ),
        out_shape=(
            jax.ShapeDtypeStruct((tiles, block, 5 * depth), jnp.bfloat16),
            jax.ShapeDtypeStruct((share_rows, width), jnp.float32),
        ),
        in_specs=[pl.BlockSpec(memory_space=pltpu.SMEM)] + [anywhere] * 5,
        out_specs=(in_vmem,) * 2,
        scratch_shapes=(
            [bf16(tiles, wide, depth)] * 4 + [bf16(tiles, block, depth)] * 4
            + [
                f32(pairs, block, wide), f32(tiles, 8, wide), f32(tiles, block, 128),
                f32(tiles, block, 2 * depth), f32(tiles, block, depth), f32(tiles, block, depth),
                bf16(3, cells, rows, depth), bf16(cells * tall, 3 * depth),
                bf16(2, group, rows, width),
                bf16(cells * tall, width), bf16(2 * depth, width),
                bf16(2 * depth, cells * tall),
            ]
            + [bf16(tiles, block, depth)] * 4
            + [
                f32(tiles, 8, span), f32(9, tiles, 8, span), f32(tiles, 8, wide),
                bf16(2, w_count // 2, t_count, share_rows, width),
                bf16(w_count // 2, t_count, share_rows, width),
                bf16(w_count // 2, t_count, share_rows, width),
                bf16(w_count // 2 - 1, t_count, share_rows, width),
                bf16(t_count - 1, share_rows, width),
                f32(t_count, share_rows, width), bf16(t_count, share_rows, width),
                dma(5, 13), dma(5, 9), dma(4), dma(2), dma(2), dma(2),
                dma(w_count // 2 - 1), dma(w_count // 2 - 1), dma(t_count - 1), dma(t_count - 1),
                dma(2),
            ]
        ),
        compiler_params=pltpu.CompilerParams(
            vmem_limit_bytes=60 << 20, collective_id=0, has_side_effects=True
        ),
        cost_estimate=pl.CostEstimate(
            flops=16 * work * depth, transcendentals=2 * work,
            bytes_accessed=4 * tiles * wide * depth,
        ),
        name="attention",
    )(
        row_valid, native(query_heads), native(key_heads), native(value_heads),
        native(grad_mixed), out_weight,
    )

    whole = lambda *shape: pl.BlockSpec(shape, lambda piece: (0,) * len(shape))
    part = lambda size: pl.BlockSpec((group, rows, size), lambda piece: (piece, 0, 0))
    cell_shape = lambda size: jax.ShapeDtypeStruct((cells, rows, size), jnp.bfloat16)
    mixed, *grads, grad_weight = pl.pallas_call(
        functools.partial(project_kernel, block=block, count=count, tall=tall, depth=depth),
        grid=(cells // group,),
        out_shape=(
            cell_shape(width), cell_shape(depth), cell_shape(depth), cell_shape(depth),
            jax.ShapeDtypeStruct((share_rows, width), jnp.float32),
        ),
        in_specs=[
            whole(tiles, block, 5 * depth), whole(2 * depth, width), whole(share_rows, width),
        ],
        out_specs=(part(width), part(depth), part(depth), part(depth), whole(share_rows, width)),
        compiler_params=pltpu.CompilerParams(vmem_limit_bytes=32 << 20),
        cost_estimate=pl.CostEstimate(
            flops=4 * cells * tall * depth * width, transcendentals=0,
            bytes_accessed=2 * cells * rows * width,
        ),
        name="project",
    )(results, out_weight, share)

    back = lambda x: x.reshape(frames, columns, rows, x.shape[-1]).transpose(swap)
    return (back(mixed), *(back(x) for x in grads), grad_weight)


def solution(mesh):
    split = P("tm", None, "width", "head")
    return jax.shard_map(
        shards,
        mesh=mesh,
        in_specs=(split, split, split, P(), P(None, "head"), split),
        out_specs=(split, split, split, split, P(("tm", "width"), "head")),
        check_vma=False,
    )
```

```python
import functools
import math

import jax
import jax.numpy as jnp
from jax import lax
from jax.experimental import pallas as pl
from jax.experimental.pallas import tpu as pltpu
from jax.sharding import PartitionSpec as P

TH = 9
FAR = 1e30
LOG2E = 1.4426950408889634


def round_up(value, step):
    return -(-value // step) * step


def dot_nt(left, right):
    return lax.dot_general(
        left, right, (((1,), (1,)), ((), ())), preferred_element_type=jnp.float32
    )


MESH = pl.DeviceIdType.MESH


def row_within(places):
    return places - TH * jnp.floor((places + 0.5) * (1.0 / TH))


def goal_spots(tiles, span, low, count, tall, none):
    columns = lax.broadcasted_iota(jnp.int32, (8, tiles * span), 1)
    goal = jnp.full((8, tiles * span), none, jnp.int32)
    for tile in range(tiles):
        place = columns - tile * span + low
        groups = jnp.floor((place.astype(jnp.float32) + 0.5) * (1.0 / TH)).astype(jnp.int32)
        here = (columns >= tile * span) & (columns < (tile + 1) * span) & (place < count)
        goal = jnp.where(here, groups * (tall - TH) + place + tile * TH, goal)
    return goal[0:1]


def window(piece, group, block):
    span = min(round_up(group * TH + 15, 16), block)
    low = jnp.minimum(piece * (group * TH) // 16 * 16, block - span)
    return span, pl.multiple_of(low, 16)


def picked(spots, goal):
    return jnp.where(spots == goal, 1.0, 0.0).astype(jnp.bfloat16)


def attention_kernel(
    valid_ref, q_hbm, k_hbm, v_hbm, gm_hbm, w_hbm,
    early_ref, all_ref, share_ref,
    k_all, v_all, q_all, g_all, q_own, k_own, v_own, g_own,
    s_buf, bias, top, out, grad_k, grad_v, landed, tall_qkv, gm_land,
    gm, weight, flat_t, att_ref, part_other, part_in, att_in,
    st_own, st_all, stats, terms, in_core, send_w, in_w, in_t, sum_w, send_t,
    send_sem, recv_sem, own_sem, gm_sem, peer_send, peer_recv, w_send, w_recv, t_send, t_recv,
    core_sem, early, early_sem,
    *, tiles, block, wide, count, tall, scale,
):
    depth = q_all.shape[-1]
    half = wide // 2
    halves = ((0, half), (half, half))
    t_index, w_index, h_index = (lax.axis_index(name) for name in ("tm", "width", "head"))
    t_count, w_count = lax.axis_size("tm"), lax.axis_size("width")
    t_back, t_ahead = t_index > 0, t_index < t_count - 1
    w_back, w_ahead = w_index > 0, w_index < w_count - 1
    exists = [
        None, t_back, t_ahead, w_back, w_ahead,
        t_back & w_back, t_ahead & w_back, t_back & w_ahead, t_ahead & w_ahead,
    ]
    t_above = (t_index + 1, w_index, h_index)
    t_below = (t_index - 1, w_index, h_index)
    w_above = (t_index, w_index + 1, h_index)
    w_below = (t_index, w_index - 1, h_index)
    peer = (t_index, w_index, 1 - h_index)
    direct = [(1, t_ahead, t_above), (2, t_back, t_below), (3, w_ahead, w_above), (4, w_back, w_below)]
    even = lax.rem(w_index, 2) == 0
    odd = jnp.logical_not(even)
    over_w = [
        (5, 1, t_back & w_ahead, even, w_above), (7, 1, t_back & w_back, odd, w_below),
        (6, 2, t_ahead & w_ahead, even, w_above), (8, 2, t_ahead & w_back, odd, w_below),
    ]
    over_t = [
        (5, 3, t_ahead & w_back & even, t_above), (7, 4, t_ahead & w_ahead & odd, t_above),
        (6, 3, t_back & w_back & even, t_below), (8, 4, t_back & w_ahead & odd, t_below),
    ]
    turned = ((), (6, 8), (5, 7), (6, 8), ())

    def routes(which):
        found = []
        for slot, via, there, within_chip, device in over_w:
            there = there & within_chip if slot in turned[which] else there
            found.append((slot, slot, via, there, device))
        for slot, via, there, device in over_t:
            if slot in turned[which]:
                found.append((slot + 4, slot, via, there, device))
        return found

    near, far = (3, 4), (5, 6, 7, 8)
    cells, high = landed.shape[1], landed.shape[2]
    group = gm_land.shape[1]
    pieces, step = cells // group, group * tall

    def slot_of(which, slot):
        if which == 4:
            return st_all.at[slot]
        dest = (k_all, v_all, q_all, g_all)[which]
        return dest.at[:, slot * block : (slot + 1) * block, :]

    def remote(which, source, slot, device, lane=None):
        return pltpu.make_async_remote_copy(
            src_ref=source, dst_ref=slot_of(which, slot),
            send_sem=send_sem.at[which, slot if lane is None else lane],
            recv_sem=recv_sem.at[which, slot],
            device_id=device, device_id_type=MESH,
        )

    def send_direct(which, source, slots=(1, 2, 3, 4)):
        for slot, there, device in direct:
            if slot in slots:
                @pl.when(there)
                def _():
                    remote(which, source, slot, device).start()

    def send_onward(which, vias):
        receive(which, vias)
        for lane, slot, via, there, device in routes(which):
            if via in vias:
                @pl.when(there)
                def _():
                    remote(which, slot_of(which, via), slot, device, lane).start()

    def receive(which, slots):
        for slot in slots:
            @pl.when(exists[slot])
            def _():
                remote(which, slot_of(which, slot), slot, peer).wait_recv()

    def sent(which, source):
        for slot, there, device in direct:
            @pl.when(there)
            def _():
                remote(which, source, slot, device).wait_send()
        for lane, slot, via, there, device in routes(which):
            @pl.when(there)
            def _():
                remote(which, slot_of(which, via), slot, device, lane).wait_send()

    def swap(index, source, dest):
        return pltpu.make_async_remote_copy(
            src_ref=source, dst_ref=dest, send_sem=peer_send.at[index],
            recv_sem=peer_recv.at[index], device_id=peer, device_id_type=MESH,
        )

    chips, core = w_count // 2, lax.rem(w_index, 2)
    chip = w_index // 2
    mate = (t_index, chip * 2 + 1 - core, h_index)

    def core_copy():
        return pltpu.make_async_remote_copy(
            src_ref=terms.at[1 - core], dst_ref=in_core, send_sem=core_sem.at[0],
            recv_sem=core_sem.at[1], device_id=mate, device_id_type=MESH,
        )

    def w_copy(hop):
        dest = lax.rem(chip + hop, chips)
        return pltpu.make_async_remote_copy(
            src_ref=send_w.at[dest], dst_ref=in_w.at[hop - 1],
            send_sem=w_send.at[hop - 1], recv_sem=w_recv.at[hop - 1],
            device_id=(t_index, dest * 2 + core, h_index), device_id_type=MESH,
        )

    def t_copy(hop):
        dest = lax.rem(t_index + hop, t_count)
        return pltpu.make_async_remote_copy(
            src_ref=send_t.at[dest], dst_ref=in_t.at[hop - 1],
            send_sem=t_send.at[hop - 1], recv_sem=t_recv.at[hop - 1],
            device_id=(dest, w_index, h_index), device_id_type=MESH,
        )

    own = [
        pltpu.make_async_copy(source, dest, own_sem.at[index])
        for index, (source, dest) in enumerate((
            (k_hbm, landed.at[0]), (v_hbm, landed.at[1]), (q_hbm, landed.at[2]), (w_hbm, weight),
        ))
    ]
    for copy in own:
        copy.start()

    def gm_copy(piece):
        return pltpu.make_async_copy(
            gm_hbm.at[pl.ds(piece * group, group)], gm_land.at[piece % 2], gm_sem.at[piece % 2]
        )

    for piece in range(2):
        gm_copy(piece).start()

    barrier = pltpu.get_barrier_semaphore()
    partners = [(there, device) for _, there, device in direct]
    for there, device in partners:
        @pl.when(there)
        def _():
            pl.semaphore_signal(barrier, inc=1, device_id=device, device_id_type=MESH)
    pl.semaphore_signal(barrier, inc=1, device_id=peer, device_id_type=MESH)
    greeted = 1 + sum(jnp.where(there, 1, 0) for there, _ in partners)
    pl.semaphore_signal(barrier, inc=1, device_id=mate, device_id_type=MESH)
    for hop in range(1, chips):
        dest = lax.rem(chip + hop, chips) * 2 + core
        pl.semaphore_signal(
            barrier, inc=1, device_id=(t_index, dest, h_index), device_id_type=MESH
        )
    for hop in range(1, t_count):
        dest = lax.rem(t_index + hop, t_count)
        pl.semaphore_signal(
            barrier, inc=1, device_id=(dest, w_index, h_index), device_id_type=MESH
        )

    cuts = []
    for start, stop in ((0, 16), (16, cells)):
        some = (block if stop == cells else stop * TH) - start * TH
        order = lax.broadcasted_iota(jnp.int32, (some, 128), 0).astype(jnp.float32)
        groups = jnp.floor((order + 0.5) * (1.0 / TH))
        goal = (groups * (tall - TH) + order).astype(jnp.int32)
        goal = jnp.where(order < count - start * TH, goal, -2 * high)[:, :1]
        spots = lax.broadcasted_iota(jnp.int32, (some, (stop - start) * tall), 1)
        rows = slice(start * TH, start * TH + some)
        cuts.append((rows, slice(start * tall, stop * tall), spots, goal))
    tall_qkv[...] = jnp.zeros(tall_qkv.shape, jnp.bfloat16)
    for copy in own[:3]:
        copy.wait()

    @pl.loop(0, cells)
    def _(cell):
        span = pl.ds(pl.multiple_of(cell * tall, tall), high)
        for index in range(3):
            tall_qkv[span, index * depth : (index + 1) * depth] = landed[index, cell]

    def place(first_column, pairs):
        columns = slice(first_column * depth, (first_column + len(pairs)) * depth)

        @pl.loop(0, tiles)
        def _(tile):
            for rows, span, spots, goal in cuts:
                moved = jnp.dot(
                    picked(spots, goal + tile * TH), tall_qkv[span, columns],
                    preferred_element_type=jnp.float32,
                ).astype(jnp.bfloat16)
                for index, (mine, dest) in enumerate(pairs):
                    part = moved[:, index * depth : (index + 1) * depth]
                    mine[tile, rows, :] = part
                    dest[tile, rows, :] = part

    place(0, ((k_own, k_all),))
    pl.semaphore_wait(barrier, greeted + chips + t_count - 1)
    send_direct(0, k_own)
    place(1, ((v_own, v_all), (q_own, q_all)))
    send_direct(1, v_own)

    fill = jnp.zeros((tiles, wide - 9 * block, depth), jnp.bfloat16)
    hole = jnp.zeros((tiles, block, depth), jnp.bfloat16)
    for dest in (k_all, v_all, q_all, g_all):
        dest[:, 9 * block :, :] = fill
        for slot in range(1, 9):
            @pl.when(jnp.logical_not(exists[slot]))
            def _():
                dest[:, slot * block : (slot + 1) * block, :] = hole

    places = lax.broadcasted_iota(jnp.int32, (8, wide), 1)
    inside = jnp.zeros((8, wide), jnp.float32)
    within = jnp.zeros((8, wide), jnp.int32)
    for slot in range(9):
        here = (places >= slot * block) & (places < slot * block + count)
        there = 1.0 if slot == 0 else jnp.where(exists[slot], 1.0, 0.0)
        inside = jnp.where(here, there, inside)
        within = jnp.where(here, places - slot * block, within)
    rows = row_within(within.astype(jnp.float32))
    for tile in range(tiles):
        allowed = jnp.zeros((8, wide), jnp.float32)
        for row in range(TH):
            valid = jnp.where(valid_ref[tile * TH + row] > 0, 1.0, 0.0)
            allowed = jnp.where(rows == row, valid, allowed)
        bias[tile] = jnp.where(allowed * inside > 0, 0.0, -FAR)

    own[3].wait()
    first = h_index == 0

    for piece in range(pieces):
        gm_copy(piece).wait()

        @pl.loop(0, group)
        def _(cell):
            low = piece * step + cell * tall
            gm[pl.ds(pl.multiple_of(low + tall - 16, 16), 16), :] = jnp.zeros(
                (16, gm.shape[1]), jnp.bfloat16
            )
            gm[pl.ds(pl.multiple_of(low, 16), high), :] = gm_land[piece % 2, cell]

        span = slice(piece * step, (piece + 1) * step)
        tall_qkv[span, : 2 * depth] = dot_nt(gm[span, :], weight[...]).astype(jnp.bfloat16)
        if piece + 2 < pieces:
            gm_copy(piece + 2).start()

    @pl.loop(0, tiles)
    def _(tile):
        for rows, span, spots, goal in cuts:
            parts = jnp.dot(
                picked(spots, goal + tile * TH), tall_qkv[span, : 2 * depth],
                preferred_element_type=jnp.float32,
            ).astype(jnp.bfloat16)
            g_own[tile, rows, :] = jnp.where(first, parts[:, :depth], parts[:, depth:])
            part_other[tile, rows, :] = jnp.where(first, parts[:, depth:], parts[:, :depth])

    swap(0, part_other, part_in).start()

    top[...] = jnp.full(top.shape, -3e38, jnp.float32)
    out[...] = jnp.zeros(out.shape, jnp.float32)
    grad_v[...] = jnp.zeros(grad_v.shape, jnp.float32)
    ones = jnp.ones((wide, depth), jnp.bfloat16)

    def over_rows(body):
        @pl.loop(0, 2)
        def _(end):
            body(end * (tiles - 1), end * (tiles - 2), 2)

        @pl.loop(1, tiles - 1)
        def _(row):
            body(row, row - 1, 2)
            body(row, row + 1, 1)

    def score_part(start, size):
        span = slice(start, start + size)

        def body(row, low, some):
            mine = pl.ds(low, some)
            queries = q_own[mine].reshape(some * block, depth)
            scores = dot_nt(queries, k_all[row, span, :]) * (scale * LOG2E)
            scores = scores + bias[row, 0:1, span]
            s_buf[pl.ds(2 * row + low, some), :, span] = scores.reshape(some, block, size)
            best = top[mine].reshape(some * block, 128)
            for lane in range(0, size, 128):
                best = jnp.maximum(best, scores[:, lane : lane + 128])
            top[mine] = best.reshape(some, block, 128)
        over_rows(body)

    def value_part(start, size):
        span = slice(start, start + size)

        def body(row, low, some):
            mine, slots = pl.ds(low, some), pl.ds(2 * row + low, some)
            peaks = top[mine].reshape(some * block, 128)[:, :1]
            expos = jnp.exp2(s_buf[slots, :, span].reshape(some * block, size) - peaks)
            s_buf[slots, :, span] = expos.reshape(some, block, size)
            values = jnp.concatenate([v_all[row, span, :], ones[:size]], axis=1)
            out[mine] += jnp.dot(
                expos.astype(jnp.bfloat16), values, preferred_element_type=jnp.float32
            ).reshape(some, block, 2 * depth)
        over_rows(body)

    def query_part(start, size):
        span = slice(start, start + size)

        def body(row, low, some):
            mine, slots = pl.ds(low, some), pl.ds(2 * row + low, some)
            deltas = grad_k[mine].reshape(some * block, depth)[:, :1]
            dprob = dot_nt(g_own[mine].reshape(some * block, depth), v_all[row, span, :])
            dscore = s_buf[slots, :, span].reshape(some * block, size) * (dprob - deltas)
            grad_v[mine] += jnp.dot(
                dscore.astype(jnp.bfloat16), k_all[row, span, :],
                preferred_element_type=jnp.float32,
            ).reshape(some, block, depth)
        over_rows(body)

    def key_part(start, size):
        span = slice(start, start + size)

        def body(row, low, some):
            mine = pl.ds(low, some)
            queries, grads = q_all[row, span, :], g_all[row, span, :]
            lse, delta = stats[row, 0:1, span], stats[row, 1:2, span]
            keys = k_own[mine].reshape(some * block, depth)
            values = v_own[mine].reshape(some * block, depth)
            probs = jnp.exp2(dot_nt(keys, queries) * (scale * LOG2E) - lse)
            grad_v[mine] += jnp.dot(
                probs.astype(jnp.bfloat16), grads, preferred_element_type=jnp.float32
            ).reshape(some, block, depth)
            dscore = probs * (dot_nt(values, grads) - delta)
            grad_k[mine] += jnp.dot(
                dscore.astype(jnp.bfloat16), queries, preferred_element_type=jnp.float32
            ).reshape(some, block, depth)
        over_rows(body)

    send_onward(0, (1, 2))
    send_onward(1, near)
    send_direct(2, q_own, (1, 2))
    receive(0, near)
    score_part(*halves[0])
    swap(0, part_other, part_in).wait()
    grads = (
        g_own[...].astype(jnp.float32) + part_in[...].astype(jnp.float32)
    ).astype(jnp.bfloat16)
    g_own[...] = grads
    g_all[:, :block, :] = grads
    send_onward(1, (1, 2))
    send_direct(2, q_own, near)
    send_direct(3, g_own)
    receive(0, far)
    score_part(*halves[1])

    @pl.loop(0, tiles)
    def _(tile):
        peak = jnp.max(top[tile], axis=1, keepdims=True)
        top[tile] = jnp.broadcast_to(peak, top.shape[1:])

    value_part(*halves[0])
    receive(1, far)
    value_part(*halves[1])
    send_onward(2, near)
    send_onward(2, (1, 2))

    @pl.loop(0, tiles)
    def _(tile):
        total = out[tile][:, depth:]
        attended = (out[tile][:, :depth] / total).astype(jnp.bfloat16)
        att_ref[tile] = attended
        grads = g_own[tile]
        delta = jnp.sum(
            grads.astype(jnp.float32) * attended.astype(jnp.float32), axis=1, keepdims=True
        )
        lanes = lax.broadcasted_iota(jnp.int32, (block, 128), 1)
        columns = jnp.where(lanes == 0, top[tile] + jnp.log2(total), delta)
        span = st_own.shape[-1]
        columns = jnp.concatenate([columns, jnp.zeros((span - block, 128), jnp.float32)], axis=0)
        st_own[tile] = columns.T[:8]
        grad_k[tile] = jnp.broadcast_to(delta, grad_k.shape[1:])

    swap(1, att_ref, att_in).start()
    send_direct(4, st_own)
    query_part(*halves[0])
    send_onward(3, near)
    send_onward(3, (1, 2))
    query_part(*halves[1])
    send_onward(4, (1, 2))

    @pl.loop(0, tiles)
    def _(tile):
        early[tile, :, 2 * depth :] = (
            grad_v[tile] * (scale / out[tile][:, depth:])
        ).astype(jnp.bfloat16)

    swap(1, att_ref, att_in).wait()
    own_att, other_att = (
        jnp.where(first, att_ref[...], att_in[...]), jnp.where(first, att_in[...], att_ref[...])
    )
    early[:, :, :depth] = own_att
    early[:, :, depth : 2 * depth] = other_att
    early_copy = pltpu.make_async_copy(early, early_ref, early_sem.at[0])
    early_copy.start()
    spots = lax.broadcasted_iota(jnp.int32, (step, 128), 0)[:, :1]

    @pl.loop(0, pieces)
    def _(piece):
        some, low = window(piece, group, block)
        goal = goal_spots(tiles, some, low, count, tall, -1) - piece * step
        heads = early[:, pl.ds(low, some), : 2 * depth].reshape(tiles * some, 2 * depth)
        moved = jnp.dot(picked(spots, goal), heads, preferred_element_type=jnp.float32)
        tall_qkv[pl.ds(pl.multiple_of(piece * step, step), step), : 2 * depth] = moved.astype(
            jnp.bfloat16
        )

    flat_t[...] = tall_qkv[:, : 2 * depth].astype(jnp.float32).T.astype(jnp.bfloat16)
    share_rows, width = share_ref.shape
    for start in range(0, width, 512):
        result = jnp.dot(
            flat_t[...], gm[:, start : start + 512], preferred_element_type=jnp.float32
        )
        for part in range(t_count * w_count):
            column, frame = part % w_count, part // w_count
            terms[column % 2, column // 2, frame, :, start : start + 512] = result[
                part * share_rows : (part + 1) * share_rows
            ].astype(jnp.bfloat16)
    core_copy().start()

    first_row = lax.broadcasted_iota(jnp.int32, (tiles, 8, wide), 1) == 0
    stats[...] = jnp.where(first_row, FAR, 0.0)
    stats[:, :, :block] = st_own[:, :, :block]

    def note(slots):
        for slot in slots:
            @pl.when(exists[slot])
            def _():
                stats[:, :, slot * block : (slot + 1) * block] = st_all[slot, :, :, :block]

    grad_k[...] = jnp.zeros(grad_k.shape, jnp.float32)
    grad_v[...] = jnp.zeros(grad_v.shape, jnp.float32)
    receive(4, near)
    note((1, 2, 3, 4))
    core_copy().wait()
    send_w[...] = (
        terms[core].astype(jnp.float32) + in_core[...].astype(jnp.float32)
    ).astype(jnp.bfloat16)
    for hop in range(1, chips):
        w_copy(hop).start()
    key_part(*halves[0])

    whole = send_w[chip].astype(jnp.float32)
    for hop in range(1, chips):
        w_copy(hop).wait()
        whole = whole + in_w[hop - 1].astype(jnp.float32)
    sum_w[...] = whole
    send_t[...] = whole.astype(jnp.bfloat16)
    for hop in range(1, t_count):
        t_copy(hop).start()

    for which in (2, 3, 4):
        receive(which, far)
    note(far)
    key_part(*halves[1])

    places = lax.broadcasted_iota(jnp.int32, (block, 128), 0)
    rows = row_within(places.astype(jnp.float32))
    for tile in range(tiles):
        live = jnp.zeros((block, 128), jnp.float32)
        for row in range(TH):
            valid = jnp.where(valid_ref[tile * TH + row] > 0, 1.0, 0.0)
            live = jnp.where(rows == row, valid, live)
        all_ref[tile, :, :depth] = jnp.where(
            live > 0, grad_k[tile] * scale, 0.0
        ).astype(jnp.bfloat16)
        all_ref[tile, :, depth:] = jnp.where(
            live > 0, grad_v[tile], 0.0
        ).astype(jnp.bfloat16)

    share = sum_w[t_index]
    for hop in range(1, t_count):
        t_copy(hop).wait()
        share = share + in_t[hop - 1].astype(jnp.float32)
    share_ref[...] = share
    early_copy.wait()
    for which, source in enumerate((k_own, v_own, q_own, g_own, st_own)):
        sent(which, source)


def project_kernel(
    early_ref, late_ref, w_ref, share_in, mixed_ref, gq_ref, gk_ref, gv_ref, share_ref,
    *, block, count, tall, depth,
):
    group, high = mixed_ref.shape[:2]
    tiles = early_ref.shape[0]
    step, piece = group * tall, pl.program_id(0)
    some, low = window(piece, group, block)
    goal = goal_spots(tiles, some, low, count, tall, -1) - piece * step
    spots = lax.broadcasted_iota(jnp.int32, (step, 128), 0)[:, :1]
    pick = picked(spots, goal)
    moved, late = (
        jnp.dot(
            pick, ref[:, pl.ds(low, some), :].reshape(tiles * some, ref.shape[2]),
            preferred_element_type=jnp.float32,
        ).astype(jnp.bfloat16)
        for ref in (early_ref, late_ref)
    )
    mixed = jnp.dot(
        moved[:, : 2 * depth], w_ref[...], preferred_element_type=jnp.float32
    ).astype(jnp.bfloat16)
    for cell in range(group):
        span = slice(cell * tall, cell * tall + high)
        mixed_ref[cell] = mixed[span]
        gq_ref[cell] = moved[span, 2 * depth :]
        gk_ref[cell] = late[span, :depth]
        gv_ref[cell] = late[span, depth:]
    share_ref[...] = share_in[...]


def shards(query_heads, key_heads, value_heads, row_valid, out_weight, grad_mixed):
    frames, rows, columns, depth = query_heads.shape
    scale = 1.0 / math.sqrt(depth)
    tiles = rows // TH
    count = frames * columns * TH
    block = round_up(count, 16)
    wide = round_up(9 * block, 256)
    cells, tall = frames * columns, round_up(rows, 16)
    group = 6
    swap = (0, 2, 1, 3)
    native = lambda x: x.transpose(swap).reshape(cells, rows, x.shape[-1])
    t_count, w_count = lax.axis_size("tm"), lax.axis_size("width")
    share_rows, width = out_weight.shape[0] // (t_count * w_count), out_weight.shape[1]

    pairs = tiles * 3 - 2
    work = pairs * block * wide
    in_vmem = pl.BlockSpec(memory_space=pltpu.VMEM)
    anywhere = pl.BlockSpec(memory_space=pl.ANY)
    bf16 = lambda *shape: pltpu.VMEM(shape, jnp.bfloat16)
    f32 = lambda *shape: pltpu.VMEM(shape, jnp.float32)
    dma = lambda *shape: pltpu.SemaphoreType.DMA(shape)
    span = round_up(block, 128)
    early, late, share = pl.pallas_call(
        functools.partial(
            attention_kernel, tiles=tiles, block=block, wide=wide, count=count, tall=tall,
            scale=scale,
        ),
        out_shape=(
            jax.ShapeDtypeStruct((tiles, block, 3 * depth), jnp.bfloat16),
            jax.ShapeDtypeStruct((tiles, block, 2 * depth), jnp.bfloat16),
            jax.ShapeDtypeStruct((share_rows, width), jnp.float32),
        ),
        in_specs=[pl.BlockSpec(memory_space=pltpu.SMEM)] + [anywhere] * 5,
        out_specs=(anywhere, in_vmem, in_vmem),
        scratch_shapes=(
            [bf16(tiles, wide, depth)] * 4 + [bf16(tiles, block, depth)] * 4
            + [
                f32(pairs, block, wide), f32(tiles, 8, wide), f32(tiles, block, 128),
                f32(tiles, block, 2 * depth), f32(tiles, block, depth), f32(tiles, block, depth),
                bf16(3, cells, rows, depth), bf16(cells * tall, 3 * depth),
                bf16(2, group, rows, width),
                bf16(cells * tall, width), bf16(2 * depth, width),
                bf16(2 * depth, cells * tall),
            ]
            + [bf16(tiles, block, depth)] * 4
            + [
                f32(tiles, 8, span), f32(9, tiles, 8, span), f32(tiles, 8, wide),
                bf16(2, w_count // 2, t_count, share_rows, width),
                bf16(w_count // 2, t_count, share_rows, width),
                bf16(w_count // 2, t_count, share_rows, width),
                bf16(w_count // 2 - 1, t_count, share_rows, width),
                bf16(t_count - 1, share_rows, width),
                f32(t_count, share_rows, width), bf16(t_count, share_rows, width),
                dma(5, 13), dma(5, 9), dma(4), dma(2), dma(2), dma(2),
                dma(w_count // 2 - 1), dma(w_count // 2 - 1), dma(t_count - 1), dma(t_count - 1),
                dma(2), bf16(tiles, block, 3 * depth), dma(1),
            ]
        ),
        compiler_params=pltpu.CompilerParams(
            vmem_limit_bytes=60 << 20, collective_id=0, has_side_effects=True
        ),
        cost_estimate=pl.CostEstimate(
            flops=16 * work * depth, transcendentals=2 * work,
            bytes_accessed=4 * tiles * wide * depth,
        ),
        name="attention",
    )(
        row_valid, native(query_heads), native(key_heads), native(value_heads),
        native(grad_mixed), out_weight,
    )

    whole = lambda *shape: pl.BlockSpec(shape, lambda piece: (0,) * len(shape))
    part = lambda size: pl.BlockSpec((group, rows, size), lambda piece: (piece, 0, 0))
    cell_shape = lambda size: jax.ShapeDtypeStruct((cells, rows, size), jnp.bfloat16)
    mixed, *grads, grad_weight = pl.pallas_call(
        functools.partial(project_kernel, block=block, count=count, tall=tall, depth=depth),
        grid=(cells // group,),
        out_shape=(
            cell_shape(width), cell_shape(depth), cell_shape(depth), cell_shape(depth),
            jax.ShapeDtypeStruct((share_rows, width), jnp.float32),
        ),
        in_specs=[
            whole(tiles, block, 3 * depth), whole(tiles, block, 2 * depth), whole(2 * depth, width), whole(share_rows, width),
        ],
        out_specs=(part(width), part(depth), part(depth), part(depth), whole(share_rows, width)),
        compiler_params=pltpu.CompilerParams(vmem_limit_bytes=60 << 20),
        cost_estimate=pl.CostEstimate(
            flops=4 * cells * tall * depth * width, transcendentals=0,
            bytes_accessed=2 * cells * rows * width,
        ),
        name="project",
    )(early, late, out_weight, share)

    back = lambda x: x.reshape(frames, columns, rows, x.shape[-1]).transpose(swap)
    return (back(mixed), *(back(x) for x in grads), grad_weight)


def solution(mesh):
    split = P("tm", None, "width", "head")
    return jax.shard_map(
        shards,
        mesh=mesh,
        in_specs=(split, split, split, P(), P(None, "head"), split),
        out_specs=(split, split, split, split, P(("tm", "width"), "head")),
        check_vma=False,
    )
```

```python
import functools
import math

import jax
import jax.numpy as jnp
from jax import lax
from jax.experimental import pallas as pl
from jax.experimental.pallas import tpu as pltpu
from jax.sharding import PartitionSpec as P

TH = 9
FAR = 1e30
LOG2E = 1.4426950408889634


def round_up(value, step):
    return -(-value // step) * step


def dot_nt(left, right):
    return lax.dot_general(
        left, right, (((1,), (1,)), ((), ())), preferred_element_type=jnp.float32
    )


MESH = pl.DeviceIdType.MESH


def row_within(places):
    return places - TH * jnp.floor((places + 0.5) * (1.0 / TH))


def goal_spots(tiles, span, low, count, tall, none):
    columns = lax.broadcasted_iota(jnp.int32, (8, tiles * span), 1)
    goal = jnp.full((8, tiles * span), none, jnp.int32)
    for tile in range(tiles):
        place = columns - tile * span + low
        groups = jnp.floor((place.astype(jnp.float32) + 0.5) * (1.0 / TH)).astype(jnp.int32)
        here = (columns >= tile * span) & (columns < (tile + 1) * span) & (place < count)
        goal = jnp.where(here, groups * (tall - TH) + place + tile * TH, goal)
    return goal[0:1]


def window(piece, group, block):
    span = min(round_up(group * TH + 15, 16), block)
    low = jnp.minimum(piece * (group * TH) // 16 * 16, block - span)
    return span, pl.multiple_of(low, 16)


def picked(spots, goal):
    return jnp.where(spots == goal, 1.0, 0.0).astype(jnp.bfloat16)


def attention_kernel(
    valid_ref, q_hbm, k_hbm, v_hbm, gm_hbm, w_hbm,
    early_ref, all_ref, share_ref,
    k_all, v_all, q_all, g_all, q_own, k_own, v_own, g_own,
    s_buf, bias, top, out, grad_k, grad_v, landed, tall_qkv, gm_land,
    gm, weight, flat_t, att_ref, part_other, part_in, att_in,
    st_own, st_all, stats, terms, in_core, send_w, in_w, in_t, sum_w, send_t,
    send_sem, recv_sem, own_sem, gm_sem, peer_send, peer_recv, w_send, w_recv, t_send, t_recv,
    core_sem, early, early_sem,
    *, tiles, block, wide, count, tall, scale,
):
    depth = q_all.shape[-1]
    half = wide // 2
    halves = ((0, half), (half, half))
    t_index, w_index, h_index = (lax.axis_index(name) for name in ("tm", "width", "head"))
    t_count, w_count = lax.axis_size("tm"), lax.axis_size("width")
    t_back, t_ahead = t_index > 0, t_index < t_count - 1
    w_back, w_ahead = w_index > 0, w_index < w_count - 1
    exists = [
        None, t_back, t_ahead, w_back, w_ahead,
        t_back & w_back, t_ahead & w_back, t_back & w_ahead, t_ahead & w_ahead,
    ]
    t_above = (t_index + 1, w_index, h_index)
    t_below = (t_index - 1, w_index, h_index)
    w_above = (t_index, w_index + 1, h_index)
    w_below = (t_index, w_index - 1, h_index)
    peer = (t_index, w_index, 1 - h_index)
    direct = [(1, t_ahead, t_above), (2, t_back, t_below), (3, w_ahead, w_above), (4, w_back, w_below)]
    even = lax.rem(w_index, 2) == 0
    odd = jnp.logical_not(even)
    over_w = [
        (5, 1, t_back & w_ahead, even, w_above), (7, 1, t_back & w_back, odd, w_below),
        (6, 2, t_ahead & w_ahead, even, w_above), (8, 2, t_ahead & w_back, odd, w_below),
    ]
    over_t = [
        (5, 3, t_ahead & w_back & even, t_above), (7, 4, t_ahead & w_ahead & odd, t_above),
        (6, 3, t_back & w_back & even, t_below), (8, 4, t_back & w_ahead & odd, t_below),
    ]
    turned = ((), (6, 8), (5, 7), (6, 8), ())

    def routes(which):
        found = []
        for slot, via, there, within_chip, device in over_w:
            there = there & within_chip if slot in turned[which] else there
            found.append((slot, slot, via, there, device))
        for slot, via, there, device in over_t:
            if slot in turned[which]:
                found.append((slot + 4, slot, via, there, device))
        return found

    near, far = (3, 4), (5, 6, 7, 8)
    cells, high = landed.shape[1], landed.shape[2]
    group = gm_land.shape[1]
    pieces, step = cells // group, group * tall

    def slot_of(which, slot):
        if which == 4:
            return st_all.at[slot]
        dest = (k_all, v_all, q_all, g_all)[which]
        return dest.at[:, slot * block : (slot + 1) * block, :]

    def remote(which, source, slot, device, lane=None):
        return pltpu.make_async_remote_copy(
            src_ref=source, dst_ref=slot_of(which, slot),
            send_sem=send_sem.at[which, slot if lane is None else lane],
            recv_sem=recv_sem.at[which, slot],
            device_id=device, device_id_type=MESH,
        )

    def send_direct(which, source, slots=(1, 2, 3, 4)):
        for slot, there, device in direct:
            if slot in slots:
                @pl.when(there)
                def _():
                    remote(which, source, slot, device).start()

    def send_onward(which, vias):
        receive(which, vias)
        for lane, slot, via, there, device in routes(which):
            if via in vias:
                @pl.when(there)
                def _():
                    remote(which, slot_of(which, via), slot, device, lane).start()

    def receive(which, slots):
        for slot in slots:
            @pl.when(exists[slot])
            def _():
                remote(which, slot_of(which, slot), slot, peer).wait_recv()

    def sent(which, source):
        for slot, there, device in direct:
            @pl.when(there)
            def _():
                remote(which, source, slot, device).wait_send()
        for lane, slot, via, there, device in routes(which):
            @pl.when(there)
            def _():
                remote(which, slot_of(which, via), slot, device, lane).wait_send()

    def swap(index, source, dest):
        return pltpu.make_async_remote_copy(
            src_ref=source, dst_ref=dest, send_sem=peer_send.at[index],
            recv_sem=peer_recv.at[index], device_id=peer, device_id_type=MESH,
        )

    chips, core = w_count // 2, lax.rem(w_index, 2)
    chip = w_index // 2
    mate = (t_index, chip * 2 + 1 - core, h_index)

    def core_copy():
        return pltpu.make_async_remote_copy(
            src_ref=terms.at[1 - core], dst_ref=in_core, send_sem=core_sem.at[0],
            recv_sem=core_sem.at[1], device_id=mate, device_id_type=MESH,
        )

    def w_copy(hop):
        dest = lax.rem(chip + hop, chips)
        return pltpu.make_async_remote_copy(
            src_ref=send_w.at[dest], dst_ref=in_w.at[hop - 1],
            send_sem=w_send.at[hop - 1], recv_sem=w_recv.at[hop - 1],
            device_id=(t_index, dest * 2 + core, h_index), device_id_type=MESH,
        )

    def t_copy(hop):
        dest = lax.rem(t_index + hop, t_count)
        return pltpu.make_async_remote_copy(
            src_ref=send_t.at[dest], dst_ref=in_t.at[hop - 1],
            send_sem=t_send.at[hop - 1], recv_sem=t_recv.at[hop - 1],
            device_id=(dest, w_index, h_index), device_id_type=MESH,
        )

    own = [
        pltpu.make_async_copy(source, dest, own_sem.at[index])
        for index, (source, dest) in enumerate((
            (k_hbm, landed.at[0]), (v_hbm, landed.at[1]), (q_hbm, landed.at[2]), (w_hbm, weight),
        ))
    ]
    for copy in own:
        copy.start()

    def gm_copy(piece):
        return pltpu.make_async_copy(
            gm_hbm.at[pl.ds(piece * group, group)], gm_land.at[piece % 2], gm_sem.at[piece % 2]
        )

    for piece in range(2):
        gm_copy(piece).start()

    barrier = pltpu.get_barrier_semaphore()
    partners = [(there, device) for _, there, device in direct]
    for there, device in partners:
        @pl.when(there)
        def _():
            pl.semaphore_signal(barrier, inc=1, device_id=device, device_id_type=MESH)
    pl.semaphore_signal(barrier, inc=1, device_id=peer, device_id_type=MESH)
    greeted = 1 + sum(jnp.where(there, 1, 0) for there, _ in partners)
    pl.semaphore_signal(barrier, inc=1, device_id=mate, device_id_type=MESH)
    for hop in range(1, chips):
        dest = lax.rem(chip + hop, chips) * 2 + core
        pl.semaphore_signal(
            barrier, inc=1, device_id=(t_index, dest, h_index), device_id_type=MESH
        )
    for hop in range(1, t_count):
        dest = lax.rem(t_index + hop, t_count)
        pl.semaphore_signal(
            barrier, inc=1, device_id=(dest, w_index, h_index), device_id_type=MESH
        )

    cuts = []
    for start, stop in ((0, 16), (16, cells)):
        some = (block if stop == cells else stop * TH) - start * TH
        order = lax.broadcasted_iota(jnp.int32, (some, 128), 0).astype(jnp.float32)
        groups = jnp.floor((order + 0.5) * (1.0 / TH))
        goal = (groups * (tall - TH) + order).astype(jnp.int32)
        goal = jnp.where(order < count - start * TH, goal, -2 * high)[:, :1]
        spots = lax.broadcasted_iota(jnp.int32, (some, (stop - start) * tall), 1)
        rows = slice(start * TH, start * TH + some)
        cuts.append((rows, slice(start * tall, stop * tall), spots, goal))
    tall_qkv[...] = jnp.zeros(tall_qkv.shape, jnp.bfloat16)
    for copy in own[:3]:
        copy.wait()

    @pl.loop(0, cells)
    def _(cell):
        span = pl.ds(pl.multiple_of(cell * tall, tall), high)
        for index in range(3):
            tall_qkv[span, index * depth : (index + 1) * depth] = landed[index, cell]

    def place(first_column, pairs):
        columns = slice(first_column * depth, (first_column + len(pairs)) * depth)

        @pl.loop(0, tiles)
        def _(tile):
            for rows, span, spots, goal in cuts:
                moved = jnp.dot(
                    picked(spots, goal + tile * TH), tall_qkv[span, columns],
                    preferred_element_type=jnp.float32,
                ).astype(jnp.bfloat16)
                for index, (mine, dest) in enumerate(pairs):
                    part = moved[:, index * depth : (index + 1) * depth]
                    mine[tile, rows, :] = part
                    dest[tile, rows, :] = part

    place(0, ((k_own, k_all),))
    pl.semaphore_wait(barrier, greeted + chips + t_count - 1)
    send_direct(0, k_own)
    place(1, ((v_own, v_all), (q_own, q_all)))
    send_direct(1, v_own)

    own[3].wait()
    first = h_index == 0

    for piece in range(pieces):
        gm_copy(piece).wait()

        @pl.loop(0, group)
        def _(cell):
            low = piece * step + cell * tall
            gm[pl.ds(pl.multiple_of(low + tall - 16, 16), 16), :] = jnp.zeros(
                (16, gm.shape[1]), jnp.bfloat16
            )
            gm[pl.ds(pl.multiple_of(low, 16), high), :] = gm_land[piece % 2, cell]

        span = slice(piece * step, (piece + 1) * step)
        tall_qkv[span, : 2 * depth] = dot_nt(gm[span, :], weight[...]).astype(jnp.bfloat16)
        if piece + 2 < pieces:
            gm_copy(piece + 2).start()

    @pl.loop(0, tiles)
    def _(tile):
        for rows, span, spots, goal in cuts:
            parts = jnp.dot(
                picked(spots, goal + tile * TH), tall_qkv[span, : 2 * depth],
                preferred_element_type=jnp.float32,
            ).astype(jnp.bfloat16)
            g_own[tile, rows, :] = jnp.where(first, parts[:, :depth], parts[:, depth:])
            part_other[tile, rows, :] = jnp.where(first, parts[:, depth:], parts[:, :depth])

    swap(0, part_other, part_in).start()

    fill = jnp.zeros((tiles, wide - 9 * block, depth), jnp.bfloat16)
    hole = jnp.zeros((tiles, block, depth), jnp.bfloat16)
    for dest in (k_all, v_all, q_all, g_all):
        dest[:, 9 * block :, :] = fill
        for slot in range(1, 9):
            @pl.when(jnp.logical_not(exists[slot]))
            def _():
                dest[:, slot * block : (slot + 1) * block, :] = hole

    places = lax.broadcasted_iota(jnp.int32, (8, wide), 1)
    inside = jnp.zeros((8, wide), jnp.float32)
    within = jnp.zeros((8, wide), jnp.int32)
    for slot in range(9):
        here = (places >= slot * block) & (places < slot * block + count)
        there = 1.0 if slot == 0 else jnp.where(exists[slot], 1.0, 0.0)
        inside = jnp.where(here, there, inside)
        within = jnp.where(here, places - slot * block, within)
    rows = row_within(within.astype(jnp.float32))
    for tile in range(tiles):
        allowed = jnp.zeros((8, wide), jnp.float32)
        for row in range(TH):
            valid = jnp.where(valid_ref[tile * TH + row] > 0, 1.0, 0.0)
            allowed = jnp.where(rows == row, valid, allowed)
        bias[tile] = jnp.where(allowed * inside > 0, 0.0, -FAR)


    top[...] = jnp.full(top.shape, -3e38, jnp.float32)
    out[...] = jnp.zeros(out.shape, jnp.float32)
    grad_v[...] = jnp.zeros(grad_v.shape, jnp.float32)
    ones = jnp.ones((wide, depth), jnp.bfloat16)

    def over_rows(body, between=None):
        @pl.loop(0, 2)
        def _(end):
            body(end * (tiles - 1), end * (tiles - 2), 2)

        if between is not None:
            between()

        @pl.loop(1, tiles - 1)
        def _(row):
            body(row, row - 1, 2)
            body(row, row + 1, 1)

    def score_part(start, size):
        span = slice(start, start + size)

        def body(row, low, some):
            mine = pl.ds(low, some)
            queries = q_own[mine].reshape(some * block, depth)
            scores = dot_nt(queries, k_all[row, span, :]) * (scale * LOG2E)
            scores = scores + bias[row, 0:1, span]
            s_buf[pl.ds(2 * row + low, some), :, span] = scores.reshape(some, block, size)
            best = top[mine].reshape(some * block, 128)
            for lane in range(0, size, 128):
                best = jnp.maximum(best, scores[:, lane : lane + 128])
            top[mine] = best.reshape(some, block, 128)
        over_rows(body)

    def value_part(start, size):
        span = slice(start, start + size)

        def body(row, low, some):
            mine, slots = pl.ds(low, some), pl.ds(2 * row + low, some)
            peaks = top[mine].reshape(some * block, 128)[:, :1]
            expos = jnp.exp2(s_buf[slots, :, span].reshape(some * block, size) - peaks)
            s_buf[slots, :, span] = expos.reshape(some, block, size)
            values = jnp.concatenate([v_all[row, span, :], ones[:size]], axis=1)
            out[mine] += jnp.dot(
                expos.astype(jnp.bfloat16), values, preferred_element_type=jnp.float32
            ).reshape(some, block, 2 * depth)
        over_rows(body)

    def query_part(start, size):
        span = slice(start, start + size)

        def body(row, low, some):
            mine, slots = pl.ds(low, some), pl.ds(2 * row + low, some)
            deltas = grad_k[mine].reshape(some * block, depth)[:, :1]
            dprob = dot_nt(g_own[mine].reshape(some * block, depth), v_all[row, span, :])
            dscore = s_buf[slots, :, span].reshape(some * block, size) * (dprob - deltas)
            grad_v[mine] += jnp.dot(
                dscore.astype(jnp.bfloat16), k_all[row, span, :],
                preferred_element_type=jnp.float32,
            ).reshape(some, block, depth)
        over_rows(body)

    def key_part(start, size, between=None):
        span = slice(start, start + size)

        def body(row, low, some):
            mine = pl.ds(low, some)
            queries, grads = q_all[row, span, :], g_all[row, span, :]
            lse, delta = stats[row, 0:1, span], stats[row, 1:2, span]
            keys = k_own[mine].reshape(some * block, depth)
            values = v_own[mine].reshape(some * block, depth)
            probs = jnp.exp2(dot_nt(keys, queries) * (scale * LOG2E) - lse)
            grad_v[mine] += jnp.dot(
                probs.astype(jnp.bfloat16), grads, preferred_element_type=jnp.float32
            ).reshape(some, block, depth)
            dscore = probs * (dot_nt(values, grads) - delta)
            grad_k[mine] += jnp.dot(
                dscore.astype(jnp.bfloat16), queries, preferred_element_type=jnp.float32
            ).reshape(some, block, depth)
        over_rows(body, between)

    send_onward(0, (1, 2))
    send_onward(1, near)
    send_direct(2, q_own, (1, 2))
    receive(0, near)
    score_part(*halves[0])
    send_onward(1, (1, 2))
    send_direct(2, q_own, near)
    receive(0, far)
    score_part(*halves[1])
    swap(0, part_other, part_in).wait()
    grads = (
        g_own[...].astype(jnp.float32) + part_in[...].astype(jnp.float32)
    ).astype(jnp.bfloat16)
    g_own[...] = grads
    g_all[:, :block, :] = grads
    send_direct(3, g_own)

    @pl.loop(0, tiles)
    def _(tile):
        peak = jnp.max(top[tile], axis=1, keepdims=True)
        top[tile] = jnp.broadcast_to(peak, top.shape[1:])

    value_part(*halves[0])
    receive(1, far)
    value_part(*halves[1])
    send_onward(2, near)
    send_onward(2, (1, 2))

    @pl.loop(0, tiles)
    def _(tile):
        total = out[tile][:, depth:]
        attended = (out[tile][:, :depth] / total).astype(jnp.bfloat16)
        att_ref[tile] = attended
        grads = g_own[tile]
        delta = jnp.sum(
            grads.astype(jnp.float32) * attended.astype(jnp.float32), axis=1, keepdims=True
        )
        lanes = lax.broadcasted_iota(jnp.int32, (block, 128), 1)
        columns = jnp.where(lanes == 0, top[tile] + jnp.log2(total), delta)
        span = st_own.shape[-1]
        columns = jnp.concatenate([columns, jnp.zeros((span - block, 128), jnp.float32)], axis=0)
        st_own[tile] = columns.T[:8]
        grad_k[tile] = jnp.broadcast_to(delta, grad_k.shape[1:])

    swap(1, att_ref, att_in).start()
    send_direct(4, st_own)
    query_part(*halves[0])
    send_onward(3, near)
    send_onward(3, (1, 2))
    query_part(*halves[1])
    send_onward(4, (1, 2))

    @pl.loop(0, tiles)
    def _(tile):
        early[tile, :, 2 * depth :] = (
            grad_v[tile] * (scale / out[tile][:, depth:])
        ).astype(jnp.bfloat16)

    swap(1, att_ref, att_in).wait()
    own_att, other_att = (
        jnp.where(first, att_ref[...], att_in[...]), jnp.where(first, att_in[...], att_ref[...])
    )
    early[:, :, :depth] = own_att
    early[:, :, depth : 2 * depth] = other_att
    early_copy = pltpu.make_async_copy(early, early_ref, early_sem.at[0])
    early_copy.start()
    spots = lax.broadcasted_iota(jnp.int32, (step, 128), 0)[:, :1]

    @pl.loop(0, pieces)
    def _(piece):
        some, low = window(piece, group, block)
        goal = goal_spots(tiles, some, low, count, tall, -1) - piece * step
        heads = early[:, pl.ds(low, some), : 2 * depth].reshape(tiles * some, 2 * depth)
        moved = jnp.dot(picked(spots, goal), heads, preferred_element_type=jnp.float32)
        tall_qkv[pl.ds(pl.multiple_of(piece * step, step), step), : 2 * depth] = moved.astype(
            jnp.bfloat16
        )

    flat_t[...] = tall_qkv[:, : 2 * depth].astype(jnp.float32).T.astype(jnp.bfloat16)
    share_rows, width = share_ref.shape
    for start in range(0, width, 512):
        result = jnp.dot(
            flat_t[...], gm[:, start : start + 512], preferred_element_type=jnp.float32
        )
        for part in range(t_count * w_count):
            column, frame = part % w_count, part // w_count
            terms[column % 2, column // 2, frame, :, start : start + 512] = result[
                part * share_rows : (part + 1) * share_rows
            ].astype(jnp.bfloat16)
    core_copy().start()

    first_row = lax.broadcasted_iota(jnp.int32, (tiles, 8, wide), 1) == 0
    stats[...] = jnp.where(first_row, FAR, 0.0)
    stats[:, :, :block] = st_own[:, :, :block]

    def note(slots):
        for slot in slots:
            @pl.when(exists[slot])
            def _():
                stats[:, :, slot * block : (slot + 1) * block] = st_all[slot, :, :, :block]

    grad_k[...] = jnp.zeros(grad_k.shape, jnp.float32)
    grad_v[...] = jnp.zeros(grad_v.shape, jnp.float32)
    receive(4, near)
    note((1, 2, 3, 4))

    def cross_chips():
        core_copy().wait()
        send_w[...] = (
            terms[core].astype(jnp.float32) + in_core[...].astype(jnp.float32)
        ).astype(jnp.bfloat16)
        for hop in range(1, chips):
            w_copy(hop).start()

    key_part(*halves[0], cross_chips)

    whole = send_w[chip].astype(jnp.float32)
    for hop in range(1, chips):
        w_copy(hop).wait()
        whole = whole + in_w[hop - 1].astype(jnp.float32)
    sum_w[...] = whole
    send_t[...] = whole.astype(jnp.bfloat16)
    for hop in range(1, t_count):
        t_copy(hop).start()

    for which in (2, 3, 4):
        receive(which, far)
    note(far)
    key_part(*halves[1])

    places = lax.broadcasted_iota(jnp.int32, (block, 128), 0)
    rows = row_within(places.astype(jnp.float32))
    for tile in range(tiles):
        live = jnp.zeros((block, 128), jnp.float32)
        for row in range(TH):
            valid = jnp.where(valid_ref[tile * TH + row] > 0, 1.0, 0.0)
            live = jnp.where(rows == row, valid, live)
        all_ref[tile, :, :depth] = jnp.where(
            live > 0, grad_k[tile] * scale, 0.0
        ).astype(jnp.bfloat16)
        all_ref[tile, :, depth:] = jnp.where(
            live > 0, grad_v[tile], 0.0
        ).astype(jnp.bfloat16)

    share = sum_w[t_index]
    for hop in range(1, t_count):
        t_copy(hop).wait()
        share = share + in_t[hop - 1].astype(jnp.float32)
    share_ref[...] = share
    early_copy.wait()
    for which, source in enumerate((k_own, v_own, q_own, g_own, st_own)):
        sent(which, source)


def project_kernel(
    early_ref, late_ref, w_ref, share_in, mixed_ref, gq_ref, gk_ref, gv_ref, share_ref,
    *, block, count, tall, depth,
):
    group, high = mixed_ref.shape[:2]
    tiles = early_ref.shape[0]
    step, piece = group * tall, pl.program_id(0)
    some, low = window(piece, group, block)
    goal = goal_spots(tiles, some, low, count, tall, -1) - piece * step
    spots = lax.broadcasted_iota(jnp.int32, (step, 128), 0)[:, :1]
    pick = picked(spots, goal)
    moved, late = (
        jnp.dot(
            pick, ref[:, pl.ds(low, some), :].reshape(tiles * some, ref.shape[2]),
            preferred_element_type=jnp.float32,
        ).astype(jnp.bfloat16)
        for ref in (early_ref, late_ref)
    )
    mixed = jnp.dot(
        moved[:, : 2 * depth], w_ref[...], preferred_element_type=jnp.float32
    ).astype(jnp.bfloat16)
    for cell in range(group):
        span = slice(cell * tall, cell * tall + high)
        mixed_ref[cell] = mixed[span]
        gq_ref[cell] = moved[span, 2 * depth :]
        gk_ref[cell] = late[span, :depth]
        gv_ref[cell] = late[span, depth:]
    share_ref[...] = share_in[...]


def shards(query_heads, key_heads, value_heads, row_valid, out_weight, grad_mixed):
    frames, rows, columns, depth = query_heads.shape
    scale = 1.0 / math.sqrt(depth)
    tiles = rows // TH
    count = frames * columns * TH
    block = round_up(count, 16)
    wide = round_up(9 * block, 256)
    cells, tall = frames * columns, round_up(rows, 16)
    group = 6
    swap = (0, 2, 1, 3)
    native = lambda x: x.transpose(swap).reshape(cells, rows, x.shape[-1])
    t_count, w_count = lax.axis_size("tm"), lax.axis_size("width")
    share_rows, width = out_weight.shape[0] // (t_count * w_count), out_weight.shape[1]

    pairs = tiles * 3 - 2
    work = pairs * block * wide
    in_vmem = pl.BlockSpec(memory_space=pltpu.VMEM)
    anywhere = pl.BlockSpec(memory_space=pl.ANY)
    bf16 = lambda *shape: pltpu.VMEM(shape, jnp.bfloat16)
    f32 = lambda *shape: pltpu.VMEM(shape, jnp.float32)
    dma = lambda *shape: pltpu.SemaphoreType.DMA(shape)
    span = round_up(block, 128)
    early, late, share = pl.pallas_call(
        functools.partial(
            attention_kernel, tiles=tiles, block=block, wide=wide, count=count, tall=tall,
            scale=scale,
        ),
        out_shape=(
            jax.ShapeDtypeStruct((tiles, block, 3 * depth), jnp.bfloat16),
            jax.ShapeDtypeStruct((tiles, block, 2 * depth), jnp.bfloat16),
            jax.ShapeDtypeStruct((share_rows, width), jnp.float32),
        ),
        in_specs=[pl.BlockSpec(memory_space=pltpu.SMEM)] + [anywhere] * 5,
        out_specs=(anywhere, in_vmem, in_vmem),
        scratch_shapes=(
            [bf16(tiles, wide, depth)] * 4 + [bf16(tiles, block, depth)] * 4
            + [
                f32(pairs, block, wide), f32(tiles, 8, wide), f32(tiles, block, 128),
                f32(tiles, block, 2 * depth), f32(tiles, block, depth), f32(tiles, block, depth),
                bf16(3, cells, rows, depth), bf16(cells * tall, 3 * depth),
                bf16(2, group, rows, width),
                bf16(cells * tall, width), bf16(2 * depth, width),
                bf16(2 * depth, cells * tall),
            ]
            + [bf16(tiles, block, depth)] * 4
            + [
                f32(tiles, 8, span), f32(9, tiles, 8, span), f32(tiles, 8, wide),
                bf16(2, w_count // 2, t_count, share_rows, width),
                bf16(w_count // 2, t_count, share_rows, width),
                bf16(w_count // 2, t_count, share_rows, width),
                bf16(w_count // 2 - 1, t_count, share_rows, width),
                bf16(t_count - 1, share_rows, width),
                f32(t_count, share_rows, width), bf16(t_count, share_rows, width),
                dma(5, 13), dma(5, 9), dma(4), dma(2), dma(2), dma(2),
                dma(w_count // 2 - 1), dma(w_count // 2 - 1), dma(t_count - 1), dma(t_count - 1),
                dma(2), bf16(tiles, block, 3 * depth), dma(1),
            ]
        ),
        compiler_params=pltpu.CompilerParams(
            vmem_limit_bytes=60 << 20, collective_id=0, has_side_effects=True
        ),
        cost_estimate=pl.CostEstimate(
            flops=16 * work * depth, transcendentals=2 * work,
            bytes_accessed=4 * tiles * wide * depth,
        ),
        name="attention",
    )(
        row_valid, native(query_heads), native(key_heads), native(value_heads),
        native(grad_mixed), out_weight,
    )

    whole = lambda *shape: pl.BlockSpec(shape, lambda piece: (0,) * len(shape))
    part = lambda size: pl.BlockSpec((group, rows, size), lambda piece: (piece, 0, 0))
    cell_shape = lambda size: jax.ShapeDtypeStruct((cells, rows, size), jnp.bfloat16)
    mixed, *grads, grad_weight = pl.pallas_call(
        functools.partial(project_kernel, block=block, count=count, tall=tall, depth=depth),
        grid=(cells // group,),
        out_shape=(
            cell_shape(width), cell_shape(depth), cell_shape(depth), cell_shape(depth),
            jax.ShapeDtypeStruct((share_rows, width), jnp.float32),
        ),
        in_specs=[
            whole(tiles, block, 3 * depth), whole(tiles, block, 2 * depth), whole(2 * depth, width), whole(share_rows, width),
        ],
        out_specs=(part(width), part(depth), part(depth), part(depth), whole(share_rows, width)),
        compiler_params=pltpu.CompilerParams(vmem_limit_bytes=60 << 20),
        cost_estimate=pl.CostEstimate(
            flops=4 * cells * tall * depth * width, transcendentals=0,
            bytes_accessed=2 * cells * rows * width,
        ),
        name="project",
    )(early, late, out_weight, share)

    back = lambda x: x.reshape(frames, columns, rows, x.shape[-1]).transpose(swap)
    return (back(mixed), *(back(x) for x in grads), grad_weight)


def solution(mesh):
    split = P("tm", None, "width", "head")
    return jax.shard_map(
        shards,
        mesh=mesh,
        in_specs=(split, split, split, P(), P(None, "head"), split),
        out_specs=(split, split, split, split, P(("tm", "width"), "head")),
        check_vma=False,
    )
```

```python
import functools
import math

import jax
import jax.numpy as jnp
from jax import lax
from jax.experimental import pallas as pl
from jax.experimental.pallas import tpu as pltpu
from jax.sharding import PartitionSpec as P

TH = 9
FAR = 1e30
LOG2E = 1.4426950408889634


def round_up(value, step):
    return -(-value // step) * step


def dot_nt(left, right):
    return lax.dot_general(
        left, right, (((1,), (1,)), ((), ())), preferred_element_type=jnp.float32
    )


MESH = pl.DeviceIdType.MESH


def row_within(places):
    return places - TH * jnp.floor((places + 0.5) * (1.0 / TH))


def goal_spots(tiles, span, low, count, tall, none):
    columns = lax.broadcasted_iota(jnp.int32, (8, tiles * span), 1)
    goal = jnp.full((8, tiles * span), none, jnp.int32)
    for tile in range(tiles):
        place = columns - tile * span + low
        groups = jnp.floor((place.astype(jnp.float32) + 0.5) * (1.0 / TH)).astype(jnp.int32)
        here = (columns >= tile * span) & (columns < (tile + 1) * span) & (place < count)
        goal = jnp.where(here, groups * (tall - TH) + place + tile * TH, goal)
    return goal[0:1]


def window(piece, group, block):
    span = min(round_up(group * TH + 15, 16), block)
    low = jnp.minimum(piece * (group * TH) // 16 * 16, block - span)
    return span, pl.multiple_of(low, 16)


def picked(spots, goal):
    return jnp.where(spots == goal, 1.0, 0.0).astype(jnp.bfloat16)


def attention_kernel(
    valid_ref, q_hbm, k_hbm, v_hbm, gm_hbm, w_hbm,
    early_ref, all_ref, share_ref,
    k_all, v_all, q_all, g_all, q_own, k_own, v_own, g_own,
    s_buf, bias, top, out, grad_k, grad_v, landed, tall_qkv, gm_land,
    gm, weight, flat_t, att_ref, part_other, part_in, att_in,
    st_own, st_all, stats, terms, in_core, send_w, in_w, in_t, sum_w, send_t,
    send_sem, recv_sem, own_sem, gm_sem, peer_send, peer_recv, w_send, w_recv, t_send, t_recv,
    core_sem, early, early_sem,
    *, tiles, block, wide, count, tall, scale,
):
    depth = q_all.shape[-1]
    half = wide // 2
    halves = ((0, half), (half, half))
    t_index, w_index, h_index = (lax.axis_index(name) for name in ("tm", "width", "head"))
    t_count, w_count = lax.axis_size("tm"), lax.axis_size("width")
    t_back, t_ahead = t_index > 0, t_index < t_count - 1
    w_back, w_ahead = w_index > 0, w_index < w_count - 1
    exists = [
        None, t_back, t_ahead, w_back, w_ahead,
        t_back & w_back, t_ahead & w_back, t_back & w_ahead, t_ahead & w_ahead,
    ]
    t_above = (t_index + 1, w_index, h_index)
    t_below = (t_index - 1, w_index, h_index)
    w_above = (t_index, w_index + 1, h_index)
    w_below = (t_index, w_index - 1, h_index)
    peer = (t_index, w_index, 1 - h_index)
    direct = [(1, t_ahead, t_above), (2, t_back, t_below), (3, w_ahead, w_above), (4, w_back, w_below)]
    even = lax.rem(w_index, 2) == 0
    odd = jnp.logical_not(even)
    over_w = [
        (5, 1, t_back & w_ahead, even, w_above), (7, 1, t_back & w_back, odd, w_below),
        (6, 2, t_ahead & w_ahead, even, w_above), (8, 2, t_ahead & w_back, odd, w_below),
    ]
    over_t = [
        (5, 3, t_ahead & w_back & even, t_above), (7, 4, t_ahead & w_ahead & odd, t_above),
        (6, 3, t_back & w_back & even, t_below), (8, 4, t_back & w_ahead & odd, t_below),
    ]
    turned = ((), (6, 8), (5, 7), (6, 8), ())

    def routes(which):
        found = []
        for slot, via, there, within_chip, device in over_w:
            there = there & within_chip if slot in turned[which] else there
            found.append((slot, slot, via, there, device))
        for slot, via, there, device in over_t:
            if slot in turned[which]:
                found.append((slot + 4, slot, via, there, device))
        return found

    near, far = (3, 4), (5, 6, 7, 8)
    cells, high = landed.shape[1], landed.shape[2]
    group = gm_land.shape[1]
    pieces, step = cells // group, group * tall

    def slot_of(which, slot):
        if which == 4:
            return st_all.at[slot]
        dest = (k_all, v_all, q_all, g_all)[which]
        return dest.at[:, slot * block : (slot + 1) * block, :]

    def remote(which, source, slot, device, lane=None):
        return pltpu.make_async_remote_copy(
            src_ref=source, dst_ref=slot_of(which, slot),
            send_sem=send_sem.at[which, slot if lane is None else lane],
            recv_sem=recv_sem.at[which, slot],
            device_id=device, device_id_type=MESH,
        )

    def send_direct(which, source, slots=(1, 2, 3, 4)):
        for slot, there, device in direct:
            if slot in slots:
                @pl.when(there)
                def _():
                    remote(which, source, slot, device).start()

    def send_onward(which, vias):
        receive(which, vias)
        for lane, slot, via, there, device in routes(which):
            if via in vias:
                @pl.when(there)
                def _():
                    remote(which, slot_of(which, via), slot, device, lane).start()

    def receive(which, slots):
        for slot in slots:
            @pl.when(exists[slot])
            def _():
                remote(which, slot_of(which, slot), slot, peer).wait_recv()

    def sent(which, source):
        for slot, there, device in direct:
            @pl.when(there)
            def _():
                remote(which, source, slot, device).wait_send()
        for lane, slot, via, there, device in routes(which):
            @pl.when(there)
            def _():
                remote(which, slot_of(which, via), slot, device, lane).wait_send()

    def swap(index, source, dest):
        return pltpu.make_async_remote_copy(
            src_ref=source, dst_ref=dest, send_sem=peer_send.at[index],
            recv_sem=peer_recv.at[index], device_id=peer, device_id_type=MESH,
        )

    chips, core = w_count // 2, lax.rem(w_index, 2)
    chip = w_index // 2
    mate = (t_index, chip * 2 + 1 - core, h_index)

    def core_copy():
        return pltpu.make_async_remote_copy(
            src_ref=terms.at[1 - core], dst_ref=in_core, send_sem=core_sem.at[0],
            recv_sem=core_sem.at[1], device_id=mate, device_id_type=MESH,
        )

    def w_copy(hop):
        dest = lax.rem(chip + hop, chips)
        return pltpu.make_async_remote_copy(
            src_ref=send_w.at[dest], dst_ref=in_w.at[hop - 1],
            send_sem=w_send.at[hop - 1], recv_sem=w_recv.at[hop - 1],
            device_id=(t_index, dest * 2 + core, h_index), device_id_type=MESH,
        )

    def t_copy(hop):
        dest = lax.rem(t_index + hop, t_count)
        return pltpu.make_async_remote_copy(
            src_ref=send_t.at[dest], dst_ref=in_t.at[hop - 1],
            send_sem=t_send.at[hop - 1], recv_sem=t_recv.at[hop - 1],
            device_id=(dest, w_index, h_index), device_id_type=MESH,
        )

    own = [
        pltpu.make_async_copy(source, dest, own_sem.at[index])
        for index, (source, dest) in enumerate((
            (k_hbm, landed.at[0]), (v_hbm, landed.at[1]), (q_hbm, landed.at[2]), (w_hbm, weight),
        ))
    ]
    for copy in own:
        copy.start()

    def gm_copy(piece):
        return pltpu.make_async_copy(
            gm_hbm.at[pl.ds(piece * group, group)], gm_land.at[piece % 2], gm_sem.at[piece % 2]
        )

    for piece in range(2):
        gm_copy(piece).start()

    barrier = pltpu.get_barrier_semaphore()
    partners = [(there, device) for _, there, device in direct]
    for there, device in partners:
        @pl.when(there)
        def _():
            pl.semaphore_signal(barrier, inc=1, device_id=device, device_id_type=MESH)
    pl.semaphore_signal(barrier, inc=1, device_id=peer, device_id_type=MESH)
    greeted = 1 + sum(jnp.where(there, 1, 0) for there, _ in partners)
    pl.semaphore_signal(barrier, inc=1, device_id=mate, device_id_type=MESH)
    for hop in range(1, chips):
        dest = lax.rem(chip + hop, chips) * 2 + core
        pl.semaphore_signal(
            barrier, inc=1, device_id=(t_index, dest, h_index), device_id_type=MESH
        )
    for hop in range(1, t_count):
        dest = lax.rem(t_index + hop, t_count)
        pl.semaphore_signal(
            barrier, inc=1, device_id=(dest, w_index, h_index), device_id_type=MESH
        )

    cuts = []
    for start, stop in ((0, 16), (16, cells)):
        some = (block if stop == cells else stop * TH) - start * TH
        order = lax.broadcasted_iota(jnp.int32, (some, 128), 0).astype(jnp.float32)
        groups = jnp.floor((order + 0.5) * (1.0 / TH))
        goal = (groups * (tall - TH) + order).astype(jnp.int32)
        goal = jnp.where(order < count - start * TH, goal, -2 * high)[:, :1]
        spots = lax.broadcasted_iota(jnp.int32, (some, (stop - start) * tall), 1)
        rows = slice(start * TH, start * TH + some)
        cuts.append((rows, slice(start * tall, stop * tall), spots, goal))
    tall_qkv[...] = jnp.zeros(tall_qkv.shape, jnp.bfloat16)
    for copy in own[:3]:
        copy.wait()

    @pl.loop(0, cells)
    def _(cell):
        span = pl.ds(pl.multiple_of(cell * tall, tall), high)
        for index in range(3):
            tall_qkv[span, index * depth : (index + 1) * depth] = landed[index, cell]

    def place(first_column, pairs):
        columns = slice(first_column * depth, (first_column + len(pairs)) * depth)

        @pl.loop(0, tiles)
        def _(tile):
            for rows, span, spots, goal in cuts:
                moved = jnp.dot(
                    picked(spots, goal + tile * TH), tall_qkv[span, columns],
                    preferred_element_type=jnp.float32,
                ).astype(jnp.bfloat16)
                for index, (mine, dest) in enumerate(pairs):
                    part = moved[:, index * depth : (index + 1) * depth]
                    mine[tile, rows, :] = part
                    dest[tile, rows, :] = part

    place(0, ((k_own, k_all),))
    pl.semaphore_wait(barrier, greeted + chips + t_count - 1)
    send_direct(0, k_own)
    place(1, ((v_own, v_all), (q_own, q_all)))
    send_direct(1, v_own)

    own[3].wait()
    first = h_index == 0

    for piece in range(pieces):
        gm_copy(piece).wait()

        @pl.loop(0, group)
        def _(cell):
            low = piece * step + cell * tall
            gm[pl.ds(pl.multiple_of(low + tall - 16, 16), 16), :] = jnp.zeros(
                (16, gm.shape[1]), jnp.bfloat16
            )
            gm[pl.ds(pl.multiple_of(low, 16), high), :] = gm_land[piece % 2, cell]

        span = slice(piece * step, (piece + 1) * step)
        tall_qkv[span, : 2 * depth] = dot_nt(gm[span, :], weight[...]).astype(jnp.bfloat16)
        if piece + 2 < pieces:
            gm_copy(piece + 2).start()

    @pl.loop(0, tiles)
    def _(tile):
        for rows, span, spots, goal in cuts:
            parts = jnp.dot(
                picked(spots, goal + tile * TH), tall_qkv[span, : 2 * depth],
                preferred_element_type=jnp.float32,
            ).astype(jnp.bfloat16)
            g_own[tile, rows, :] = jnp.where(first, parts[:, :depth], parts[:, depth:])
            part_other[tile, rows, :] = jnp.where(first, parts[:, depth:], parts[:, :depth])

    swap(0, part_other, part_in).start()

    fill = jnp.zeros((tiles, wide - 9 * block, depth), jnp.bfloat16)
    hole = jnp.zeros((tiles, block, depth), jnp.bfloat16)
    for dest in (k_all, v_all, q_all, g_all):
        dest[:, 9 * block :, :] = fill
        for slot in range(1, 9):
            @pl.when(jnp.logical_not(exists[slot]))
            def _():
                dest[:, slot * block : (slot + 1) * block, :] = hole

    places = lax.broadcasted_iota(jnp.int32, (8, wide), 1)
    inside = jnp.zeros((8, wide), jnp.float32)
    within = jnp.zeros((8, wide), jnp.int32)
    for slot in range(9):
        here = (places >= slot * block) & (places < slot * block + count)
        there = 1.0 if slot == 0 else jnp.where(exists[slot], 1.0, 0.0)
        inside = jnp.where(here, there, inside)
        within = jnp.where(here, places - slot * block, within)
    rows = row_within(within.astype(jnp.float32))
    for tile in range(tiles):
        allowed = jnp.zeros((8, wide), jnp.float32)
        for row in range(TH):
            valid = jnp.where(valid_ref[tile * TH + row] > 0, 1.0, 0.0)
            allowed = jnp.where(rows == row, valid, allowed)
        bias[tile] = jnp.where(allowed * inside > 0, 0.0, -FAR)


    top[...] = jnp.full(top.shape, -3e38, jnp.float32)
    out[...] = jnp.zeros(out.shape, jnp.float32)
    grad_v[...] = jnp.zeros(grad_v.shape, jnp.float32)
    ones = jnp.ones((wide, depth), jnp.bfloat16)

    def over_rows(body, between=None):
        @pl.loop(0, 2)
        def _(end):
            body(end * (tiles - 1), end * (tiles - 2), 2)

        if between is not None:
            between()

        @pl.loop(1, tiles - 1)
        def _(row):
            body(row, row - 1, 2)
            body(row, row + 1, 1)

    def score_part(start, size):
        span = slice(start, start + size)

        def body(row, low, some):
            mine = pl.ds(low, some)
            queries = q_own[mine].reshape(some * block, depth)
            scores = dot_nt(queries, k_all[row, span, :]) * (scale * LOG2E)
            scores = scores + bias[row, 0:1, span]
            s_buf[pl.ds(2 * row + low, some), :, span] = scores.reshape(some, block, size)
            best = top[mine].reshape(some * block, 128)
            for lane in range(0, size, 128):
                best = jnp.maximum(best, scores[:, lane : lane + 128])
            top[mine] = best.reshape(some, block, 128)
        over_rows(body)

    def value_part(start, size):
        span = slice(start, start + size)

        def body(row, low, some):
            mine, slots = pl.ds(low, some), pl.ds(2 * row + low, some)
            peaks = top[mine].reshape(some * block, 128)[:, :1]
            expos = jnp.exp2(s_buf[slots, :, span].reshape(some * block, size) - peaks)
            s_buf[slots, :, span] = expos.reshape(some, block, size)
            values = jnp.concatenate([v_all[row, span, :], ones[:size]], axis=1)
            out[mine] += jnp.dot(
                expos.astype(jnp.bfloat16), values, preferred_element_type=jnp.float32
            ).reshape(some, block, 2 * depth)
        over_rows(body)

    def query_part(start, size):
        span = slice(start, start + size)

        def body(row, low, some):
            mine, slots = pl.ds(low, some), pl.ds(2 * row + low, some)
            deltas = grad_k[mine].reshape(some * block, depth)[:, :1]
            dprob = dot_nt(g_own[mine].reshape(some * block, depth), v_all[row, span, :])
            dscore = s_buf[slots, :, span].reshape(some * block, size) * (dprob - deltas)
            grad_v[mine] += jnp.dot(
                dscore.astype(jnp.bfloat16), k_all[row, span, :],
                preferred_element_type=jnp.float32,
            ).reshape(some, block, depth)
        over_rows(body)

    def key_part(start, size, between=None):
        span = slice(start, start + size)

        def body(row, low, some):
            mine = pl.ds(low, some)
            queries, grads = q_all[row, span, :], g_all[row, span, :]
            lse, delta = stats[row, 0:1, span], stats[row, 1:2, span]
            keys = k_own[mine].reshape(some * block, depth)
            values = v_own[mine].reshape(some * block, depth)
            probs = jnp.exp2(dot_nt(keys, queries) * (scale * LOG2E) - lse)
            grad_v[mine] += jnp.dot(
                probs.astype(jnp.bfloat16), grads, preferred_element_type=jnp.float32
            ).reshape(some, block, depth)
            dscore = probs * (dot_nt(values, grads) - delta)
            grad_k[mine] += jnp.dot(
                dscore.astype(jnp.bfloat16), queries, preferred_element_type=jnp.float32
            ).reshape(some, block, depth)
        over_rows(body, between)

    send_onward(0, (1, 2))
    send_onward(1, near)
    send_direct(2, q_own, (1, 2))
    receive(0, near)
    score_part(*halves[0])
    send_onward(1, (1, 2))
    send_direct(2, q_own, near)
    swap(0, part_other, part_in).wait()
    grads = (
        g_own[...].astype(jnp.float32) + part_in[...].astype(jnp.float32)
    ).astype(jnp.bfloat16)
    g_own[...] = grads
    g_all[:, :block, :] = grads
    send_direct(3, g_own)
    receive(0, far)
    score_part(*halves[1])

    @pl.loop(0, tiles)
    def _(tile):
        peak = jnp.max(top[tile], axis=1, keepdims=True)
        top[tile] = jnp.broadcast_to(peak, top.shape[1:])

    value_part(*halves[0])
    receive(1, far)
    value_part(*halves[1])
    send_onward(2, near)
    send_onward(2, (1, 2))

    @pl.loop(0, tiles)
    def _(tile):
        total = out[tile][:, depth:]
        attended = (out[tile][:, :depth] / total).astype(jnp.bfloat16)
        att_ref[tile] = attended
        grads = g_own[tile]
        delta = jnp.sum(
            grads.astype(jnp.float32) * attended.astype(jnp.float32), axis=1, keepdims=True
        )
        lanes = lax.broadcasted_iota(jnp.int32, (block, 128), 1)
        columns = jnp.where(lanes == 0, top[tile] + jnp.log2(total), delta)
        span = st_own.shape[-1]
        columns = jnp.concatenate([columns, jnp.zeros((span - block, 128), jnp.float32)], axis=0)
        st_own[tile] = columns.T[:8]
        grad_k[tile] = jnp.broadcast_to(delta, grad_k.shape[1:])

    swap(1, att_ref, att_in).start()
    send_direct(4, st_own)
    query_part(*halves[0])
    send_onward(3, near)
    send_onward(3, (1, 2))
    query_part(*halves[1])
    send_onward(4, (1, 2))

    @pl.loop(0, tiles)
    def _(tile):
        early[tile, :, 2 * depth :] = (
            grad_v[tile] * (scale / out[tile][:, depth:])
        ).astype(jnp.bfloat16)

    swap(1, att_ref, att_in).wait()
    own_att, other_att = (
        jnp.where(first, att_ref[...], att_in[...]), jnp.where(first, att_in[...], att_ref[...])
    )
    early[:, :, :depth] = own_att
    early[:, :, depth : 2 * depth] = other_att
    early_copy = pltpu.make_async_copy(early, early_ref, early_sem.at[0])
    early_copy.start()
    spots = lax.broadcasted_iota(jnp.int32, (step, 128), 0)[:, :1]

    @pl.loop(0, pieces)
    def _(piece):
        some, low = window(piece, group, block)
        goal = goal_spots(tiles, some, low, count, tall, -1) - piece * step
        heads = early[:, pl.ds(low, some), : 2 * depth].reshape(tiles * some, 2 * depth)
        moved = jnp.dot(picked(spots, goal), heads, preferred_element_type=jnp.float32)
        tall_qkv[pl.ds(pl.multiple_of(piece * step, step), step), : 2 * depth] = moved.astype(
            jnp.bfloat16
        )

    flat_t[...] = tall_qkv[:, : 2 * depth].astype(jnp.float32).T.astype(jnp.bfloat16)
    share_rows, width = share_ref.shape
    for start in range(0, width, 512):
        result = jnp.dot(
            flat_t[...], gm[:, start : start + 512], preferred_element_type=jnp.float32
        )
        for part in range(t_count * w_count):
            column, frame = part % w_count, part // w_count
            terms[column % 2, column // 2, frame, :, start : start + 512] = result[
                part * share_rows : (part + 1) * share_rows
            ].astype(jnp.bfloat16)
    core_copy().start()

    first_row = lax.broadcasted_iota(jnp.int32, (tiles, 8, wide), 1) == 0
    stats[...] = jnp.where(first_row, FAR, 0.0)
    stats[:, :, :block] = st_own[:, :, :block]

    def note(slots):
        for slot in slots:
            @pl.when(exists[slot])
            def _():
                stats[:, :, slot * block : (slot + 1) * block] = st_all[slot, :, :, :block]

    grad_k[...] = jnp.zeros(grad_k.shape, jnp.float32)
    grad_v[...] = jnp.zeros(grad_v.shape, jnp.float32)
    receive(4, near)
    note((1, 2, 3, 4))

    def cross_chips():
        core_copy().wait()
        send_w[...] = (
            terms[core].astype(jnp.float32) + in_core[...].astype(jnp.float32)
        ).astype(jnp.bfloat16)
        for hop in range(1, chips):
            w_copy(hop).start()

    key_part(*halves[0], cross_chips)

    whole = send_w[chip].astype(jnp.float32)
    for hop in range(1, chips):
        w_copy(hop).wait()
        whole = whole + in_w[hop - 1].astype(jnp.float32)
    sum_w[...] = whole
    send_t[...] = whole.astype(jnp.bfloat16)
    for hop in range(1, t_count):
        t_copy(hop).start()

    for which in (2, 3, 4):
        receive(which, far)
    note(far)
    key_part(*halves[1])

    places = lax.broadcasted_iota(jnp.int32, (block, 128), 0)
    rows = row_within(places.astype(jnp.float32))
    for tile in range(tiles):
        live = jnp.zeros((block, 128), jnp.float32)
        for row in range(TH):
            valid = jnp.where(valid_ref[tile * TH + row] > 0, 1.0, 0.0)
            live = jnp.where(rows == row, valid, live)
        all_ref[tile, :, :depth] = jnp.where(
            live > 0, grad_k[tile] * scale, 0.0
        ).astype(jnp.bfloat16)
        all_ref[tile, :, depth:] = jnp.where(
            live > 0, grad_v[tile], 0.0
        ).astype(jnp.bfloat16)

    share = sum_w[t_index]
    for hop in range(1, t_count):
        t_copy(hop).wait()
        share = share + in_t[hop - 1].astype(jnp.float32)
    share_ref[...] = share
    early_copy.wait()
    for which, source in enumerate((k_own, v_own, q_own, g_own, st_own)):
        sent(which, source)


def project_kernel(
    early_ref, late_ref, w_ref, share_in, mixed_ref, gq_ref, gk_ref, gv_ref, share_ref,
    *, block, count, tall, depth,
):
    group, high = mixed_ref.shape[:2]
    tiles = early_ref.shape[0]
    step, piece = group * tall, pl.program_id(0)
    some, low = window(piece, group, block)
    goal = goal_spots(tiles, some, low, count, tall, -1) - piece * step
    spots = lax.broadcasted_iota(jnp.int32, (step, 128), 0)[:, :1]
    pick = picked(spots, goal)
    moved, late = (
        jnp.dot(
            pick, ref[:, pl.ds(low, some), :].reshape(tiles * some, ref.shape[2]),
            preferred_element_type=jnp.float32,
        ).astype(jnp.bfloat16)
        for ref in (early_ref, late_ref)
    )
    mixed = jnp.dot(
        moved[:, : 2 * depth], w_ref[...], preferred_element_type=jnp.float32
    ).astype(jnp.bfloat16)
    for cell in range(group):
        span = slice(cell * tall, cell * tall + high)
        mixed_ref[cell] = mixed[span]
        gq_ref[cell] = moved[span, 2 * depth :]
        gk_ref[cell] = late[span, :depth]
        gv_ref[cell] = late[span, depth:]
    share_ref[...] = share_in[...]


def shards(query_heads, key_heads, value_heads, row_valid, out_weight, grad_mixed):
    frames, rows, columns, depth = query_heads.shape
    scale = 1.0 / math.sqrt(depth)
    tiles = rows // TH
    count = frames * columns * TH
    block = round_up(count, 16)
    wide = round_up(9 * block, 256)
    cells, tall = frames * columns, round_up(rows, 16)
    group = 6
    swap = (0, 2, 1, 3)
    native = lambda x: x.transpose(swap).reshape(cells, rows, x.shape[-1])
    t_count, w_count = lax.axis_size("tm"), lax.axis_size("width")
    share_rows, width = out_weight.shape[0] // (t_count * w_count), out_weight.shape[1]

    pairs = tiles * 3 - 2
    work = pairs * block * wide
    in_vmem = pl.BlockSpec(memory_space=pltpu.VMEM)
    anywhere = pl.BlockSpec(memory_space=pl.ANY)
    bf16 = lambda *shape: pltpu.VMEM(shape, jnp.bfloat16)
    f32 = lambda *shape: pltpu.VMEM(shape, jnp.float32)
    dma = lambda *shape: pltpu.SemaphoreType.DMA(shape)
    span = round_up(block, 128)
    early, late, share = pl.pallas_call(
        functools.partial(
            attention_kernel, tiles=tiles, block=block, wide=wide, count=count, tall=tall,
            scale=scale,
        ),
        out_shape=(
            jax.ShapeDtypeStruct((tiles, block, 3 * depth), jnp.bfloat16),
            jax.ShapeDtypeStruct((tiles, block, 2 * depth), jnp.bfloat16),
            jax.ShapeDtypeStruct((share_rows, width), jnp.float32),
        ),
        in_specs=[pl.BlockSpec(memory_space=pltpu.SMEM)] + [anywhere] * 5,
        out_specs=(anywhere, in_vmem, in_vmem),
        scratch_shapes=(
            [bf16(tiles, wide, depth)] * 4 + [bf16(tiles, block, depth)] * 4
            + [
                f32(pairs, block, wide), f32(tiles, 8, wide), f32(tiles, block, 128),
                f32(tiles, block, 2 * depth), f32(tiles, block, depth), f32(tiles, block, depth),
                bf16(3, cells, rows, depth), bf16(cells * tall, 3 * depth),
                bf16(2, group, rows, width),
                bf16(cells * tall, width), bf16(2 * depth, width),
                bf16(2 * depth, cells * tall),
            ]
            + [bf16(tiles, block, depth)] * 4
            + [
                f32(tiles, 8, span), f32(9, tiles, 8, span), f32(tiles, 8, wide),
                bf16(2, w_count // 2, t_count, share_rows, width),
                bf16(w_count // 2, t_count, share_rows, width),
                bf16(w_count // 2, t_count, share_rows, width),
                bf16(w_count // 2 - 1, t_count, share_rows, width),
                bf16(t_count - 1, share_rows, width),
                f32(t_count, share_rows, width), bf16(t_count, share_rows, width),
                dma(5, 13), dma(5, 9), dma(4), dma(2), dma(2), dma(2),
                dma(w_count // 2 - 1), dma(w_count // 2 - 1), dma(t_count - 1), dma(t_count - 1),
                dma(2), bf16(tiles, block, 3 * depth), dma(1),
            ]
        ),
        compiler_params=pltpu.CompilerParams(
            vmem_limit_bytes=60 << 20, collective_id=0, has_side_effects=True
        ),
        cost_estimate=pl.CostEstimate(
            flops=16 * work * depth, transcendentals=2 * work,
            bytes_accessed=4 * tiles * wide * depth,
        ),
        name="attention",
    )(
        row_valid, native(query_heads), native(key_heads), native(value_heads),
        native(grad_mixed), out_weight,
    )

    whole = lambda *shape: pl.BlockSpec(shape, lambda piece: (0,) * len(shape))
    part = lambda size: pl.BlockSpec((group, rows, size), lambda piece: (piece, 0, 0))
    cell_shape = lambda size: jax.ShapeDtypeStruct((cells, rows, size), jnp.bfloat16)
    mixed, *grads, grad_weight = pl.pallas_call(
        functools.partial(project_kernel, block=block, count=count, tall=tall, depth=depth),
        grid=(cells // group,),
        out_shape=(
            cell_shape(width), cell_shape(depth), cell_shape(depth), cell_shape(depth),
            jax.ShapeDtypeStruct((share_rows, width), jnp.float32),
        ),
        in_specs=[
            whole(tiles, block, 3 * depth), whole(tiles, block, 2 * depth), whole(2 * depth, width), whole(share_rows, width),
        ],
        out_specs=(part(width), part(depth), part(depth), part(depth), whole(share_rows, width)),
        compiler_params=pltpu.CompilerParams(vmem_limit_bytes=60 << 20),
        cost_estimate=pl.CostEstimate(
            flops=4 * cells * tall * depth * width, transcendentals=0,
            bytes_accessed=2 * cells * rows * width,
        ),
        name="project",
    )(early, late, out_weight, share)

    back = lambda x: x.reshape(frames, columns, rows, x.shape[-1]).transpose(swap)
    return (back(mixed), *(back(x) for x in grads), grad_weight)


def solution(mesh):
    split = P("tm", None, "width", "head")
    return jax.shard_map(
        shards,
        mesh=mesh,
        in_specs=(split, split, split, P(), P(None, "head"), split),
        out_specs=(split, split, split, split, P(("tm", "width"), "head")),
        check_vma=False,
    )
```
